32 devices in a mesh: ctx: 8 (over z, y), fsdp: 4 (over x, core).
Axes of the slice: x: 2, y: 2, z: 4, core: 2. Of those that a mesh axis runs over, the one named last changes fastest.
Arguments:
- hidden_in: bfloat16 [4, 2048, 1536], P('fsdp', 'ctx'), may hold values from -6 to 6
- out_grad: bfloat16 [4, 2048, 1536], P('fsdp', 'ctx'), may hold values from -6 to 6
- positions: int32 [4, 2048], P('fsdp'), may hold values from 0 to 2047, as said below
- attn_gain: bfloat16 [1536], P('fsdp'), may hold values from 0.5 to 1.5
- w_query: bfloat16 [1536, 1536], P('fsdp'), may hold values from -0.15625 to 0.15625
- w_key: bfloat16 [1536, 768], P('fsdp'), may hold values from -0.15625 to 0.15625
- w_value: bfloat16 [1536, 768], P('fsdp'), may hold values from -0.15625 to 0.15625
- w_out: bfloat16 [1536, 1536], P('fsdp'), may hold values from -3 to 3
- ffn_gain: bfloat16 [1536], P('fsdp'), may hold values from 0.5 to 1.5
- w_gate: bfloat16 [1536, 4096], P('fsdp'), may hold values from -0.15625 to 0.15625
- w_up: bfloat16 [1536, 4096], P('fsdp'), may hold values from -0.15625 to 0.15625
- w_down: bfloat16 [1536, 4096], P('fsdp'), may hold values from -0.09375 to 0.09375
Outputs:
- out: bfloat16 [4, 2048, 1536], P('fsdp', 'ctx')
- input_grad: float32 [4, 2048, 1536], P('fsdp', 'ctx')
- attn_gain_grad: float32 [1536], P('fsdp')
- w_query_grad: float32 [1536, 1536], P('fsdp')
- w_key_grad: float32 [1536, 768], P('fsdp')
- w_value_grad: float32 [1536, 768], P('fsdp')
- w_out_grad: float32 [1536, 1536], P('fsdp')
- ffn_gain_grad: float32 [1536], P('fsdp')
- w_gate_grad: float32 [1536, 4096], P('fsdp')
- w_up_grad: float32 [1536, 4096], P('fsdp')
- w_down_grad: float32 [1536, 4096], P('fsdp')
The draws below stay inside these ranges and needn't reach their ends.
Inputs may be any that keep to these rules, and one draw needn't show every extreme that they name: In each sequence, the 256 rows of one ctx index hold the positions of causal block b followed by those of block 15 - b, each in increasing order, where b is that index's place in a permutation of the 8 pairs drawn for that sequence; each sequence's positions are a permutation of 0 to 2047.
All inputs are finite; a program needn't handle non-finite values.
Results may differ from the reference program's by a relative error of at most 0.022.
Values may be sent and summed in bfloat16 or wider, within the bound.
No kernel may reach another device: no remote copies, remote signals or barrier semaphores. Data moves between devices by JAX's collectives and lax.ppermute only.
A program may use at most 448 MiB of HBM per device.

```python
import math
import jax
import jax.numpy as jnp
from jax import lax

D = 1536
HQ = 16
HK = 8
HD = 96
FF = 4096
BLK = 128
LENGTH = 2048
SEQS = 4


def draw_positions(key, part):
    pair_count = LENGTH // (2 * BLK)

    def per_sequence(sequence_index):
        deal_order = jax.random.permutation(jax.random.fold_in(key, sequence_index), pair_count)
        offsets = jnp.arange(BLK, dtype=jnp.int32)[None, :]
        early_rows = deal_order[:, None] * BLK + offsets
        late_rows = (2 * pair_count - 1 - deal_order)[:, None] * BLK + offsets
        return jnp.concatenate([early_rows, late_rows], axis=1).reshape(LENGTH)
    return jax.vmap(per_sequence)(jnp.arange(SEQS, dtype=jnp.int32)).astype(jnp.int32)


def block_scale(stream_key, dims, split, low, largest):
    def one(dim, blocks):
        heights = jax.random.uniform(jax.random.fold_in(jax.random.fold_in(stream_key, 6), dim), (blocks,), jnp.float32, low / len(split), largest / len(split))
        return jnp.repeat(jnp.exp(heights), dims[dim] // blocks).reshape((-1,) + (1,) * (len(dims) - dim - 1))

    factor_of = one(*split[0])
    for cut in split[1:]:
        factor_of = factor_of * one(*cut)
    return factor_of


def noise(stream_key, shape, scale, bound, cuts=(), kind=jnp.bfloat16):
    drawn = scale * jax.random.normal(stream_key, shape, jnp.float32)
    if cuts:
        drawn = drawn * block_scale(stream_key, shape, cuts, -0.22, 0.18)
    return jnp.clip(drawn, -bound, bound).astype(kind)


def setup_inputs(seed: int = 0) -> dict:
    arg_keys = jax.random.split(jax.random.key(seed), 13)
    return {
        "hidden_in": noise(arg_keys[0], (SEQS, LENGTH, D), 1.0, 6.0, ((0, 4), (1, 8))),
        "out_grad": noise(arg_keys[1], (SEQS, LENGTH, D), 1.0, 6.0, ((0, 4), (1, 8))),
        "positions": draw_positions(jax.random.fold_in(arg_keys[12], 71), 0),
        "attn_gain": jnp.clip(1.0 + 0.1 * jax.random.normal(arg_keys[3], (D,), jnp.float32), 0.5, 1.5).astype(jnp.bfloat16),
        "w_query": noise(arg_keys[4], (D, HQ * HD), D ** -0.5, 0.15625, ((0, 4),)),
        "w_key": noise(arg_keys[5], (D, HK * HD), D ** -0.5, 0.15625, ((0, 4),)),
        "w_value": noise(arg_keys[6], (D, HK * HD), D ** -0.5, 0.15625, ((0, 4),)),
        "w_out": noise(arg_keys[7], (D, HQ * HD), 4 ** -0.5, 3.0, ((0, 4),)),
        "ffn_gain": jnp.clip(1.0 + 0.1 * jax.random.normal(arg_keys[8], (D,), jnp.float32), 0.5, 1.5).astype(jnp.bfloat16),
        "w_gate": noise(arg_keys[9], (D, FF), D ** -0.5, 0.15625, ((0, 4),)),
        "w_up": noise(arg_keys[10], (D, FF), D ** -0.5, 0.15625, ((0, 4),)),
        "w_down": noise(arg_keys[11], (D, FF), FF ** -0.5, 0.09375, ((0, 4),)),
    }


epsilon = 1e-05
rope_base = 100000.0
masked_score = -1e+30
highest = lax.Precision.HIGHEST

@jax.custom_vjp
def low(v):
    return lax.optimization_barrier(v.astype(jnp.bfloat16)).astype(jnp.float32)

@jax.custom_vjp
def low_back(v):
    return v

def low_keep(v):
    return (low(v), None)

def low_pass(kept, grad):
    return (grad,)

def back_keep(v):
    return (v, None)

def back_low(kept, grad):
    return (low(grad),)
low.defvjp(low_keep, low_pass)
low_back.defvjp(back_keep, back_low)

def rms_scale(values, gain):
    inverse = lax.rsqrt(lax.optimization_barrier(jnp.mean(values * values, axis=-1, keepdims=True)) + epsilon)
    return values * inverse * gain

def rotate(values, cosine, sine):
    half_size = values.shape[-1] // 2
    first_half = values[..., :half_size]
    second_half = values[..., half_size:]
    return jnp.concatenate([first_half * cosine - second_half * sine, second_half * cosine + first_half * sine], axis=-1)

def angles_of(places):
    frequency = jnp.exp(jnp.arange(HD // 2, dtype=jnp.float32) * (-2.0 * math.log(rope_base) / HD))
    turned = places.astype(jnp.float32)[:, None] * frequency[None, :]
    return (jnp.cos(turned)[:, None, :], jnp.sin(turned)[:, None, :])

def one_sequence(weights, rows_in, places):
    attn_gain, w_query, w_key, w_value, w_out, ffn_gain, w_gate, w_up, w_down = weights
    group_size = HQ // HK
    scale = 1.0 / math.sqrt(HD)
    cosine, sine = angles_of(places)
    normed_one = low(rms_scale(rows_in, attn_gain))
    query = low_back(jnp.dot(normed_one, w_query, precision=highest))
    keys = low_back(jnp.dot(normed_one, w_key, precision=highest))
    values = low(low_back(jnp.dot(normed_one, w_value, precision=highest)))
    query_rot = low(rotate(query.reshape(LENGTH, HQ, HD), cosine, sine)).reshape(LENGTH, HK, group_size, HD)
    keys_rot = low(rotate(keys.reshape(LENGTH, HK, HD), cosine, sine))
    values = values.reshape(LENGTH, HK, HD)
    block_size = math.gcd(LENGTH, 512)

    def attend(block_index):
        start = block_index * block_size
        query_block = lax.dynamic_slice_in_dim(query_rot, start, block_size, 0)
        query_places = lax.dynamic_slice_in_dim(places, start, block_size, 0)
        scores = low_back(jnp.einsum('qkgd,skd->qkgs', query_block, keys_rot, precision=highest) * scale)
        allowed = places[None, None, None, :] <= query_places[:, None, None, None]
        scores = jnp.where(allowed, scores, masked_score)
        soft = low(jax.nn.softmax(scores, axis=-1))
        return jnp.einsum('qkgs,skd->qkgd', soft, values, precision=highest)
    mixed = lax.map(jax.checkpoint(attend), jnp.arange(LENGTH // block_size, dtype=jnp.int32))
    mixed = low(low_back(mixed.reshape(LENGTH, HQ * HD)))
    branch = low_back(jnp.dot(mixed, w_out.T, precision=highest))
    middle = rows_in + branch
    normed_two = low(rms_scale(middle, ffn_gain))
    gate = low_back(jnp.dot(normed_two, w_gate, precision=highest))
    upward = low_back(jnp.dot(normed_two, w_up, precision=highest))
    hidden = low(jax.nn.silu(gate) * upward)
    return middle + low_back(jnp.dot(hidden, w_down.T, precision=highest))

def forward(weights, rows_all, positions):

    def per_sequence(carry, pieces):
        return (carry, one_sequence(weights, pieces[0], pieces[1]))
    unused, outputs = lax.scan(per_sequence, jnp.zeros((), jnp.float32), (rows_all, positions))
    return outputs

def reference(hidden_in, out_grad, positions, attn_gain, w_query, w_key, w_value, w_out, ffn_gain, w_gate, w_up, w_down):
    weights = tuple((matrix.astype(jnp.float32) for matrix in (attn_gain, w_query, w_key, w_value, w_out, ffn_gain, w_gate, w_up, w_down)))
    rows_all = hidden_in.astype(jnp.float32)
    result, pullback = jax.vjp(lambda params, inputs: forward(params, inputs, positions), weights, rows_all)
    weight_grads, input_grad = pullback(out_grad.astype(jnp.float32))
    return (result.astype(jnp.bfloat16), input_grad, weight_grads[0], weight_grads[1], weight_grads[2], weight_grads[3], weight_grads[4], weight_grads[5], weight_grads[6], weight_grads[7], weight_grads[8])
```

```python
import functools
import math

import jax
import jax.numpy as jnp
from jax import lax
from jax.experimental import pallas as pl
from jax.experimental.pallas import tpu as pltpu
from jax.sharding import PartitionSpec as P

HQ = 16
HK = 8
HD = 96
GROUP = HQ // HK
BLK = 128

epsilon = 1e-05
rope_base = 100000.0
masked_score = -1e30
scale = 1.0 / math.sqrt(HD)
low = jnp.bfloat16
wide = jnp.float32


def angles_of(places):
    frequency = jnp.exp(jnp.arange(HD // 2, dtype=wide) * (-2.0 * math.log(rope_base) / HD))
    turned = places.astype(wide)[:, None] * frequency[None, :]
    return (jnp.cos(turned)[:, None, :], jnp.sin(turned)[:, None, :])


def rotate(values, cosine, sine):
    half_size = values.shape[-1] // 2
    first_half = values[..., :half_size]
    second_half = values[..., half_size:]
    return jnp.concatenate(
        [first_half * cosine - second_half * sine, second_half * cosine + first_half * sine],
        axis=-1,
    )


def product(left, right):
    return jnp.dot(left, right, preferred_element_type=wide)


def contract_last(left, right):
    return lax.dot_general(left, right, (((1,), (1,)), ((), ())), preferred_element_type=wide)


def contract_first(left, right):
    return lax.dot_general(left, right, (((0,), (0,)), ((), ())), preferred_element_type=wide)


def rms_back(values, inverse, gain, grad_normed):
    weighted = gain * grad_normed
    inner = jnp.mean(values * weighted, axis=1, keepdims=True)
    grad_values = inverse * weighted - values * inverse * inverse * inverse * inner
    return (grad_values, jnp.sum(grad_normed * values * inverse, axis=0))


def swap(array, axis, bits, size):
    return lax.ppermute(array, axis, [(i, i ^ bits) for i in range(size)])


def over_fsdp(array, bits):
    return swap(array, "fsdp", bits, 4)


def over_ctx(array, bits):
    return swap(array, "ctx", bits, 8)


def columns(array, index, width):
    return lax.dynamic_slice_in_dim(array, index * width, width, 1)


def rows(array, index, height):
    return lax.dynamic_slice_in_dim(array, index * height, height, 0)


def gather_fsdp(array):
    far = over_fsdp(array, 2)
    near = over_fsdp(array, 1)
    both = over_fsdp(far, 1)
    return (array, near, far, both)


def scatter_fsdp(parts):
    near = [over_fsdp(parts[1].astype(low), 1), over_fsdp(parts[3].astype(low), 1)]
    own = parts[0].astype(wide) + near[0].astype(wide)
    away = parts[2].astype(wide) + near[1].astype(wide)
    return own + over_fsdp(away.astype(low), 2).astype(wide)


def stack_kernel(index_ref, *refs):
    parts, out_ref = refs[:4], refs[4]
    for k in range(4):

        @pl.when(pl.program_id(1) == index_ref[0] ^ k)
        def _(k=k):
            out_ref[...] = parts[k][...]


def stack_rows(index, parts):
    height, width = parts[0].shape
    tile = math.gcd(width, 768) if width % 768 == 0 else math.gcd(width, 512)
    return pl.pallas_call(
        stack_kernel,
        grid_spec=pltpu.PrefetchScalarGridSpec(
            num_scalar_prefetch=1,
            grid=(width // tile, 4),
            in_specs=[pl.BlockSpec((height, tile), lambda j, i, index: (0, j))] * 4,
            out_specs=pl.BlockSpec((height, tile), lambda j, i, index: (i, j)),
        ),
        out_shape=jax.ShapeDtypeStruct((4 * height, width), parts[0].dtype),
        cost_estimate=pl.CostEstimate(
            flops=0, bytes_accessed=16 * height * width, transcendentals=0
        ),
        name="stack_rows",
    )(index.reshape(1), *parts)


def sort_rows(order_ref, load_ref, queries, keys, values):
    for slot in range(load_ref.shape[0] // BLK):
        block = order_ref[slot]
        piece = load_ref[slot * BLK : (slot + 1) * BLK, :]
        place = pl.ds(pl.multiple_of(block * BLK, BLK), BLK)
        half = pl.ds(pl.multiple_of((block % 2) * BLK, BLK), BLK)
        other = pl.ds(pl.multiple_of((block % 2) * BLK + 2 * BLK, BLK), BLK)
        queries[block // 2, half, :] = piece[:, :HD]
        queries[block // 2, other, :] = piece[:, HD : 2 * HD]
        keys[place, :] = piece[:, 2 * HD : 3 * HD]
        values[place, :] = piece[:, 3 * HD :]


def forward_kernel(order_ref, load_ref, out_ref, queries, keys, values, mixed):
    sort_rows(order_ref, load_ref, queries, keys, values)
    step = 2 * BLK
    query_at = lax.broadcasted_iota(jnp.int32, (2 * step, step), 0) % step
    key_at = lax.broadcasted_iota(jnp.int32, (2 * step, step), 1)
    allowed = key_at <= query_at
    for i in range(keys.shape[0] // step):
        reach = (i + 1) * step
        query = queries[i]
        ahead = contract_last(query, keys[i * step : reach, :]) * scale
        ahead = jnp.where(allowed, ahead, masked_score)
        top = jnp.max(ahead, axis=1, keepdims=True)
        if i:
            before = contract_last(query, keys[: i * step, :]) * scale
            top = jnp.maximum(top, jnp.max(before, axis=1, keepdims=True))
        soft = jnp.exp(ahead - top)
        total = jnp.sum(soft, axis=1, keepdims=True)
        result = product(soft.astype(low), values[i * step : reach, :])
        if i:
            soft = jnp.exp(before - top)
            total = total + jnp.sum(soft, axis=1, keepdims=True)
            result = result + product(soft.astype(low), values[: i * step, :])
        result = (result / total).astype(low)
        mixed[i * step : reach, :HD] = result[:step]
        mixed[i * step : reach, HD:] = result[step:]
    for slot in range(load_ref.shape[0] // BLK):
        place = pl.ds(pl.multiple_of(order_ref[slot] * BLK, BLK), BLK)
        out_ref[slot * BLK : (slot + 1) * BLK, :] = mixed[place, :]


def backward_kernel(
    order_ref, load_ref, grad_ref, out_ref, queries, keys, values, grads, key_sum, value_sum, sent
):
    sort_rows(order_ref, load_ref, queries, keys, values)
    step = 2 * BLK
    length = keys.shape[0]
    for slot in range(length // BLK):
        block = order_ref[slot]
        piece = grad_ref[slot * BLK : (slot + 1) * BLK, :]
        half = pl.ds(pl.multiple_of((block % 2) * BLK, BLK), BLK)
        other = pl.ds(pl.multiple_of((block % 2) * BLK + 2 * BLK, BLK), BLK)
        grads[block // 2, half, :] = piece[:, :HD]
        grads[block // 2, other, :] = piece[:, HD:]
    key_at = lax.broadcasted_iota(jnp.int32, (step, 2 * step), 0)
    query_at = lax.broadcasted_iota(jnp.int32, (step, 2 * step), 1) % step
    allowed = key_at <= query_at
    for i in range(length // step):
        query = queries[i]
        grad = grads[i]
        scores = []
        top = None
        for j in range(i + 1):
            score = contract_last(keys[j * step : (j + 1) * step, :], query) * scale
            if j == i:
                score = jnp.where(allowed, score, masked_score)
            high = jnp.max(score, axis=0, keepdims=True)
            top = high if top is None else jnp.maximum(top, high)
            scores.append(score)
        total = jnp.zeros_like(top)
        delta = jnp.zeros_like(top)
        softs = []
        slopes = []
        for j in range(i + 1):
            soft = jnp.exp(scores[j] - top)
            slope = contract_last(values[j * step : (j + 1) * step, :], grad)
            total = total + jnp.sum(soft, axis=0, keepdims=True)
            delta = delta + jnp.sum(soft * slope, axis=0, keepdims=True)
            softs.append(soft)
            slopes.append(slope)
        share = 1.0 / total
        delta = delta * share
        query_sum = jnp.zeros((2 * step, HD), wide)
        for j in range(i + 1):
            place = slice(j * step, (j + 1) * step)
            soft = softs[j] * share
            steep = (soft * (slopes[j] - delta)).astype(low)
            key_part = product(steep, query)
            value_part = product(soft.astype(low), grad)
            if j == i:
                key_sum[place, :] = key_part
                value_sum[place, :] = value_part
            else:
                key_sum[place, :] += key_part
                value_sum[place, :] += value_part
            query_sum = query_sum + contract_first(steep, keys[place, :])
        query_sum = (query_sum * scale).astype(low)
        sent[i * step : (i + 1) * step, :HD] = query_sum[:step]
        sent[i * step : (i + 1) * step, HD : 2 * HD] = query_sum[step:]
    sent[:, 2 * HD : 3 * HD] = (key_sum[...] * scale).astype(low)
    sent[:, 3 * HD :] = value_sum[...].astype(low)
    for slot in range(length // BLK):
        place = pl.ds(pl.multiple_of(order_ref[slot] * BLK, BLK), BLK)
        out_ref[slot * BLK : (slot + 1) * BLK, :] = sent[place, :]


def attention_call(kernel, order, arrays, width, scratch, products, name):
    length = arrays[0].shape[0]
    half = (length * length) // 2 * GROUP
    whole = pl.BlockSpec(memory_space=pltpu.VMEM)
    return pl.pallas_call(
        kernel,
        grid_spec=pltpu.PrefetchScalarGridSpec(
            num_scalar_prefetch=1,
            grid=(),
            in_specs=[whole] * len(arrays),
            out_specs=whole,
            scratch_shapes=scratch,
        ),
        out_shape=jax.ShapeDtypeStruct((length, width), low),
        compiler_params=pltpu.CompilerParams(vmem_limit_bytes=56 << 20),
        cost_estimate=pl.CostEstimate(
            flops=2 * products * half * 256, bytes_accessed=8 * length * width, transcendentals=half
        ),
        name=name,
    )(order, *arrays)


def attention_forward(order, load):
    length = load.shape[0]
    scratch = [
        pltpu.VMEM((length // (2 * BLK), 4 * BLK, HD), low),
        pltpu.VMEM((length, HD), low),
        pltpu.VMEM((length, HD), low),
        pltpu.VMEM((length, 2 * HD), low),
    ]
    return attention_call(forward_kernel, order, (load,), 2 * HD, scratch, 2, "attention_forward")


def attention_backward(order, load, grad):
    length = load.shape[0]
    scratch = [
        pltpu.VMEM((length // (2 * BLK), 4 * BLK, HD), low),
        pltpu.VMEM((length, HD), low),
        pltpu.VMEM((length, HD), low),
        pltpu.VMEM((length // (2 * BLK), 4 * BLK, HD), low),
        pltpu.VMEM((length, HD), wide),
        pltpu.VMEM((length, HD), wide),
        pltpu.VMEM((length, 4 * HD), low),
    ]
    return attention_call(
        backward_kernel, order, (load, grad), 4 * HD, scratch, 5, "attention_backward"
    )


def scores_of(query_rot, keys_all, own_places, all_places, start, block_size):
    key_block = lax.dynamic_slice_in_dim(keys_all, start, block_size, 0)
    key_places = lax.dynamic_slice_in_dim(all_places, start, block_size, 0)
    raw = (
        jnp.einsum("rkgd,skd->rkgs", query_rot, key_block, preferred_element_type=wide) * scale
    )
    allowed = key_places[None, None, None, :] <= own_places[:, None, None, None]
    return (jnp.where(allowed, raw, masked_score), key_block)


def rows_forward(query_rot, keys_all, values_all, own_places, all_places):
    row_count = query_rot.shape[0]
    key_total = keys_all.shape[0]
    block_size = math.gcd(key_total, 512)

    def step(block_index, carry):
        top_score, total, mixed = carry
        start = block_index * block_size
        scores, _ = scores_of(query_rot, keys_all, own_places, all_places, start, block_size)
        value_block = lax.dynamic_slice_in_dim(values_all, start, block_size, 0)
        new_top = jnp.maximum(top_score, jnp.max(scores, axis=-1))
        soft = jnp.exp(scores - new_top[..., None])
        shrink = jnp.exp(top_score - new_top)
        total = total * shrink + jnp.sum(soft, axis=-1)
        mixed = mixed * shrink[..., None] + jnp.einsum(
            "rkgs,skd->rkgd", soft.astype(low), value_block, preferred_element_type=wide
        )
        return (new_top, total, mixed)

    start_top = jnp.full((row_count, HK, GROUP), masked_score, wide)
    start_total = jnp.zeros((row_count, HK, GROUP), wide)
    start_mixed = jnp.zeros((row_count, HK, GROUP, HD), wide)
    top_score, total, mixed = lax.fori_loop(
        0, key_total // block_size, step, (start_top, start_total, start_mixed)
    )
    return (mixed / total[..., None], top_score + jnp.log(total))


def rows_backward(
    query_rot, keys_all, values_all, own_places, all_places, log_total, delta, grad_mixed
):
    row_count = query_rot.shape[0]
    key_total = keys_all.shape[0]
    block_size = math.gcd(key_total, 512)

    def step(block_index, carry):
        grad_query, grad_keys, grad_values = carry
        start = block_index * block_size
        scores, key_block = scores_of(
            query_rot, keys_all, own_places, all_places, start, block_size
        )
        value_block = lax.dynamic_slice_in_dim(values_all, start, block_size, 0)
        soft = jnp.exp(scores - log_total[..., None])
        grad_soft = jnp.einsum(
            "rkgd,skd->rkgs", grad_mixed, value_block, preferred_element_type=wide
        )
        steep = (soft * (grad_soft - delta[..., None])).astype(low)
        grad_query = grad_query + scale * jnp.einsum(
            "rkgs,skd->rkgd", steep, key_block, preferred_element_type=wide
        )
        key_part = scale * jnp.einsum(
            "rkgs,rkgd->skd", steep, query_rot, preferred_element_type=wide
        )
        value_part = jnp.einsum(
            "rkgs,rkgd->skd", soft.astype(low), grad_mixed, preferred_element_type=wide
        )
        grad_keys = lax.dynamic_update_slice_in_dim(
            grad_keys, key_part.reshape(block_size, HK * HD), start, 0
        )
        grad_values = lax.dynamic_update_slice_in_dim(
            grad_values, value_part.reshape(block_size, HK * HD), start, 0
        )
        return (grad_query, grad_keys, grad_values)

    start_query = jnp.zeros((row_count, HK, GROUP, HD), wide)
    start_keys = jnp.zeros((key_total, HK * HD), wide)
    return lax.fori_loop(
        0, key_total // block_size, step, (start_query, start_keys, start_keys)
    )


def add_low(first, *others):
    total = first.astype(wide)
    for other in others:
        total = total + other.astype(wide)
    return total.astype(low)


def reduce_ctx(grad, dim, size):
    here = lax.axis_index("ctx")
    if size != 8:
        return lax.psum_scatter(grad, "ctx", scatter_dimension=dim, tiled=True)
    cut = (rows, columns)[dim]
    side, level = here % 2, here // 2
    half = grad.shape[dim] // 2
    piece = grad.shape[dim] // 8
    kept = add_low(cut(grad, side, half), over_ctx(cut(grad, 1 - side, half), 1))
    got = [over_ctx(cut(kept, level ^ k, piece), 2 * k) for k in (1, 2, 3)]
    return add_low(cut(kept, level, piece), *got)


def spread_kernel(where_ref, *refs):
    parts, out_ref = refs[:8], refs[8]
    piece = parts[0].shape[0]
    for k in range(8):
        place = pl.multiple_of((where_ref[0] ^ k) * piece, piece)
        out_ref[pl.ds(place, piece), :] = parts[k][...].astype(wide)


def spread_columns_kernel(where_ref, *refs):
    parts, out_ref = refs[:8], refs[8]
    piece = parts[0].shape[2]
    for k in range(8):
        place = pl.multiple_of((where_ref[0] ^ k) * piece, piece)
        out_ref[:, pl.ds(place, piece)] = parts[k][0].astype(wide)


def gather_ctx(piece):
    near = [piece] + [over_ctx(piece, 2 * k) for k in (1, 2, 3)]
    return near + [over_ctx(part, 1) for part in near]


def place_code(here):
    return (here % 2) * 4 + here // 2


def finish_rows(piece, size):
    if size != 8:
        return lax.all_gather(piece, "ctx", axis=0, tiled=True).astype(wide)
    parts = gather_ctx(piece)
    height, width = piece.shape
    tile = 384
    return pl.pallas_call(
        spread_kernel,
        grid_spec=pltpu.PrefetchScalarGridSpec(
            num_scalar_prefetch=1,
            grid=(width // tile,),
            in_specs=[pl.BlockSpec((height, tile), lambda i, where: (0, i))] * 8,
            out_specs=pl.BlockSpec((8 * height, tile), lambda i, where: (0, i)),
        ),
        out_shape=jax.ShapeDtypeStruct((8 * height, width), wide),
        cost_estimate=pl.CostEstimate(
            flops=0, bytes_accessed=48 * height * width, transcendentals=0
        ),
        name="spread_rows",
    )(place_code(lax.axis_index("ctx")).reshape(1), *parts)


def finish_columns(piece, size):
    here, part = lax.axis_index("ctx"), lax.axis_index("fsdp")
    height, width = piece.shape[1:]
    if size != 8:
        whole = lax.all_gather(piece, "ctx", axis=2, tiled=True)
        return jnp.concatenate(
            [
                lax.dynamic_index_in_dim(whole, part ^ k, 0, keepdims=False)
                for k in range(4)
            ],
            axis=1,
        ).astype(wide)
    parts = gather_ctx(piece)
    return pl.pallas_call(
        spread_columns_kernel,
        grid_spec=pltpu.PrefetchScalarGridSpec(
            num_scalar_prefetch=1,
            grid=(4,),
            in_specs=[pl.BlockSpec((1, height, width), lambda i, where: (where[1] ^ i, 0, 0))] * 8,
            out_specs=pl.BlockSpec((height, 8 * width), lambda i, where: (0, i)),
        ),
        out_shape=jax.ShapeDtypeStruct((height, 32 * width), wide),
        cost_estimate=pl.CostEstimate(
            flops=0, bytes_accessed=192 * height * width, transcendentals=0
        ),
        name="spread_columns",
    )(jnp.stack([place_code(here), part]), *parts)


def split_weight_grad(left, right, size):
    part = lax.axis_index("fsdp")
    piece = reduce_ctx(contract_first(left, right).astype(low), 1, size)
    height = piece.shape[0] // 4
    got = [over_fsdp(rows(piece, part ^ k, height), k) for k in (1, 2, 3)]
    return finish_columns(jnp.stack([rows(piece, part, height)] + got), size)


def own_rows_grad(left, right, size):
    part = lax.axis_index("fsdp")
    width = left.shape[1] // 4

    def term(k):
        return contract_first(columns(left, part ^ k, width), right)

    summed = scatter_fsdp([term(0), term(1), term(2), term(3)]).astype(low)
    return finish_rows(reduce_ctx(summed, 0, size), size)


def body(
    size,
    hidden_in,
    out_grad,
    positions,
    attn_gain,
    w_query,
    w_key,
    w_value,
    w_out,
    ffn_gain,
    w_gate,
    w_up,
    w_down,
):
    part, here = lax.axis_index("fsdp"), lax.axis_index("ctx")
    gains = lax.all_gather(jnp.stack([attn_gain, ffn_gain]), "fsdp", axis=1, tiled=True)
    gain_one, gain_two = gains[0].astype(wide), gains[1].astype(wide)

    def gathered(weight):
        return stack_rows(part, gather_fsdp(weight))

    def dealt(weight):
        width = weight.shape[1] // 4
        got = [over_fsdp(columns(weight, part ^ k, width), k) for k in (1, 2, 3)]
        return stack_rows(part, [columns(weight, part, width)] + got)

    full_query, full_key, full_value = gathered(w_query), gathered(w_key), gathered(w_value)
    full_out = gathered(w_out)
    part_gate, part_up, part_down = dealt(w_gate), dealt(w_up), dealt(w_down)

    rows_in = hidden_in[0].astype(wide)
    row_count = rows_in.shape[0]
    all_places = positions[0]
    own_places = lax.dynamic_slice_in_dim(all_places, here * row_count, row_count, 0)
    cosine, sine = angles_of(own_places)
    inverse_one = lax.rsqrt(jnp.mean(rows_in * rows_in, axis=1, keepdims=True) + epsilon)
    normed_one = (rows_in * inverse_one * gain_one).astype(low)
    query = product(normed_one, full_query)
    keys = product(normed_one, full_key)
    values = product(normed_one, full_value).astype(low)
    query_rot = rotate(query.reshape(row_count, HQ, HD), cosine, sine).astype(low)
    keys_rot = rotate(keys.reshape(row_count, HK, HD), cosine, sine).astype(low)

    if size == HK:
        load = jnp.concatenate(
            [
                query_rot.reshape(row_count, HK, GROUP * HD),
                keys_rot,
                values.reshape(row_count, HK, HD),
            ],
            axis=-1,
        ).transpose(1, 0, 2)
        load = lax.all_to_all(load, "ctx", 0, 0, tiled=True).reshape(size * row_count, 4 * HD)
        order = all_places[:: BLK] // BLK
        mixed = attention_forward(order, load).reshape(size, row_count, GROUP * HD)
        mixed_low = lax.all_to_all(mixed, "ctx", 0, 0, tiled=True)
        mixed_low = mixed_low.transpose(1, 0, 2).reshape(row_count, HQ * HD)
    else:
        keys_all = lax.all_gather(keys_rot, "ctx", axis=0, tiled=True)
        values_all = lax.all_gather(
            values.reshape(row_count, HK, HD), "ctx", axis=0, tiled=True
        )
        query_rot = query_rot.reshape(row_count, HK, GROUP, HD)
        mixed_exact, log_total = rows_forward(
            query_rot, keys_all, values_all, own_places, all_places
        )
        mixed_low = mixed_exact.reshape(row_count, HQ * HD).astype(low)

    middle = rows_in + contract_last(mixed_low, full_out)
    inverse_two = lax.rsqrt(jnp.mean(middle * middle, axis=1, keepdims=True) + epsilon)
    normed_two = (middle * inverse_two * gain_two).astype(low)

    normed_all = jnp.concatenate(gather_fsdp(normed_two), axis=0)
    grad_all = jnp.concatenate(gather_fsdp(out_grad[0]), axis=0)

    def quarters(array):
        return [array[k * row_count : (k + 1) * row_count] for k in range(4)]

    gate = product(normed_all, part_gate)
    upward = product(normed_all, part_up)
    sigmoid_gate = jax.nn.sigmoid(gate)
    swish = gate * sigmoid_gate
    hidden = (swish * upward).astype(low)
    result = (middle + scatter_fsdp(quarters(contract_last(hidden, part_down)))).astype(low)
    grad_hidden = product(grad_all, part_down)
    grad_gate = (grad_hidden * upward * sigmoid_gate * (1.0 + gate * (1.0 - sigmoid_gate))).astype(
        low
    )
    grad_up = (grad_hidden * swish).astype(low)
    grad_normed_two = scatter_fsdp(
        quarters(contract_last(grad_gate, part_gate) + contract_last(grad_up, part_up))
    )
    grad_middle_norm, grad_gain_two = rms_back(middle, inverse_two, gain_two, grad_normed_two)
    grad_middle = out_grad[0].astype(wide) + grad_middle_norm
    grad_branch = grad_middle.astype(low)
    grad_mixed = product(grad_branch, full_out).astype(low)

    if size == HK:
        grad_mixed = grad_mixed.reshape(row_count, HK, GROUP * HD).transpose(1, 0, 2)
        grad_mixed = lax.all_to_all(grad_mixed, "ctx", 0, 0, tiled=True)
        grad_load = attention_backward(
            order, load, grad_mixed.reshape(size * row_count, GROUP * HD)
        ).reshape(size, row_count, 4 * HD)
        grad_load = lax.all_to_all(grad_load, "ctx", 0, 0, tiled=True)
        grad_load = grad_load.transpose(1, 0, 2).astype(wide)
        grad_query = grad_load[:, :, : GROUP * HD].reshape(row_count, HQ, HD)
        grad_keys = grad_load[:, :, GROUP * HD : (GROUP + 1) * HD]
        grad_values = grad_load[:, :, (GROUP + 1) * HD :].reshape(row_count, HK * HD)
    else:
        grad_mixed = grad_mixed.reshape(row_count, HK, GROUP, HD)
        delta = jnp.sum(grad_mixed.astype(wide) * mixed_exact, axis=-1)
        grad_query, grad_keys, grad_values = rows_backward(
            query_rot, keys_all, values_all, own_places, all_places, log_total, delta, grad_mixed
        )
        grad_query = grad_query.reshape(row_count, HQ, HD)
        grad_keys, grad_values = (
            lax.psum_scatter(whole.astype(low), "ctx", scatter_dimension=0, tiled=True).astype(
                wide
            )
            for whole in (grad_keys, grad_values)
        )
        grad_keys = grad_keys.reshape(row_count, HK, HD)
    grad_query_raw = rotate(grad_query, cosine, -sine).reshape(row_count, HQ * HD).astype(low)
    grad_keys_raw = rotate(grad_keys, cosine, -sine).reshape(row_count, HK * HD).astype(low)
    grad_values_low = grad_values.astype(low)
    grad_normed_one = (
        contract_last(grad_query_raw, full_query)
        + contract_last(grad_keys_raw, full_key)
        + contract_last(grad_values_low, full_value)
    )
    grad_rows_norm, grad_gain_one = rms_back(rows_in, inverse_one, gain_one, grad_normed_one)
    input_grad = (grad_middle + grad_rows_norm)[None]

    down_grad = split_weight_grad(grad_all, hidden, size)
    gate_grad = split_weight_grad(normed_all, grad_gate, size)
    up_grad = split_weight_grad(normed_all, grad_up, size)
    out_weight_grad = own_rows_grad(grad_branch, mixed_low, size)
    value_grad = own_rows_grad(normed_one, grad_values_low, size)
    key_grad = own_rows_grad(normed_one, grad_keys_raw, size)
    query_grad = own_rows_grad(normed_one, grad_query_raw, size)
    gain_grads = lax.psum(jnp.stack([grad_gain_one, grad_gain_two]), ("ctx", "fsdp"))
    gain_grads = columns(gain_grads, part, attn_gain.shape[0])
    return (
        result[None],
        input_grad,
        gain_grads[0],
        query_grad,
        key_grad,
        value_grad,
        out_weight_grad,
        gain_grads[1],
        gate_grad,
        up_grad,
        down_grad,
    )


def solution(mesh):
    matrix = P("fsdp", None)
    stream = P("fsdp", "ctx", None)
    return jax.shard_map(
        functools.partial(body, mesh.shape["ctx"]),
        mesh=mesh,
        in_specs=(stream, stream, matrix, P("fsdp"))
        + (matrix,) * 4
        + (P("fsdp"),)
        + (matrix,) * 3,
        out_specs=(stream, stream, P("fsdp")) + (matrix,) * 4 + (P("fsdp"),) + (matrix,) * 3,
        check_vma=False,
    )
```

```python
import math

import jax
import jax.numpy as jnp
from jax import lax
from jax.experimental import pallas as pl
from jax.experimental.pallas import tpu as pltpu
from jax.sharding import PartitionSpec as P

HQ = 16
HK = 8
HD = 96
GROUP = HQ // HK
BLK = 128

epsilon = 1e-05
rope_base = 100000.0
masked_score = -1e30
scale = 1.0 / math.sqrt(HD)
low = jnp.bfloat16
wide = jnp.float32
brief = pl.CostEstimate(flops=0, bytes_accessed=0, transcendentals=0)
lasting = pl.CostEstimate(flops=10**11, bytes_accessed=0, transcendentals=0)


def angles_of(places):
    frequency = jnp.exp(jnp.arange(HD // 2, dtype=wide) * (-2.0 * math.log(rope_base) / HD))
    turned = places.astype(wide)[:, None] * frequency[None, :]
    return (jnp.cos(turned)[:, None, :], jnp.sin(turned)[:, None, :])


def product(left, right):
    return jnp.dot(left, right, preferred_element_type=wide)


def contract_last(left, right):
    return lax.dot_general(left, right, (((1,), (1,)), ((), ())), preferred_element_type=wide)


def contract_first(left, right):
    return lax.dot_general(left, right, (((0,), (0,)), ((), ())), preferred_element_type=wide)


def swap(array, axis, bits, size):
    return lax.ppermute(array, axis, [(i, i ^ bits) for i in range(size)])


def over_fsdp(array, bits):
    return swap(array, "fsdp", bits, 4)


def over_ctx(array, bits):
    return swap(array, "ctx", bits, lax.axis_size("ctx"))


def columns(array, index, width):
    return lax.dynamic_slice_in_dim(array, index * width, width, array.ndim - 1)


def rows(array, index, height):
    return lax.dynamic_slice_in_dim(array, index * height, height, 0)


def after(array, *others):
    return lax.optimization_barrier((array, *others))[0]


def add_low(first, *others):
    total = first.astype(wide)
    for other in others:
        total = total + other.astype(wide)
    return total.astype(low)


def gather_fsdp(array, *others):
    far = after(over_fsdp(array, 2), *others)
    pair = over_fsdp(jnp.concatenate([array, far], axis=0), 1)
    return jnp.concatenate([array, far, pair], axis=0)


def scatter_fsdp(terms, *others):
    half, height = terms.shape[0] // 2, terms.shape[0] // 4
    kept, got = terms[:half], over_fsdp(terms[half:], 1)
    passed = add_low(kept[height:], got[height:])
    away = after(over_fsdp(passed, 2), *others)
    total = kept[:height].astype(wide) + got[:height].astype(wide) + away.astype(wide)
    return total, passed


ALL, REST, MINE, OTHER = 0, 3, 4, 8
heads_plan = (
    (0, ALL),
    (1, ALL),
    (2, MINE + 1),
    (2, OTHER + 1),
    (2, REST),
    (3, MINE + 1),
    (3, OTHER + 1),
    (3, REST),
)
outward_plan = ((0, ALL), (1, ALL), (2, MINE + 2), (2, OTHER + 2), (3, MINE + 2), (3, OTHER + 2))
units_plan = ((0, ALL), (1, ALL), (2, MINE + 1), (2, OTHER + 1), (3, MINE + 2), (3, OTHER + 2))


def gather_thirds(own):
    side = lax.axis_index("ctx") % 2
    third = own.shape[1] // 3
    far = over_fsdp(columns(own, side, third), 2)
    rest = over_fsdp(after(own[:, 2 * third :], far), 2)
    near = over_fsdp(own, 1)
    other = over_ctx(far, 1)
    return (
        own,
        near,
        far,
        other,
        rest,
        over_fsdp(far, 1),
        over_fsdp(other, 1),
        over_fsdp(rest, 1),
    )


def gather_halves(own):
    far = over_fsdp(columns(own, lax.axis_index("ctx") // 2 % 2, own.shape[1] // 2), 2)
    near = over_fsdp(own, 1)
    other = over_ctx(far, 2)
    return (own, near, far, other, over_fsdp(far, 1), over_fsdp(other, 1))


def fill_weight(code_ref, plan, pieces, out):
    part = code_ref[0]
    for (k, which), piece in zip(plan, pieces):
        height, width = piece.shape
        across = pl.ds(pl.multiple_of((part ^ k) * height, height), height)
        if which == ALL:
            out[across, :] = piece[...]
        elif which == REST:
            out[across, 2 * width :] = piece[...]
        else:
            side = code_ref[which % MINE]
            place = 1 - side if which >= OTHER else side
            out[across, lanes(place, width)] = piece[...]


def whole_call(kernel, code, arrays, outs, scratch, flops, name):
    spec = pl.BlockSpec(memory_space=pltpu.VMEM)
    moved = sum(math.prod(a.shape) * a.dtype.itemsize for a in (*arrays, *outs))
    return pl.pallas_call(
        kernel,
        grid_spec=pltpu.PrefetchScalarGridSpec(
            num_scalar_prefetch=1,
            grid=(),
            in_specs=[spec] * len(arrays),
            out_specs=[spec] * len(outs),
            scratch_shapes=scratch,
        ),
        out_shape=outs,
        compiler_params=pltpu.CompilerParams(vmem_limit_bytes=56 << 20),
        cost_estimate=pl.CostEstimate(flops=flops, bytes_accessed=moved, transcendentals=0),
        name=name,
    )(code, *arrays)


def lanes(index, width):
    return pl.ds(pl.multiple_of(index * width, 128), width)


def gained(code_ref, gains, row, out):
    for k in range(4):
        out[:, lanes(code_ref[0] ^ k, gains[k].shape[1])] = gains[k][row : row + 1, :].astype(wide)


def turned(values, cosine, sine):
    half = values.shape[1] // 2
    return values * cosine + jnp.concatenate([values[:, half:], values[:, :half]], axis=1) * sine


def inverse_rms(values):
    return lax.rsqrt(jnp.mean(values * values, axis=1, keepdims=True) + epsilon)


def slot_of_head(head):
    if head < HQ:
        return head // GROUP, head % GROUP
    return (head - HQ) % HK, GROUP + (head - HQ) // HK


def heads_kernel(code_ref, rows_ref, cosine_ref, sine_ref, *refs):
    gains, pieces = refs[:4], refs[4:12]
    normed_ref, load_ref, gain, weight, total = refs[12:]
    gained(code_ref, gains, 0, gain)
    fill_weight(code_ref, heads_plan, pieces, weight)
    values = rows_ref[...].astype(wide)
    normed_ref[...] = (values * inverse_rms(values) * gain[...]).astype(low)
    total[...] = product(normed_ref[...], weight[...])
    cosine, sine = cosine_ref[...], sine_ref[...]
    for head in range(HQ + 2 * HK):
        part = total[:, head * HD : (head + 1) * HD]
        if head < HQ + HK:
            part = turned(part, cosine, sine)
        group, place = slot_of_head(head)
        load_ref[group, :, place * HD : (place + 1) * HD] = part.astype(low)


def heads_call(code, rows_in, cosine, sine, gains, pieces):
    count, width = rows_in.shape
    total = pieces[0].shape[1]
    outs = [
        jax.ShapeDtypeStruct((count, width), low),
        jax.ShapeDtypeStruct((HK, count, (GROUP + 2) * HD), low),
    ]
    scratch = [
        pltpu.VMEM((1, width), wide),
        pltpu.VMEM((width, total), low),
        pltpu.VMEM((count, total), wide),
    ]
    return whole_call(
        heads_kernel,
        code,
        (rows_in, cosine, sine, *gains, *pieces),
        outs,
        scratch,
        2 * count * width * total,
        "query_key_value",
    )


def middle_kernel(code_ref, rows_ref, mixed_ref, *refs):
    gains, pieces = refs[:4], refs[4:10]
    flat_ref, middle_ref, normed_ref, gain, weight = refs[10:]
    gained(code_ref, gains, 1, gain)
    fill_weight(code_ref, outward_plan, pieces, weight)
    span = mixed_ref.shape[2]
    for group in range(mixed_ref.shape[0]):
        flat_ref[:, group * span : (group + 1) * span] = mixed_ref[group]
    middle = contract_last(flat_ref[...], weight[...]) + rows_ref[...].astype(wide)
    middle_ref[...] = middle
    normed_ref[...] = (middle * inverse_rms(middle) * gain[...]).astype(low)


def middle_call(code, rows_in, mixed, gains, pieces):
    count, width = rows_in.shape
    outs = [
        jax.ShapeDtypeStruct((count, HQ * HD), low),
        jax.ShapeDtypeStruct((count, width), wide),
        jax.ShapeDtypeStruct((count, width), low),
    ]
    return whole_call(
        middle_kernel,
        code,
        (rows_in, mixed, *gains, *pieces),
        outs,
        [pltpu.VMEM((1, width), wide), pltpu.VMEM((width, HQ * HD), low)],
        2 * count * width * HQ * HD,
        "attention_output",
    )


def norm_back(values, gain, grad):
    inverse = inverse_rms(values)
    weighted = gain * grad
    inner = jnp.mean(values * weighted, axis=1, keepdims=True)
    back = inverse * weighted - values * inverse * inverse * inverse * inner
    return back, jnp.sum(grad * values * inverse, axis=0, keepdims=True)


def middle_back_kernel(code_ref, middle_ref, grad_ref, out_grad_ref, *refs):
    gains, pieces = refs[:4], refs[4:10]
    grad_middle_ref, branch_ref, sent_ref, gain_grad_ref, gain, weight = refs[10:]
    gained(code_ref, gains, 1, gain)
    fill_weight(code_ref, outward_plan, pieces, weight)
    back, gain_grad_ref[...] = norm_back(middle_ref[...], gain[...], grad_ref[...])
    grad_middle = out_grad_ref[...].astype(wide) + back
    grad_middle_ref[...] = grad_middle
    branch_ref[...] = grad_middle.astype(low)
    total = product(branch_ref[...], weight[...]).astype(low)
    span = sent_ref.shape[2]
    for group in range(sent_ref.shape[0]):
        sent_ref[group] = total[:, group * span : (group + 1) * span]


def middle_back_call(code, middle, grad, out_grad, gains, pieces):
    count, width = middle.shape
    outs = [
        jax.ShapeDtypeStruct((count, width), wide),
        jax.ShapeDtypeStruct((count, width), low),
        jax.ShapeDtypeStruct((HK, count, GROUP * HD), low),
        jax.ShapeDtypeStruct((1, width), wide),
    ]
    return whole_call(
        middle_back_kernel,
        code,
        (middle, grad, out_grad, *gains, *pieces),
        outs,
        [pltpu.VMEM((1, width), wide), pltpu.VMEM((width, HQ * HD), low)],
        2 * count * width * HQ * HD,
        "attention_output_back",
    )


def heads_back_kernel(
    code_ref, load_ref, rows_ref, grad_middle_ref, cosine_ref, sine_ref, *refs
):
    gains, pieces = refs[:4], refs[4:12]
    raw_ref, input_grad_ref, gain_grad_ref, gain, weight, raw = refs[12:]
    gained(code_ref, gains, 0, gain)
    fill_weight(code_ref, heads_plan, pieces, weight)
    cosine, sine = cosine_ref[...], sine_ref[...]
    for head in range(HQ + 2 * HK):
        group, place = slot_of_head(head)
        part = load_ref[group, :, place * HD : (place + 1) * HD]
        if head < HQ + HK:
            part = turned(part.astype(wide), cosine, -sine).astype(low)
        raw[:, head * HD : (head + 1) * HD] = part
    quarter = raw_ref.shape[3]
    for k in range(4):
        for i in range(2):
            first = (4 * i + k) * quarter
            raw_ref[i, k] = raw[:, first : first + quarter]
    grad = contract_last(raw[...], weight[...])
    back, gain_grad_ref[...] = norm_back(rows_ref[...].astype(wide), gain[...], grad)
    input_grad_ref[...] = grad_middle_ref[...] + back


def heads_back_call(code, load, rows_in, grad_middle, cosine, sine, gains, pieces):
    count, width = rows_in.shape
    total = pieces[0].shape[1]
    outs = [
        jax.ShapeDtypeStruct((2, 4, count, total // 8), low),
        jax.ShapeDtypeStruct((count, width), wide),
        jax.ShapeDtypeStruct((1, width), wide),
    ]
    return whole_call(
        heads_back_kernel,
        code,
        (load, rows_in, grad_middle, cosine, sine, *gains, *pieces),
        outs,
        [
            pltpu.VMEM((1, width), wide),
            pltpu.VMEM((width, total), low),
            pltpu.VMEM((count, total), low),
        ],
        2 * count * width * total,
        "query_key_value_back",
    )


def units_kernel(code_ref, normed_ref, grad_ref, *refs):
    pieces = refs[:6]
    out_ref, back_ref, hidden_ref, grad_gate_ref, grad_up_ref, weights = refs[6:]

    @pl.when(pl.program_id(0) == 0)
    def _():
        for i in range(3):
            fill_weight(code_ref, units_plan, [piece.at[i] for piece in pieces], weights.at[i])

    gate = product(normed_ref[...], weights[0])
    upward = product(normed_ref[...], weights[1])
    sigmoid_gate = jax.nn.sigmoid(gate)
    swish = gate * sigmoid_gate
    hidden = (swish * upward).astype(low)
    hidden_ref[...] = hidden
    grad_hidden = product(grad_ref[...], weights[2])
    grad_gate = (
        grad_hidden * upward * sigmoid_gate * (1.0 + gate * (1.0 - sigmoid_gate))
    ).astype(low)
    grad_up = (grad_hidden * swish).astype(low)
    grad_gate_ref[...] = grad_gate
    grad_up_ref[...] = grad_up
    back_ref[...] = (
        contract_last(grad_gate, weights[0]) + contract_last(grad_up, weights[1])
    ).astype(low)
    out_ref[...] = contract_last(hidden, weights[2]).astype(low)


def units_call(code, normed, grad, pieces):
    count, width = normed.shape
    units = pieces[0].shape[2]
    tile = 512
    wide_block = pl.BlockSpec((tile, width), lambda i, code: (i, 0))
    unit_block = pl.BlockSpec((tile, units), lambda i, code: (i, 0))
    return pl.pallas_call(
        units_kernel,
        grid_spec=pltpu.PrefetchScalarGridSpec(
            num_scalar_prefetch=1,
            grid=(count // tile,),
            in_specs=[wide_block, wide_block]
            + [pl.BlockSpec(memory_space=pltpu.VMEM)] * len(pieces),
            out_specs=[wide_block, wide_block, unit_block, unit_block, unit_block],
            scratch_shapes=[pltpu.VMEM((3, width, units), low)],
        ),
        out_shape=[jax.ShapeDtypeStruct((count, width), low)] * 2
        + [jax.ShapeDtypeStruct((count, units), low)] * 3,
        compiler_params=pltpu.CompilerParams(vmem_limit_bytes=60 << 20),
        cost_estimate=pl.CostEstimate(
            flops=12 * count * width * units,
            bytes_accessed=8 * count * width + 6 * width * units,
            transcendentals=count * units,
        ),
        name="feed_forward",
    )(code, normed, grad, *pieces)


def deal_weights(weights):
    part, here = lax.axis_index("fsdp"), lax.axis_index("ctx")
    width = weights[0].shape[1] // 4

    def taken(k):
        return jnp.stack([columns(weight, part ^ k, width) for weight in weights])

    def half(k, side):
        return jnp.stack(
            [columns(weight, (part ^ k) * 2 + side, width // 2) for weight in weights]
        )

    return taken(0), taken(1), half(2, here % 2), half(3, here // 2 % 2)


def slot_of(ref, slot):
    return ref.at[slot // 2, (slot % 2) * BLK : (slot % 2 + 1) * BLK, :]


def sort_rows(order_ref, load_ref, queries, keys, values):
    for slot in range(2 * load_ref.shape[0]):
        block = order_ref[slot]
        piece = slot_of(load_ref, slot)[...]
        place = pl.ds(pl.multiple_of(block * BLK, BLK), BLK)
        half = pl.ds(pl.multiple_of((block % 2) * BLK, BLK), BLK)
        other = pl.ds(pl.multiple_of((block % 2) * BLK + 2 * BLK, BLK), BLK)
        queries[block // 2, half, :] = piece[:, :HD]
        queries[block // 2, other, :] = piece[:, HD : 2 * HD]
        keys[place, :] = piece[:, 2 * HD : 3 * HD]
        values[place, :] = piece[:, 3 * HD :]


def forward_kernel(order_ref, load_ref, out_ref, queries, keys, values, mixed):
    sort_rows(order_ref, load_ref, queries, keys, values)
    step = 2 * BLK
    query_at = lax.broadcasted_iota(jnp.int32, (2 * step, step), 0) % step
    key_at = lax.broadcasted_iota(jnp.int32, (2 * step, step), 1)
    allowed = key_at <= query_at
    for i in range(keys.shape[0] // step):
        reach = (i + 1) * step
        query = queries[i]
        ahead = contract_last(query, keys[i * step : reach, :]) * scale
        ahead = jnp.where(allowed, ahead, masked_score)
        top = jnp.max(ahead, axis=1, keepdims=True)
        if i:
            before = contract_last(query, keys[: i * step, :]) * scale
            top = jnp.maximum(top, jnp.max(before, axis=1, keepdims=True))
        soft = jnp.exp(ahead - top)
        total = jnp.sum(soft, axis=1, keepdims=True)
        result = product(soft.astype(low), values[i * step : reach, :])
        if i:
            soft = jnp.exp(before - top)
            total = total + jnp.sum(soft, axis=1, keepdims=True)
            result = result + product(soft.astype(low), values[: i * step, :])
        result = (result / total).astype(low)
        mixed[i * step : reach, :HD] = result[:step]
        mixed[i * step : reach, HD:] = result[step:]
    for slot in range(2 * load_ref.shape[0]):
        place = pl.ds(pl.multiple_of(order_ref[slot] * BLK, BLK), BLK)
        slot_of(out_ref, slot)[...] = mixed[place, :]


def backward_kernel(
    order_ref, load_ref, grad_ref, out_ref, queries, keys, values, grads, key_sum, value_sum, sent
):
    sort_rows(order_ref, load_ref, queries, keys, values)
    step = 2 * BLK
    length = keys.shape[0]
    for slot in range(length // BLK):
        block = order_ref[slot]
        piece = slot_of(grad_ref, slot)[...]
        half = pl.ds(pl.multiple_of((block % 2) * BLK, BLK), BLK)
        other = pl.ds(pl.multiple_of((block % 2) * BLK + 2 * BLK, BLK), BLK)
        grads[block // 2, half, :] = piece[:, :HD]
        grads[block // 2, other, :] = piece[:, HD:]
    key_at = lax.broadcasted_iota(jnp.int32, (step, 2 * step), 0)
    query_at = lax.broadcasted_iota(jnp.int32, (step, 2 * step), 1) % step
    allowed = key_at <= query_at
    for i in range(length // step):
        query = queries[i]
        grad = grads[i]
        scores = []
        top = None
        for j in range(i + 1):
            score = contract_last(keys[j * step : (j + 1) * step, :], query) * scale
            if j == i:
                score = jnp.where(allowed, score, masked_score)
            high = jnp.max(score, axis=0, keepdims=True)
            top = high if top is None else jnp.maximum(top, high)
            scores.append(score)
        total = jnp.zeros_like(top)
        delta = jnp.zeros_like(top)
        softs = []
        slopes = []
        for j in range(i + 1):
            soft = jnp.exp(scores[j] - top)
            slope = contract_last(values[j * step : (j + 1) * step, :], grad)
            total = total + jnp.sum(soft, axis=0, keepdims=True)
            delta = delta + jnp.sum(soft * slope, axis=0, keepdims=True)
            softs.append(soft)
            slopes.append(slope)
        share = 1.0 / total
        delta = delta * share
        query_sum = jnp.zeros((2 * step, HD), wide)
        for j in range(i + 1):
            place = slice(j * step, (j + 1) * step)
            soft = softs[j] * share
            steep = (soft * (slopes[j] - delta)).astype(low)
            key_part = product(steep, query)
            value_part = product(soft.astype(low), grad)
            if j == i:
                key_sum[place, :] = key_part
                value_sum[place, :] = value_part
            else:
                key_sum[place, :] += key_part
                value_sum[place, :] += value_part
            query_sum = query_sum + contract_first(steep, keys[place, :])
        query_sum = (query_sum * scale).astype(low)
        sent[i * step : (i + 1) * step, :HD] = query_sum[:step]
        sent[i * step : (i + 1) * step, HD : 2 * HD] = query_sum[step:]
    sent[:, 2 * HD : 3 * HD] = (key_sum[...] * scale).astype(low)
    sent[:, 3 * HD :] = value_sum[...].astype(low)
    for slot in range(length // BLK):
        place = pl.ds(pl.multiple_of(order_ref[slot] * BLK, BLK), BLK)
        slot_of(out_ref, slot)[...] = sent[place, :]


def attention_call(kernel, order, arrays, width, scratch, products, name):
    devices, height = arrays[0].shape[:2]
    length = devices * height
    half = (length * length) // 2 * GROUP
    whole = pl.BlockSpec(memory_space=pltpu.VMEM)
    return pl.pallas_call(
        kernel,
        grid_spec=pltpu.PrefetchScalarGridSpec(
            num_scalar_prefetch=1,
            grid=(),
            in_specs=[whole] * len(arrays),
            out_specs=whole,
            scratch_shapes=scratch,
        ),
        out_shape=jax.ShapeDtypeStruct((devices, height, width), low),
        compiler_params=pltpu.CompilerParams(vmem_limit_bytes=56 << 20),
        cost_estimate=pl.CostEstimate(
            flops=2 * products * half * 256, bytes_accessed=8 * length * width, transcendentals=half
        ),
        name=name,
    )(order, *arrays)


def attention_forward(order, load):
    length = load.shape[0] * load.shape[1]
    scratch = [
        pltpu.VMEM((length // (2 * BLK), 4 * BLK, HD), low),
        pltpu.VMEM((length, HD), low),
        pltpu.VMEM((length, HD), low),
        pltpu.VMEM((length, 2 * HD), low),
    ]
    return attention_call(forward_kernel, order, (load,), 2 * HD, scratch, 2, "attention_forward")


def attention_backward(order, load, grad):
    length = load.shape[0] * load.shape[1]
    scratch = [
        pltpu.VMEM((length // (2 * BLK), 4 * BLK, HD), low),
        pltpu.VMEM((length, HD), low),
        pltpu.VMEM((length, HD), low),
        pltpu.VMEM((length // (2 * BLK), 4 * BLK, HD), low),
        pltpu.VMEM((length, HD), wide),
        pltpu.VMEM((length, HD), wide),
        pltpu.VMEM((length, 4 * HD), low),
    ]
    return attention_call(
        backward_kernel, order, (load, grad), 4 * HD, scratch, 5, "attention_backward"
    )


def scores_of(query_rot, keys_all, own_places, all_places, start, block_size):
    key_block = lax.dynamic_slice_in_dim(keys_all, start, block_size, 0)
    key_places = lax.dynamic_slice_in_dim(all_places, start, block_size, 0)
    raw = (
        jnp.einsum("rkgd,skd->rkgs", query_rot, key_block, preferred_element_type=wide) * scale
    )
    allowed = key_places[None, None, None, :] <= own_places[:, None, None, None]
    return (jnp.where(allowed, raw, masked_score), key_block)


def rows_forward(query_rot, keys_all, values_all, own_places, all_places):
    row_count = query_rot.shape[0]
    key_total = keys_all.shape[0]
    block_size = math.gcd(key_total, 512)

    def step(block_index, carry):
        top_score, total, mixed = carry
        start = block_index * block_size
        scores, _ = scores_of(query_rot, keys_all, own_places, all_places, start, block_size)
        value_block = lax.dynamic_slice_in_dim(values_all, start, block_size, 0)
        new_top = jnp.maximum(top_score, jnp.max(scores, axis=-1))
        soft = jnp.exp(scores - new_top[..., None])
        shrink = jnp.exp(top_score - new_top)
        total = total * shrink + jnp.sum(soft, axis=-1)
        mixed = mixed * shrink[..., None] + jnp.einsum(
            "rkgs,skd->rkgd", soft.astype(low), value_block, preferred_element_type=wide
        )
        return (new_top, total, mixed)

    start_top = jnp.full((row_count, HK, GROUP), masked_score, wide)
    start_total = jnp.zeros((row_count, HK, GROUP), wide)
    start_mixed = jnp.zeros((row_count, HK, GROUP, HD), wide)
    top_score, total, mixed = lax.fori_loop(
        0, key_total // block_size, step, (start_top, start_total, start_mixed)
    )
    return (mixed / total[..., None], top_score + jnp.log(total))


def rows_backward(
    query_rot, keys_all, values_all, own_places, all_places, log_total, delta, grad_mixed
):
    row_count = query_rot.shape[0]
    key_total = keys_all.shape[0]
    block_size = math.gcd(key_total, 512)

    def step(block_index, carry):
        grad_query, grad_keys, grad_values = carry
        start = block_index * block_size
        scores, key_block = scores_of(
            query_rot, keys_all, own_places, all_places, start, block_size
        )
        value_block = lax.dynamic_slice_in_dim(values_all, start, block_size, 0)
        soft = jnp.exp(scores - log_total[..., None])
        grad_soft = jnp.einsum(
            "rkgd,skd->rkgs", grad_mixed, value_block, preferred_element_type=wide
        )
        steep = (soft * (grad_soft - delta[..., None])).astype(low)
        grad_query = grad_query + scale * jnp.einsum(
            "rkgs,skd->rkgd", steep, key_block, preferred_element_type=wide
        )
        key_part = scale * jnp.einsum(
            "rkgs,rkgd->skd", steep, query_rot, preferred_element_type=wide
        )
        value_part = jnp.einsum(
            "rkgs,rkgd->skd", soft.astype(low), grad_mixed, preferred_element_type=wide
        )
        grad_keys = lax.dynamic_update_slice_in_dim(
            grad_keys, key_part.reshape(block_size, HK * HD), start, 0
        )
        grad_values = lax.dynamic_update_slice_in_dim(
            grad_values, value_part.reshape(block_size, HK * HD), start, 0
        )
        return (grad_query, grad_keys, grad_values)

    start_query = jnp.zeros((row_count, HK, GROUP, HD), wide)
    start_keys = jnp.zeros((key_total, HK * HD), wide)
    return lax.fori_loop(
        0, key_total // block_size, step, (start_query, start_keys, start_keys)
    )


def exchange_levels(cut):
    return [over_ctx(cut(k), 2 * k) for k in (1, 2, 3)]


def reduce_ctx(grad, dim, *others):
    here, size = lax.axis_index("ctx"), lax.axis_size("ctx")
    if size != 8:
        return lax.psum_scatter(grad, "ctx", scatter_dimension=dim, tiled=True)

    def cut(array, index, width):
        return lax.dynamic_slice_in_dim(array, index * width, width, dim)

    first, second = (others[:1], others[1:]) if others else ((), ())
    side, level = here % 2, here // 2
    half, piece = grad.shape[dim] // 2, grad.shape[dim] // 8
    got = after(over_ctx(cut(grad, 1 - side, half), 1), *first)
    kept = add_low(cut(grad, side, half), got)
    got = exchange_levels(lambda k: cut(kept, level ^ k, piece))
    got = [after(array, *second) for array in got]
    return add_low(cut(kept, level, piece), *got)


def place_code():
    here = lax.axis_index("ctx")
    return jnp.stack([(here % 2) * 4 + here // 2, lax.axis_index("fsdp")]).astype(jnp.int32)


def deal_fsdp(cut, *others):
    got = [over_fsdp(cut(k), k) for k in (1, 2, 3)]
    return jnp.stack([cut(0)] + [after(array, *others) for array in got])


def spread_rows_kernel(where_ref, *refs):
    parts, outs = refs[:5], refs[5:]
    piece = parts[0].shape[1]
    for i, out_ref in enumerate(outs):

        @pl.when(pl.program_id(0) // (4 // len(outs)) == i)
        def _(out_ref=out_ref):
            for k in range(8):
                part = parts[k][0] if k < 4 else parts[4][k - 4, 0]
                place = pl.multiple_of((where_ref[0] ^ k) * piece, piece)
                out_ref[pl.ds(place, piece), :] = part.astype(wide)


def spread_rows_call(near, far, count):
    _, height, width = near[0].shape
    each = 4 // count

    def place_of(number):
        return lambda i, where: (0, jnp.clip(i - number * each, 0, each - 1))

    return pl.pallas_call(
        spread_rows_kernel,
        grid_spec=pltpu.PrefetchScalarGridSpec(
            num_scalar_prefetch=1,
            grid=(4,),
            in_specs=[pl.BlockSpec((1, height, width), lambda i, where: (where[1] ^ i, 0, 0))] * 4
            + [pl.BlockSpec((4, 1, height, width), lambda i, where: (0, where[1] ^ i, 0, 0))],
            out_specs=[pl.BlockSpec((8 * height, width), place_of(k)) for k in range(count)],
        ),
        out_shape=[jax.ShapeDtypeStruct((8 * height, each * width), wide)] * count,
        cost_estimate=brief,
        name="spread_rows",
    )(place_code(), *near, far)


def dealt_grads(left, right, count, *others):
    size = lax.axis_size("ctx")
    grad = contract_first(left, right).astype(low).reshape(4, left.shape[1] // 4, right.shape[1])
    part = lax.axis_index("fsdp")
    piece = reduce_ctx(grad, 1, *others[:2])
    _, height, width = piece.shape
    mine = deal_fsdp(
        lambda k: lax.dynamic_index_in_dim(piece, part ^ k, 0, keepdims=False), *others[2:3]
    )
    if size != 8:
        whole = lax.all_gather(mine, "ctx", axis=1, tiled=True).astype(wide)
        blocks = [lax.dynamic_index_in_dim(whole, part ^ k, 0, keepdims=False) for k in range(4)]
        each = 4 // count
        whole = [jnp.concatenate(blocks[i * each : (i + 1) * each], axis=1) for i in range(count)]
        return [*whole, grad, piece, piece]
    near = [mine] + [after(array, *others[3:4]) for array in exchange_levels(lambda k: mine)]
    far = after(over_ctx(jnp.stack(near), 1), *others[4:5])
    return [*spread_rows_call(near, far, count), grad, piece, near[-1]]


ring = (0, 2, 4, 6, 7, 5, 3, 1)


def turn_ring(array, step):
    count = len(ring)
    return lax.ppermute(
        array, "ctx", [(ring[i], ring[(i + step) % count]) for i in range(count)]
    )


def deal_kernel(code_ref, *refs):
    count = len(ring)
    outs = refs[2 * count :]
    for lower in range(2):
        for step in range(count):
            part = refs[lower * count + step]
            height = part.shape[1]
            width = part.shape[2] // len(outs)
            place = pl.multiple_of(code_ref[1 + lower * count + step] * width, width)
            for i, out_ref in enumerate(outs):
                out_ref[lower * height : (lower + 1) * height, pl.ds(place, width)] = part[
                    0, :, i * width : (i + 1) * width
                ].astype(wide)


def gather_ring(mine, count):
    here, size, part = lax.axis_index("ctx"), lax.axis_size("ctx"), lax.axis_index("fsdp")
    _, height, span = mine.shape
    width = span // count * size
    if size != 8:
        whole = lax.all_gather(mine, "ctx", axis=0)
        whole = jnp.stack(
            [lax.dynamic_index_in_dim(whole, part ^ k, 1, keepdims=False) for k in range(4)]
        ).reshape(4, size, height, count, span // count)
        whole = whole.transpose(3, 2, 0, 1, 4).reshape(count, height, 4 * width)
        return tuple(whole[i].astype(wide) for i in range(count))
    upper, lower = [mine[:, : height // 2]], [mine[:, height // 2 :]]
    for _ in range(size - 1):
        upper.append(turn_ring(upper[-1], 1))
        lower.append(turn_ring(lower[-1], -1))
    order = jnp.asarray(ring, jnp.int32)
    turn = jnp.argmax(order == here).astype(jnp.int32)
    steps = jnp.arange(size, dtype=jnp.int32)
    code = jnp.concatenate(
        [part.reshape(1), order[(turn - steps) % size], order[(turn + steps) % size]]
    ).astype(jnp.int32)
    half = (1, height // 2, span)
    return pl.pallas_call(
        deal_kernel,
        grid_spec=pltpu.PrefetchScalarGridSpec(
            num_scalar_prefetch=1,
            grid=(4,),
            in_specs=[pl.BlockSpec(half, lambda i, code: (code[0] ^ i, 0, 0))] * (2 * size),
            out_specs=[pl.BlockSpec((height, width), lambda i, code: (0, i))] * count,
        ),
        out_shape=[jax.ShapeDtypeStruct((height, 4 * width), wide)] * count,
        compiler_params=pltpu.CompilerParams(vmem_limit_bytes=56 << 20),
        cost_estimate=brief,
        name="deal_columns",
    )(code, *upper, *lower)


def deal_rows(piece, *others):
    part = lax.axis_index("fsdp")
    return deal_fsdp(lambda k: rows(piece, part ^ k, piece.shape[0] // 4), *others)


def unit_grads_kernel(normed_ref, grad_ref, gate_ref, up_ref, hidden_ref, out_ref, flipped):
    @pl.when(pl.program_id(0) == 0)
    def _():
        flipped[0] = normed_ref[...].T
        flipped[1] = grad_ref[...].T

    piece = hidden_ref.shape[1]
    right = jnp.concatenate([gate_ref[...], up_ref[...]], axis=1)
    out_ref[:, : 2 * piece] = product(flipped[0], right).astype(low)
    out_ref[:, 2 * piece :] = product(flipped[1], hidden_ref[...]).astype(low)


def unit_grads(normed, grad, grad_gate, grad_up, hidden):
    size = lax.axis_size("ctx")
    count, depth = normed.shape
    piece = hidden.shape[1] // size
    rights = (grad_gate, grad_up, hidden)
    if piece % 128:
        cut = [
            contract_first(left, right).astype(low).reshape(depth, size, piece)
            for left, right in zip((normed, normed, grad), rights)
        ]
        return jnp.concatenate(cut, axis=2).transpose(1, 0, 2).reshape(size * depth, 3 * piece)
    whole = pl.BlockSpec(memory_space=pltpu.VMEM)
    return pl.pallas_call(
        unit_grads_kernel,
        grid=(size,),
        in_specs=[whole, whole] + [pl.BlockSpec((count, piece), lambda i: (0, i))] * 3,
        out_specs=pl.BlockSpec((depth, 3 * piece), lambda i: (i, 0)),
        scratch_shapes=[pltpu.VMEM((2, depth, count), low)],
        out_shape=jax.ShapeDtypeStruct((size * depth, 3 * piece), low),
        compiler_params=pltpu.CompilerParams(vmem_limit_bytes=40 << 20),
        cost_estimate=lasting,
        name="unit_grads",
    )(normed, grad, *rights)


def sum_gains(array, *others):
    part, size = lax.axis_index("fsdp"), lax.axis_size("ctx")
    width = array.shape[1] // 4
    array = jnp.sum(deal_fsdp(lambda k: columns(array, part ^ k, width)), axis=0)
    array = array + after(over_ctx(array, 1), others[0])
    if size == 8:
        return array + sum(after(got, others[1]) for got in exchange_levels(lambda k: array))
    bits = 2
    while bits < size:
        array = array + over_ctx(array, bits)
        bits *= 2
    return array


def body(
    hidden_in,
    out_grad,
    positions,
    attn_gain,
    w_query,
    w_key,
    w_value,
    w_out,
    ffn_gain,
    w_gate,
    w_up,
    w_down,
):
    part, here, size = lax.axis_index("fsdp"), lax.axis_index("ctx"), lax.axis_size("ctx")
    code = jnp.stack([part, here % 2, here // 2 % 2]).astype(jnp.int32)
    own_gains = jnp.stack([attn_gain, ffn_gain])
    gains = [own_gains] + [over_fsdp(own_gains, k) for k in (1, 2, 3)]
    rows_in, grad_down = hidden_in[0], out_grad[0]
    row_count = rows_in.shape[0]
    all_places = positions[0]
    own_places = lax.dynamic_slice_in_dim(all_places, here * row_count, row_count, 0)
    cosine, sine = angles_of(own_places)
    cosine = jnp.concatenate([cosine[:, 0], cosine[:, 0]], axis=1)
    sine = jnp.concatenate([-sine[:, 0], sine[:, 0]], axis=1)

    heads = gather_thirds(jnp.concatenate([w_query, w_key, w_value], axis=1))
    normed_one, load = heads_call(code, rows_in, cosine, sine, gains, heads)
    outward = gather_halves(w_out)
    own, near, far, both = deal_weights((w_gate, w_up, w_down))
    load, near, far, both, _ = lax.optimization_barrier((load, near, far, both, outward[2]))
    far, both = over_fsdp(far, 2), over_fsdp(both, 3)
    near = over_fsdp(near, 1)
    far_other, both_other = over_ctx(far, 1), over_ctx(both, 2)
    grad_all = gather_fsdp(grad_down)

    if size == HK:
        load = lax.all_to_all(load, "ctx", 0, 0, tiled=True)
        order = all_places[::BLK] // BLK
        mixed = attention_forward(order, load)
        mixed = lax.all_to_all(after(mixed, far, outward[3]), "ctx", 0, 0, tiled=True)
    else:
        query_rot = load[:, :, : GROUP * HD].transpose(1, 0, 2)
        query_rot = query_rot.reshape(row_count, HK, GROUP, HD)
        keys_values = load[:, :, GROUP * HD :].transpose(1, 0, 2)
        keys_values = lax.all_gather(keys_values, "ctx", axis=0, tiled=True)
        keys_all, values_all = keys_values[:, :, :HD], keys_values[:, :, HD:]
        mixed_exact, log_total = rows_forward(
            query_rot, keys_all, values_all, own_places, all_places
        )
        mixed = mixed_exact.reshape(row_count, HK, GROUP * HD).transpose(1, 0, 2).astype(low)

    dealt = (own, near, far, far_other, both, both_other)
    mixed_low, middle, normed_two = middle_call(
        code, rows_in, after(mixed, both, far_other, grad_all), gains, outward
    )
    normed_all = gather_fsdp(normed_two, both_other)
    out_terms, back_terms, hidden, grad_gate, grad_up = units_call(
        code, normed_all, grad_all, dealt
    )
    grad_normed_two, passed = scatter_fsdp(back_terms)
    unit_terms = unit_grads(normed_all, grad_all, after(grad_gate, passed), grad_up, hidden)
    grad_normed_two, unit_terms = lax.optimization_barrier((grad_normed_two, unit_terms))
    grad_middle, grad_branch, grad_mixed, grad_gain_two = middle_back_call(
        code, middle, grad_normed_two, grad_down, gains, outward
    )
    unit_sums = lax.psum_scatter(unit_terms, "ctx", scatter_dimension=0, tiled=True)

    if size == HK:
        grad_mixed = lax.all_to_all(grad_mixed, "ctx", 0, 0, tiled=True)
        grad_load = attention_backward(order, load, grad_mixed)
        mid = grad_load
        grad_load = lax.all_to_all(grad_load, "ctx", 0, 0, tiled=True)
    else:
        grad_mixed = grad_mixed.transpose(1, 0, 2).reshape(row_count, HK, GROUP, HD)
        delta = jnp.sum(grad_mixed.astype(wide) * mixed_exact, axis=-1)
        grad_query, grad_keys, grad_values = rows_backward(
            query_rot, keys_all, values_all, own_places, all_places, log_total, delta, grad_mixed
        )
        grad_keys, grad_values = (
            lax.psum_scatter(whole.astype(low), "ctx", scatter_dimension=0, tiled=True)
            for whole in (grad_keys, grad_values)
        )
        grad_load = jnp.concatenate(
            [
                grad_query.reshape(row_count, HK, GROUP * HD).astype(low),
                grad_keys.reshape(row_count, HK, HD),
                grad_values.reshape(row_count, HK, HD),
            ],
            axis=2,
        ).transpose(1, 0, 2)
        mid = grad_load

    grad_raw, input_grad, grad_gain_one = heads_back_call(
        code, grad_load, rows_in, grad_middle, cosine, sine, gains, heads
    )
    early, late = grad_branch, input_grad
    result, _ = scatter_fsdp(after(out_terms, grad_normed_two), mid)
    result = (middle + result).astype(low)
    quarter = HQ * HD // 4
    turn = (0, 2, 1, 3)

    def own_columns(cut, *others):
        dealt = deal_fsdp(cut, *others)
        return jnp.concatenate([dealt[k] for k in turn], axis=0)

    branch_all = gather_fsdp(grad_branch, mid)
    mixed_part = own_columns(lambda k: columns(mixed_low, part ^ k, quarter), mid)
    normed_one_all = gather_fsdp(after(normed_one, early), mid)
    out_weight_grad, *_ = dealt_grads(branch_all, mixed_part, 1, mid, late, late, late, late)

    def raw_part(i):
        return own_columns(
            lambda k: lax.dynamic_index_in_dim(grad_raw[i], part ^ k, 0, keepdims=False)
        )

    query_grad, first_terms, summed, last = dealt_grads(normed_one_all, raw_part(0), 1)
    key_grad, value_grad, second_terms, *_ = dealt_grads(normed_one_all, raw_part(1), 2)
    unit_sums = after(unit_sums, first_terms, second_terms)
    gate_grad, up_grad, down_grad = gather_ring(deal_rows(unit_sums), 3)
    gain_grads = sum_gains(
        jnp.concatenate([grad_gain_one, grad_gain_two], axis=0), summed, last
    )
    return (
        result[None],
        input_grad[None],
        gain_grads[0],
        query_grad,
        key_grad,
        value_grad,
        out_weight_grad,
        gain_grads[1],
        gate_grad,
        up_grad,
        down_grad,
    )


def solution(mesh):
    matrix = P("fsdp", None)
    stream = P("fsdp", "ctx", None)
    return jax.shard_map(
        body,
        mesh=mesh,
        in_specs=(stream, stream, matrix, P("fsdp"))
        + (matrix,) * 4
        + (P("fsdp"),)
        + (matrix,) * 3,
        out_specs=(stream, stream, P("fsdp")) + (matrix,) * 4 + (P("fsdp"),) + (matrix,) * 3,
        check_vma=False,
    )
```

```python
import math

import jax
import jax.numpy as jnp
from jax import lax
from jax.experimental import pallas as pl
from jax.experimental.pallas import tpu as pltpu
from jax.sharding import PartitionSpec as P

HQ = 16
HK = 8
HD = 96
GROUP = HQ // HK
BLK = 128

epsilon = 1e-05
rope_base = 100000.0
masked_score = -1e30
scale = 1.0 / math.sqrt(HD)
low = jnp.bfloat16
wide = jnp.float32
brief = pl.CostEstimate(flops=0, bytes_accessed=0, transcendentals=0)
lasting = pl.CostEstimate(flops=10**11, bytes_accessed=0, transcendentals=0)


def angles_of(places):
    frequency = jnp.exp(jnp.arange(HD // 2, dtype=wide) * (-2.0 * math.log(rope_base) / HD))
    turned = places.astype(wide)[:, None] * frequency[None, :]
    return (jnp.cos(turned)[:, None, :], jnp.sin(turned)[:, None, :])


def product(left, right):
    return jnp.dot(left, right, preferred_element_type=wide)


def contract_last(left, right):
    return lax.dot_general(left, right, (((1,), (1,)), ((), ())), preferred_element_type=wide)


def contract_first(left, right):
    return lax.dot_general(left, right, (((0,), (0,)), ((), ())), preferred_element_type=wide)


def swap(array, axis, bits, size):
    return lax.ppermute(array, axis, [(i, i ^ bits) for i in range(size)])


def over_fsdp(array, bits):
    return swap(array, "fsdp", bits, 4)


def over_ctx(array, bits):
    return swap(array, "ctx", bits, lax.axis_size("ctx"))


def columns(array, index, width):
    return lax.dynamic_slice_in_dim(array, index * width, width, array.ndim - 1)


def rows(array, index, height):
    return lax.dynamic_slice_in_dim(array, index * height, height, 0)


def together(*arrays):
    return lax.optimization_barrier(arrays)


def after(array, *others):
    return lax.optimization_barrier((array, *others))[0]


def add_low(first, *others):
    total = first.astype(wide)
    for other in others:
        total = total + other.astype(wide)
    return total.astype(low)


def gather_fsdp(array, *others):
    far = after(over_fsdp(array, 2), *others)
    pair = over_fsdp(jnp.concatenate([array, far], axis=0), 1)
    return jnp.concatenate([array, far, pair], axis=0)


def scatter_fsdp(terms, *others):
    half, height = terms.shape[0] // 2, terms.shape[0] // 4
    kept, got = terms[:half], over_fsdp(terms[half:], 1)
    passed = add_low(kept[height:], got[height:])
    away = after(over_fsdp(passed, 2), *others)
    total = kept[:height].astype(wide) + got[:height].astype(wide) + away.astype(wide)
    return total, passed


ALL, REST, MINE, OTHER = 0, 3, 4, 8
heads_plan = (
    (0, ALL),
    (1, ALL),
    (2, MINE + 1),
    (2, OTHER + 1),
    (2, REST),
    (3, MINE + 1),
    (3, OTHER + 1),
    (3, REST),
)
outward_plan = ((0, ALL), (1, ALL), (2, MINE + 2), (2, OTHER + 2), (3, MINE + 2), (3, OTHER + 2))
units_plan = ((0, ALL), (1, ALL), (2, MINE + 1), (2, OTHER + 1), (3, MINE + 2), (3, OTHER + 2))


def gather_thirds(own, *others):
    side = lax.axis_index("ctx") % 2
    third = own.shape[1] // 3
    far = after(over_fsdp(columns(own, side, third), 2), *others)
    rest = over_fsdp(after(own[:, 2 * third :], far), 2)
    near = over_fsdp(own, 1)
    other = over_ctx(far, 1)
    return (
        own,
        near,
        far,
        other,
        rest,
        over_fsdp(far, 1),
        over_fsdp(other, 1),
        over_fsdp(rest, 1),
    )


def gather_halves(own):
    far = over_fsdp(columns(own, lax.axis_index("ctx") // 2 % 2, own.shape[1] // 2), 2)
    near = over_fsdp(own, 1)
    other = over_ctx(far, 2)
    return (own, near, far, other, over_fsdp(far, 1), over_fsdp(other, 1))


def fill_weight(code_ref, plan, pieces, out):
    part = code_ref[0]
    for (k, which), piece in zip(plan, pieces):
        height, width = piece.shape
        across = pl.ds(pl.multiple_of((part ^ k) * height, height), height)
        if which == ALL:
            out[across, :] = piece[...]
        elif which == REST:
            out[across, 2 * width :] = piece[...]
        else:
            side = code_ref[which % MINE]
            place = 1 - side if which >= OTHER else side
            out[across, lanes(place, width)] = piece[...]


def whole_call(kernel, code, arrays, outs, scratch, flops, name):
    spec = pl.BlockSpec(memory_space=pltpu.VMEM)
    moved = sum(math.prod(a.shape) * a.dtype.itemsize for a in (*arrays, *outs))
    return pl.pallas_call(
        kernel,
        grid_spec=pltpu.PrefetchScalarGridSpec(
            num_scalar_prefetch=1,
            grid=(),
            in_specs=[spec] * len(arrays),
            out_specs=[spec] * len(outs),
            scratch_shapes=scratch,
        ),
        out_shape=outs,
        compiler_params=pltpu.CompilerParams(vmem_limit_bytes=56 << 20),
        cost_estimate=pl.CostEstimate(flops=flops, bytes_accessed=moved, transcendentals=0),
        name=name,
    )(code, *arrays)


def lanes(index, width):
    return pl.ds(pl.multiple_of(index * width, 128), width)


def gained(code_ref, gains, row, out):
    for k in range(4):
        out[:, lanes(code_ref[0] ^ k, gains[k].shape[1])] = gains[k][row : row + 1, :].astype(wide)


def turned(values, cosine, sine):
    half = values.shape[1] // 2
    return values * cosine + jnp.concatenate([values[:, half:], values[:, :half]], axis=1) * sine


def inverse_rms(values):
    return lax.rsqrt(jnp.mean(values * values, axis=1, keepdims=True) + epsilon)


def slot_of_head(head):
    if head < HQ:
        return head // GROUP, head % GROUP
    return (head - HQ) % HK, GROUP + (head - HQ) // HK


def heads_kernel(code_ref, rows_ref, cosine_ref, sine_ref, *refs):
    gains, pieces = refs[:4], refs[4:12]
    normed_ref, load_ref, gain, weight, total = refs[12:]
    gained(code_ref, gains, 0, gain)
    fill_weight(code_ref, heads_plan, pieces, weight)
    values = rows_ref[...].astype(wide)
    normed_ref[...] = (values * inverse_rms(values) * gain[...]).astype(low)
    total[...] = product(normed_ref[...], weight[...])
    cosine, sine = cosine_ref[...], sine_ref[...]
    for head in range(HQ + 2 * HK):
        part = total[:, head * HD : (head + 1) * HD]
        if head < HQ + HK:
            part = turned(part, cosine, sine)
        group, place = slot_of_head(head)
        load_ref[group, :, place * HD : (place + 1) * HD] = part.astype(low)


def heads_call(code, rows_in, cosine, sine, gains, pieces):
    count, width = rows_in.shape
    total = pieces[0].shape[1]
    outs = [
        jax.ShapeDtypeStruct((count, width), low),
        jax.ShapeDtypeStruct((HK, count, (GROUP + 2) * HD), low),
    ]
    scratch = [
        pltpu.VMEM((1, width), wide),
        pltpu.VMEM((width, total), low),
        pltpu.VMEM((count, total), wide),
    ]
    return whole_call(
        heads_kernel,
        code,
        (rows_in, cosine, sine, *gains, *pieces),
        outs,
        scratch,
        2 * count * width * total,
        "query_key_value",
    )


def middle_kernel(code_ref, rows_ref, mixed_ref, *refs):
    gains, pieces = refs[:4], refs[4:10]
    flat_ref, middle_ref, normed_ref, gain, weight = refs[10:]
    gained(code_ref, gains, 1, gain)
    fill_weight(code_ref, outward_plan, pieces, weight)
    span = mixed_ref.shape[2]
    for group in range(mixed_ref.shape[0]):
        flat_ref[:, group * span : (group + 1) * span] = mixed_ref[group]
    middle = contract_last(flat_ref[...], weight[...]) + rows_ref[...].astype(wide)
    middle_ref[...] = middle
    normed_ref[...] = (middle * inverse_rms(middle) * gain[...]).astype(low)


def middle_call(code, rows_in, mixed, gains, pieces):
    count, width = rows_in.shape
    outs = [
        jax.ShapeDtypeStruct((count, HQ * HD), low),
        jax.ShapeDtypeStruct((count, width), wide),
        jax.ShapeDtypeStruct((count, width), low),
    ]
    return whole_call(
        middle_kernel,
        code,
        (rows_in, mixed, *gains, *pieces),
        outs,
        [pltpu.VMEM((1, width), wide), pltpu.VMEM((width, HQ * HD), low)],
        2 * count * width * HQ * HD,
        "attention_output",
    )


def norm_back(values, gain, grad):
    inverse = inverse_rms(values)
    weighted = gain * grad
    inner = jnp.mean(values * weighted, axis=1, keepdims=True)
    back = inverse * weighted - values * inverse * inverse * inverse * inner
    return back, jnp.sum(grad * values * inverse, axis=0, keepdims=True)


def middle_back_kernel(code_ref, middle_ref, grad_ref, out_grad_ref, *refs):
    gains, pieces = refs[:4], refs[4:10]
    grad_middle_ref, branch_ref, sent_ref, gain_grad_ref, gain, weight = refs[10:]
    gained(code_ref, gains, 1, gain)
    fill_weight(code_ref, outward_plan, pieces, weight)
    back, gain_grad_ref[...] = norm_back(middle_ref[...], gain[...], grad_ref[...])
    grad_middle = out_grad_ref[...].astype(wide) + back
    grad_middle_ref[...] = grad_middle
    branch_ref[...] = grad_middle.astype(low)
    total = product(branch_ref[...], weight[...]).astype(low)
    span = sent_ref.shape[2]
    for group in range(sent_ref.shape[0]):
        sent_ref[group] = total[:, group * span : (group + 1) * span]


def middle_back_call(code, middle, grad, out_grad, gains, pieces):
    count, width = middle.shape
    outs = [
        jax.ShapeDtypeStruct((count, width), wide),
        jax.ShapeDtypeStruct((count, width), low),
        jax.ShapeDtypeStruct((HK, count, GROUP * HD), low),
        jax.ShapeDtypeStruct((1, width), wide),
    ]
    return whole_call(
        middle_back_kernel,
        code,
        (middle, grad, out_grad, *gains, *pieces),
        outs,
        [pltpu.VMEM((1, width), wide), pltpu.VMEM((width, HQ * HD), low)],
        2 * count * width * HQ * HD,
        "attention_output_back",
    )


def heads_back_kernel(
    code_ref, load_ref, rows_ref, grad_middle_ref, cosine_ref, sine_ref, *refs
):
    gains, pieces = refs[:4], refs[4:12]
    raw_ref, input_grad_ref, gain_grad_ref, gain, weight, raw = refs[12:]
    gained(code_ref, gains, 0, gain)
    fill_weight(code_ref, heads_plan, pieces, weight)
    cosine, sine = cosine_ref[...], sine_ref[...]
    for head in range(HQ + 2 * HK):
        group, place = slot_of_head(head)
        part = load_ref[group, :, place * HD : (place + 1) * HD]
        if head < HQ + HK:
            part = turned(part.astype(wide), cosine, -sine).astype(low)
        raw[:, head * HD : (head + 1) * HD] = part
    quarter = raw_ref.shape[2] // 2
    for k in range(4):
        for i in range(2):
            first = (4 * i + k) * quarter
            raw_ref[k, :, i * quarter : (i + 1) * quarter] = raw[:, first : first + quarter]
    grad = contract_last(raw[...], weight[...])
    back, gain_grad_ref[...] = norm_back(rows_ref[...].astype(wide), gain[...], grad)
    input_grad_ref[...] = grad_middle_ref[...] + back


def heads_back_call(code, load, rows_in, grad_middle, cosine, sine, gains, pieces):
    count, width = rows_in.shape
    total = pieces[0].shape[1]
    outs = [
        jax.ShapeDtypeStruct((4, count, total // 4), low),
        jax.ShapeDtypeStruct((count, width), wide),
        jax.ShapeDtypeStruct((1, width), wide),
    ]
    return whole_call(
        heads_back_kernel,
        code,
        (load, rows_in, grad_middle, cosine, sine, *gains, *pieces),
        outs,
        [
            pltpu.VMEM((1, width), wide),
            pltpu.VMEM((width, total), low),
            pltpu.VMEM((count, total), low),
        ],
        2 * count * width * total,
        "query_key_value_back",
    )


def units_kernel(code_ref, normed_ref, grad_ref, *refs):
    pieces = refs[:6]
    out_ref, back_ref, hidden_ref, grad_gate_ref, grad_up_ref, weights = refs[6:]

    @pl.when(pl.program_id(0) == 0)
    def _():
        for i in range(3):
            fill_weight(code_ref, units_plan, [piece.at[i] for piece in pieces], weights.at[i])

    gate = product(normed_ref[...], weights[0])
    upward = product(normed_ref[...], weights[1])
    sigmoid_gate = jax.nn.sigmoid(gate)
    swish = gate * sigmoid_gate
    hidden = (swish * upward).astype(low)
    hidden_ref[...] = hidden
    grad_hidden = product(grad_ref[...], weights[2])
    grad_gate = (
        grad_hidden * upward * sigmoid_gate * (1.0 + gate * (1.0 - sigmoid_gate))
    ).astype(low)
    grad_up = (grad_hidden * swish).astype(low)
    grad_gate_ref[...] = grad_gate
    grad_up_ref[...] = grad_up
    back_ref[...] = (
        contract_last(grad_gate, weights[0]) + contract_last(grad_up, weights[1])
    ).astype(low)
    out_ref[...] = contract_last(hidden, weights[2]).astype(low)


def units_call(code, normed, grad, pieces):
    count, width = normed.shape
    units = pieces[0].shape[2]
    tile = 512
    wide_block = pl.BlockSpec((tile, width), lambda i, code: (i, 0))
    unit_block = pl.BlockSpec((tile, units), lambda i, code: (i, 0))
    return pl.pallas_call(
        units_kernel,
        grid_spec=pltpu.PrefetchScalarGridSpec(
            num_scalar_prefetch=1,
            grid=(count // tile,),
            in_specs=[wide_block, wide_block]
            + [pl.BlockSpec(memory_space=pltpu.VMEM)] * len(pieces),
            out_specs=[wide_block, wide_block, unit_block, unit_block, unit_block],
            scratch_shapes=[pltpu.VMEM((3, width, units), low)],
        ),
        out_shape=[jax.ShapeDtypeStruct((count, width), low)] * 2
        + [jax.ShapeDtypeStruct((count, units), low)] * 3,
        compiler_params=pltpu.CompilerParams(vmem_limit_bytes=60 << 20),
        cost_estimate=pl.CostEstimate(
            flops=12 * count * width * units,
            bytes_accessed=8 * count * width + 6 * width * units,
            transcendentals=count * units,
        ),
        name="feed_forward",
    )(code, normed, grad, *pieces)


def deal_weights(weights):
    part, here = lax.axis_index("fsdp"), lax.axis_index("ctx")
    width = weights[0].shape[1] // 4

    def taken(k):
        return jnp.stack([columns(weight, part ^ k, width) for weight in weights])

    def half(k, side):
        return jnp.stack(
            [columns(weight, (part ^ k) * 2 + side, width // 2) for weight in weights]
        )

    return taken(0), taken(1), half(2, here % 2), half(3, here // 2 % 2)


def slot_of(ref, slot):
    return ref.at[slot // 2, (slot % 2) * BLK : (slot % 2 + 1) * BLK, :]


def sort_rows(order_ref, load_ref, queries, keys, values):
    for slot in range(2 * load_ref.shape[0]):
        block = order_ref[slot]
        piece = slot_of(load_ref, slot)[...]
        place = pl.ds(pl.multiple_of(block * BLK, BLK), BLK)
        half = pl.ds(pl.multiple_of((block % 2) * BLK, BLK), BLK)
        other = pl.ds(pl.multiple_of((block % 2) * BLK + 2 * BLK, BLK), BLK)
        queries[block // 2, half, :] = piece[:, :HD]
        queries[block // 2, other, :] = piece[:, HD : 2 * HD]
        keys[place, :] = piece[:, 2 * HD : 3 * HD]
        values[place, :] = piece[:, 3 * HD :]


def forward_kernel(order_ref, load_ref, out_ref, queries, keys, values, mixed):
    sort_rows(order_ref, load_ref, queries, keys, values)
    step = 2 * BLK
    query_at = lax.broadcasted_iota(jnp.int32, (2 * step, step), 0) % step
    key_at = lax.broadcasted_iota(jnp.int32, (2 * step, step), 1)
    allowed = key_at <= query_at
    for i in range(keys.shape[0] // step):
        reach = (i + 1) * step
        query = queries[i]
        ahead = contract_last(query, keys[i * step : reach, :]) * scale
        ahead = jnp.where(allowed, ahead, masked_score)
        top = jnp.max(ahead, axis=1, keepdims=True)
        if i:
            before = contract_last(query, keys[: i * step, :]) * scale
            top = jnp.maximum(top, jnp.max(before, axis=1, keepdims=True))
        soft = jnp.exp(ahead - top)
        total = jnp.sum(soft, axis=1, keepdims=True)
        result = product(soft.astype(low), values[i * step : reach, :])
        if i:
            soft = jnp.exp(before - top)
            total = total + jnp.sum(soft, axis=1, keepdims=True)
            result = result + product(soft.astype(low), values[: i * step, :])
        result = (result / total).astype(low)
        mixed[i * step : reach, :HD] = result[:step]
        mixed[i * step : reach, HD:] = result[step:]
    for slot in range(2 * load_ref.shape[0]):
        place = pl.ds(pl.multiple_of(order_ref[slot] * BLK, BLK), BLK)
        slot_of(out_ref, slot)[...] = mixed[place, :]


def backward_kernel(
    order_ref, load_ref, grad_ref, out_ref, queries, keys, values, grads, key_sum, value_sum, sent
):
    sort_rows(order_ref, load_ref, queries, keys, values)
    step = 2 * BLK
    length = keys.shape[0]
    for slot in range(length // BLK):
        block = order_ref[slot]
        piece = slot_of(grad_ref, slot)[...]
        half = pl.ds(pl.multiple_of((block % 2) * BLK, BLK), BLK)
        other = pl.ds(pl.multiple_of((block % 2) * BLK + 2 * BLK, BLK), BLK)
        grads[block // 2, half, :] = piece[:, :HD]
        grads[block // 2, other, :] = piece[:, HD:]
    key_at = lax.broadcasted_iota(jnp.int32, (step, 2 * step), 0)
    query_at = lax.broadcasted_iota(jnp.int32, (step, 2 * step), 1) % step
    allowed = key_at <= query_at
    for i in range(length // step):
        query = queries[i]
        grad = grads[i]
        scores = []
        top = None
        for j in range(i + 1):
            score = contract_last(keys[j * step : (j + 1) * step, :], query) * scale
            if j == i:
                score = jnp.where(allowed, score, masked_score)
            high = jnp.max(score, axis=0, keepdims=True)
            top = high if top is None else jnp.maximum(top, high)
            scores.append(score)
        total = jnp.zeros_like(top)
        delta = jnp.zeros_like(top)
        softs = []
        slopes = []
        for j in range(i + 1):
            soft = jnp.exp(scores[j] - top)
            slope = contract_last(values[j * step : (j + 1) * step, :], grad)
            total = total + jnp.sum(soft, axis=0, keepdims=True)
            delta = delta + jnp.sum(soft * slope, axis=0, keepdims=True)
            softs.append(soft)
            slopes.append(slope)
        share = 1.0 / total
        delta = delta * share
        query_sum = jnp.zeros((2 * step, HD), wide)
        for j in range(i + 1):
            place = slice(j * step, (j + 1) * step)
            soft = softs[j] * share
            steep = (soft * (slopes[j] - delta)).astype(low)
            key_part = product(steep, query)
            value_part = product(soft.astype(low), grad)
            if j == i:
                key_sum[place, :] = key_part
                value_sum[place, :] = value_part
            else:
                key_sum[place, :] += key_part
                value_sum[place, :] += value_part
            query_sum = query_sum + contract_first(steep, keys[place, :])
        query_sum = (query_sum * scale).astype(low)
        sent[i * step : (i + 1) * step, :HD] = query_sum[:step]
        sent[i * step : (i + 1) * step, HD : 2 * HD] = query_sum[step:]
    sent[:, 2 * HD : 3 * HD] = (key_sum[...] * scale).astype(low)
    sent[:, 3 * HD :] = value_sum[...].astype(low)
    for slot in range(length // BLK):
        place = pl.ds(pl.multiple_of(order_ref[slot] * BLK, BLK), BLK)
        slot_of(out_ref, slot)[...] = sent[place, :]


def attention_call(kernel, order, arrays, width, scratch, products, name):
    devices, height = arrays[0].shape[:2]
    length = devices * height
    half = (length * length) // 2 * GROUP
    whole = pl.BlockSpec(memory_space=pltpu.VMEM)
    return pl.pallas_call(
        kernel,
        grid_spec=pltpu.PrefetchScalarGridSpec(
            num_scalar_prefetch=1,
            grid=(),
            in_specs=[whole] * len(arrays),
            out_specs=whole,
            scratch_shapes=scratch,
        ),
        out_shape=jax.ShapeDtypeStruct((devices, height, width), low),
        compiler_params=pltpu.CompilerParams(vmem_limit_bytes=56 << 20),
        cost_estimate=pl.CostEstimate(
            flops=2 * products * half * 256, bytes_accessed=8 * length * width, transcendentals=half
        ),
        name=name,
    )(order, *arrays)


def attention_forward(order, load):
    length = load.shape[0] * load.shape[1]
    scratch = [
        pltpu.VMEM((length // (2 * BLK), 4 * BLK, HD), low),
        pltpu.VMEM((length, HD), low),
        pltpu.VMEM((length, HD), low),
        pltpu.VMEM((length, 2 * HD), low),
    ]
    return attention_call(forward_kernel, order, (load,), 2 * HD, scratch, 2, "attention_forward")


def attention_backward(order, load, grad):
    length = load.shape[0] * load.shape[1]
    scratch = [
        pltpu.VMEM((length // (2 * BLK), 4 * BLK, HD), low),
        pltpu.VMEM((length, HD), low),
        pltpu.VMEM((length, HD), low),
        pltpu.VMEM((length // (2 * BLK), 4 * BLK, HD), low),
        pltpu.VMEM((length, HD), wide),
        pltpu.VMEM((length, HD), wide),
        pltpu.VMEM((length, 4 * HD), low),
    ]
    return attention_call(
        backward_kernel, order, (load, grad), 4 * HD, scratch, 5, "attention_backward"
    )


def scores_of(query_rot, keys_all, own_places, all_places, start, block_size):
    key_block = lax.dynamic_slice_in_dim(keys_all, start, block_size, 0)
    key_places = lax.dynamic_slice_in_dim(all_places, start, block_size, 0)
    raw = (
        jnp.einsum("rkgd,skd->rkgs", query_rot, key_block, preferred_element_type=wide) * scale
    )
    allowed = key_places[None, None, None, :] <= own_places[:, None, None, None]
    return (jnp.where(allowed, raw, masked_score), key_block)


def rows_forward(query_rot, keys_all, values_all, own_places, all_places):
    row_count = query_rot.shape[0]
    key_total = keys_all.shape[0]
    block_size = math.gcd(key_total, 512)

    def step(block_index, carry):
        top_score, total, mixed = carry
        start = block_index * block_size
        scores, _ = scores_of(query_rot, keys_all, own_places, all_places, start, block_size)
        value_block = lax.dynamic_slice_in_dim(values_all, start, block_size, 0)
        new_top = jnp.maximum(top_score, jnp.max(scores, axis=-1))
        soft = jnp.exp(scores - new_top[..., None])
        shrink = jnp.exp(top_score - new_top)
        total = total * shrink + jnp.sum(soft, axis=-1)
        mixed = mixed * shrink[..., None] + jnp.einsum(
            "rkgs,skd->rkgd", soft.astype(low), value_block, preferred_element_type=wide
        )
        return (new_top, total, mixed)

    start_top = jnp.full((row_count, HK, GROUP), masked_score, wide)
    start_total = jnp.zeros((row_count, HK, GROUP), wide)
    start_mixed = jnp.zeros((row_count, HK, GROUP, HD), wide)
    top_score, total, mixed = lax.fori_loop(
        0, key_total // block_size, step, (start_top, start_total, start_mixed)
    )
    return (mixed / total[..., None], top_score + jnp.log(total))


def rows_backward(
    query_rot, keys_all, values_all, own_places, all_places, log_total, delta, grad_mixed
):
    row_count = query_rot.shape[0]
    key_total = keys_all.shape[0]
    block_size = math.gcd(key_total, 512)

    def step(block_index, carry):
        grad_query, grad_keys, grad_values = carry
        start = block_index * block_size
        scores, key_block = scores_of(
            query_rot, keys_all, own_places, all_places, start, block_size
        )
        value_block = lax.dynamic_slice_in_dim(values_all, start, block_size, 0)
        soft = jnp.exp(scores - log_total[..., None])
        grad_soft = jnp.einsum(
            "rkgd,skd->rkgs", grad_mixed, value_block, preferred_element_type=wide
        )
        steep = (soft * (grad_soft - delta[..., None])).astype(low)
        grad_query = grad_query + scale * jnp.einsum(
            "rkgs,skd->rkgd", steep, key_block, preferred_element_type=wide
        )
        key_part = scale * jnp.einsum(
            "rkgs,rkgd->skd", steep, query_rot, preferred_element_type=wide
        )
        value_part = jnp.einsum(
            "rkgs,rkgd->skd", soft.astype(low), grad_mixed, preferred_element_type=wide
        )
        grad_keys = lax.dynamic_update_slice_in_dim(
            grad_keys, key_part.reshape(block_size, HK * HD), start, 0
        )
        grad_values = lax.dynamic_update_slice_in_dim(
            grad_values, value_part.reshape(block_size, HK * HD), start, 0
        )
        return (grad_query, grad_keys, grad_values)

    start_query = jnp.zeros((row_count, HK, GROUP, HD), wide)
    start_keys = jnp.zeros((key_total, HK * HD), wide)
    return lax.fori_loop(
        0, key_total // block_size, step, (start_query, start_keys, start_keys)
    )


def exchange_levels(cut):
    return [over_ctx(cut(k), 2 * k) for k in (1, 2, 3)]


def deal_fsdp(cut, *others):
    got = [over_fsdp(cut(k), k) for k in (1, 2, 3)]
    return jnp.stack([cut(0)] + [after(array, *others) for array in got])


def terms_of(left, right):
    return contract_first(left, right).astype(low).reshape(4, left.shape[1] // 4, right.shape[1])


def side_of(terms, other):
    side, half = lax.axis_index("ctx") % 2, terms.shape[1] // 2
    return lax.dynamic_slice_in_dim(terms, (side ^ other) * half, half, 1)


def level_of(terms, k):
    level, quarter = lax.axis_index("ctx") // 2, terms.shape[1] // 4
    return lax.dynamic_slice_in_dim(terms, (level ^ k) * quarter, quarter, 1)


ring = (0, 2, 4, 6, 7, 5, 3, 1)


def turn_ring(array, step):
    count = len(ring)
    return lax.ppermute(
        array, "ctx", [(ring[i], ring[(i + step) % count]) for i in range(count)]
    )


def gather_plain(units, sums):
    size, part = lax.axis_size("ctx"), lax.axis_index("fsdp")
    _, height, span = units.shape
    units = lax.all_gather(units, "ctx", axis=0)
    units = jnp.stack(
        [lax.dynamic_index_in_dim(units, part ^ k, 1, keepdims=False) for k in range(4)]
    ).reshape(4, size, height, 3, span // 3)
    units = units.transpose(3, 2, 0, 1, 4).reshape(3, height, -1).astype(wide)
    sums = lax.all_gather(sums, "ctx", axis=1, tiled=True)
    sums = [lax.dynamic_index_in_dim(sums, part ^ k, 0, keepdims=False) for k in range(4)]
    sums = jnp.stack(sums, axis=1).astype(wide)
    sums = sums.reshape(height, 4, 3, -1).transpose(2, 0, 1, 3).reshape(3, height, -1)
    half = sums.shape[2] // 2
    return (*units, sums[0], sums[1], sums[2, :, :half], sums[2, :, half:])


UPPER = 176


def deal_kernel(code_ref, *refs):
    count = len(ring)
    outs = refs[2 * count :]
    units, (out_ref, query_ref, key_ref, value_ref) = outs[:3], outs[3:]
    quarter = pl.program_id(0)
    for lower in range(2):
        for step in range(count):
            part = refs[lower * count + step]
            place = code_ref[1 + lower * count + step]
            piece = part.shape[2] // 3
            height = out_ref.shape[0] // count
            first = (2 - lower) * height
            here = slice(UPPER, None) if lower else slice(0, UPPER)
            across = pl.ds(pl.multiple_of(place * piece, piece), piece)
            for i, unit_ref in enumerate(units):
                unit_ref[here, across] = part[0, first:, i * piece : (i + 1) * piece].astype(wide)
            rows_at = pl.multiple_of(((place % 2) * 4 + place // 2) * height, height)
            down = pl.ds(rows_at, height)
            if not lower:
                out_ref[down, :] = part[0, :height].astype(wide)
                query_ref[down, :] = part[0, height:first].astype(wide)
                continue

            @pl.when(quarter < 2)
            def _(part=part, down=down):
                key_ref[down, :] = part[0, :height].astype(wide)

            @pl.when(quarter >= 2)
            def _(part=part, down=down):
                value_ref[down, :] = part[0, :height].astype(wide)


def gather_all(units, sums):
    here, size, part = lax.axis_index("ctx"), lax.axis_size("ctx"), lax.axis_index("fsdp")
    if size != 8:
        return gather_plain(units, sums)
    width = sums.shape[2] // 3
    thirds = [sums[:, :, i * width : (i + 1) * width] for i in range(3)]
    upper = [jnp.concatenate([thirds[0], thirds[1], units[:, :UPPER]], axis=1)]
    lower = [jnp.concatenate([thirds[2], units[:, UPPER:]], axis=1)]
    for _ in range(size - 1):
        upper.append(turn_ring(upper[-1], 1))
        lower.append(turn_ring(lower[-1], -1))
    order = jnp.asarray(ring, jnp.int32)
    turn = jnp.argmax(order == here).astype(jnp.int32)
    steps = jnp.arange(size, dtype=jnp.int32)
    code = jnp.concatenate(
        [part.reshape(1), order[(turn - steps) % size], order[(turn + steps) % size]]
    ).astype(jnp.int32)
    height, across = units.shape[1], units.shape[2] // 3 * size

    def incoming(array):
        return pl.BlockSpec((1,) + array.shape[1:], lambda i, code: (code[0] ^ i, 0, 0))

    def outgoing(count, index):
        return pl.BlockSpec((height, count), lambda i, code: (0, index(i)))

    return pl.pallas_call(
        deal_kernel,
        grid_spec=pltpu.PrefetchScalarGridSpec(
            num_scalar_prefetch=1,
            grid=(4,),
            in_specs=[incoming(array) for array in (*upper, *lower)],
            out_specs=[outgoing(across, lambda i: i)] * 3
            + [outgoing(width, lambda i: i)] * 2
            + [
                outgoing(width, lambda i: jnp.minimum(i, 1)),
                outgoing(width, lambda i: jnp.maximum(i - 2, 0)),
            ],
        ),
        out_shape=[jax.ShapeDtypeStruct((height, 4 * across), wide)] * 3
        + [jax.ShapeDtypeStruct((height, 4 * width), wide)] * 2
        + [jax.ShapeDtypeStruct((height, 2 * width), wide)] * 2,
        compiler_params=pltpu.CompilerParams(vmem_limit_bytes=56 << 20),
        cost_estimate=brief,
        name="deal_gradients",
    )(code, *upper, *lower)


def deal_rows(piece, *others):
    part = lax.axis_index("fsdp")
    return deal_fsdp(lambda k: rows(piece, part ^ k, piece.shape[0] // 4), *others)


def unit_grads_kernel(normed_ref, grad_ref, gate_ref, up_ref, hidden_ref, out_ref, flipped):
    @pl.when(pl.program_id(0) == 0)
    def _():
        flipped[0] = normed_ref[...].T
        flipped[1] = grad_ref[...].T

    piece = hidden_ref.shape[1]
    right = jnp.concatenate([gate_ref[...], up_ref[...]], axis=1)
    out_ref[:, : 2 * piece] = product(flipped[0], right).astype(low)
    out_ref[:, 2 * piece :] = product(flipped[1], hidden_ref[...]).astype(low)


def unit_grads(normed, grad, grad_gate, grad_up, hidden):
    size = lax.axis_size("ctx")
    count, depth = normed.shape
    piece = hidden.shape[1] // size
    rights = (grad_gate, grad_up, hidden)
    if piece % 128:
        cut = [
            contract_first(left, right).astype(low).reshape(depth, size, piece)
            for left, right in zip((normed, normed, grad), rights)
        ]
        return jnp.concatenate(cut, axis=2).transpose(1, 0, 2).reshape(size * depth, 3 * piece)
    whole = pl.BlockSpec(memory_space=pltpu.VMEM)
    return pl.pallas_call(
        unit_grads_kernel,
        grid=(size,),
        in_specs=[whole, whole] + [pl.BlockSpec((count, piece), lambda i: (0, i))] * 3,
        out_specs=pl.BlockSpec((depth, 3 * piece), lambda i: (i, 0)),
        scratch_shapes=[pltpu.VMEM((2, depth, count), low)],
        out_shape=jax.ShapeDtypeStruct((size * depth, 3 * piece), low),
        compiler_params=pltpu.CompilerParams(vmem_limit_bytes=40 << 20),
        cost_estimate=lasting,
        name="unit_grads",
    )(normed, grad, *rights)


def sum_gains(array, *others):
    part, size = lax.axis_index("fsdp"), lax.axis_size("ctx")
    width = array.shape[1] // 4
    array = jnp.sum(deal_fsdp(lambda k: columns(array, part ^ k, width)), axis=0)
    array = array + after(over_ctx(array, 1), *others[0])
    if size == 8:
        return array + sum(after(got, *others[1]) for got in exchange_levels(lambda k: array))
    bits = 2
    while bits < size:
        array = array + over_ctx(array, bits)
        bits *= 2
    return array


def body(
    hidden_in,
    out_grad,
    positions,
    attn_gain,
    w_query,
    w_key,
    w_value,
    w_out,
    ffn_gain,
    w_gate,
    w_up,
    w_down,
):
    part, here, size = lax.axis_index("fsdp"), lax.axis_index("ctx"), lax.axis_size("ctx")
    code = jnp.stack([part, here % 2, here // 2 % 2]).astype(jnp.int32)
    own_gains = jnp.stack([attn_gain, ffn_gain])
    gains = [own_gains] + [over_fsdp(own_gains, k) for k in (1, 2, 3)]
    rows_in, grad_down = hidden_in[0], out_grad[0]
    row_count = rows_in.shape[0]
    all_places = positions[0]
    own_places = lax.dynamic_slice_in_dim(all_places, here * row_count, row_count, 0)
    cosine, sine = angles_of(own_places)
    cosine = jnp.concatenate([cosine[:, 0], cosine[:, 0]], axis=1)
    sine = jnp.concatenate([-sine[:, 0], sine[:, 0]], axis=1)

    own, near, far, both = deal_weights((w_gate, w_up, w_down))
    heads = gather_thirds(jnp.concatenate([w_query, w_key, w_value], axis=1), near, far, both)
    normed_one, load = heads_call(code, rows_in, cosine, sine, gains, heads)
    outward = gather_halves(w_out)
    load, near, far, both, _ = lax.optimization_barrier((load, near, far, both, outward[2]))
    far, both = over_fsdp(far, 2), over_fsdp(both, 3)
    near = over_fsdp(near, 1)
    far_other, both_other = over_ctx(far, 1), over_ctx(both, 2)

    if size == HK:
        load = lax.all_to_all(load, "ctx", 0, 0, tiled=True)
        order = all_places[::BLK] // BLK
        mixed = attention_forward(order, after(load, far))
        grad_all = gather_fsdp(grad_down, mixed)
        mixed = lax.all_to_all(after(mixed, far_other, outward[3]), "ctx", 0, 0, tiled=True)
    else:
        query_rot = load[:, :, : GROUP * HD].transpose(1, 0, 2)
        query_rot = query_rot.reshape(row_count, HK, GROUP, HD)
        keys_values = load[:, :, GROUP * HD :].transpose(1, 0, 2)
        keys_values = lax.all_gather(keys_values, "ctx", axis=0, tiled=True)
        keys_all, values_all = keys_values[:, :, :HD], keys_values[:, :, HD:]
        mixed_exact, log_total = rows_forward(
            query_rot, keys_all, values_all, own_places, all_places
        )
        mixed = mixed_exact.reshape(row_count, HK, GROUP * HD).transpose(1, 0, 2).astype(low)
        grad_all = gather_fsdp(grad_down)

    dealt = (own, near, far, far_other, both, both_other)
    mixed_low, middle, normed_two = middle_call(
        code, rows_in, after(mixed, both, grad_all), gains, outward
    )
    normed_all = gather_fsdp(normed_two, both_other)
    out_terms, back_terms, hidden, grad_gate, grad_up = units_call(
        code, normed_all, grad_all, dealt
    )
    grad_normed_two, passed = scatter_fsdp(back_terms)
    unit_terms = unit_grads(normed_all, grad_all, after(grad_gate, passed), grad_up, hidden)
    grad_normed_two, unit_terms = lax.optimization_barrier((grad_normed_two, unit_terms))
    grad_middle, grad_branch, grad_mixed, grad_gain_two = middle_back_call(
        code, middle, grad_normed_two, grad_down, gains, outward
    )
    unit_sums = lax.psum_scatter(unit_terms, "ctx", scatter_dimension=0, tiled=True)

    if size == HK:
        grad_mixed = lax.all_to_all(grad_mixed, "ctx", 0, 0, tiled=True)
        grad_load = attention_backward(order, load, grad_mixed)
        mid = grad_load
        grad_load = lax.all_to_all(grad_load, "ctx", 0, 0, tiled=True)
    else:
        grad_mixed = grad_mixed.transpose(1, 0, 2).reshape(row_count, HK, GROUP, HD)
        delta = jnp.sum(grad_mixed.astype(wide) * mixed_exact, axis=-1)
        grad_query, grad_keys, grad_values = rows_backward(
            query_rot, keys_all, values_all, own_places, all_places, log_total, delta, grad_mixed
        )
        grad_keys, grad_values = (
            lax.psum_scatter(whole.astype(low), "ctx", scatter_dimension=0, tiled=True)
            for whole in (grad_keys, grad_values)
        )
        grad_load = jnp.concatenate(
            [
                grad_query.reshape(row_count, HK, GROUP * HD).astype(low),
                grad_keys.reshape(row_count, HK, HD),
                grad_values.reshape(row_count, HK, HD),
            ],
            axis=2,
        ).transpose(1, 0, 2)
        mid = grad_load

    quarter = HQ * HD // 4
    turn = (0, 2, 1, 3)

    def own_columns(cut, *others):
        dealt = deal_fsdp(cut, *others)
        return jnp.concatenate([dealt[k] for k in turn], axis=0)

    branch_all = gather_fsdp(grad_branch, mid)
    mixed_part = own_columns(lambda k: columns(mixed_low, part ^ k, quarter), mid)
    normed_one_all = gather_fsdp(after(normed_one, grad_branch), mid)
    branch_terms = terms_of(branch_all, mixed_part)
    if size == HK:
        out_got = over_ctx(side_of(branch_terms, 1), 1)
    grad_raw, input_grad, grad_gain_one = heads_back_call(
        code, grad_load, rows_in, grad_middle, cosine, sine, gains, heads
    )
    result, _ = scatter_fsdp(after(out_terms, grad_normed_two), mid)
    result = (middle + result).astype(low)
    raw_part = own_columns(
        lambda k: lax.dynamic_index_in_dim(grad_raw, part ^ k, 0, keepdims=False)
    )
    gain_terms = jnp.concatenate([grad_gain_one, grad_gain_two], axis=0)
    if size == HK:
        raw_part, out_got = together(raw_part, out_got)
        out_kept = add_low(side_of(branch_terms, 0), out_got)
        raw_terms = terms_of(normed_one_all, raw_part)
        raw_got = over_ctx(side_of(raw_terms, 1), 1)
        out_got = exchange_levels(lambda k: level_of(out_kept, k))
        raw_got, out_got = together(raw_got, out_got)
        raw_kept = add_low(side_of(raw_terms, 0), raw_got)
        out_sums = add_low(level_of(out_kept, 0), *out_got)
        raw_kept, unit_sums = together(raw_kept, unit_sums)
        raw_got = exchange_levels(lambda k: level_of(raw_kept, k))
        unit_mine = deal_rows(unit_sums)
        raw_got, unit_mine = together(raw_got, unit_mine)
        raw_sums = add_low(level_of(raw_kept, 0), *raw_got)
    else:
        raw_terms = terms_of(normed_one_all, raw_part)
        out_sums, raw_sums = (
            lax.psum_scatter(terms, "ctx", scatter_dimension=1, tiled=True)
            for terms in (branch_terms, raw_terms)
        )
        raw_kept = raw_terms
        unit_mine = deal_rows(unit_sums)
    sums = jnp.concatenate([out_sums, raw_sums], axis=2)
    sums = deal_fsdp(lambda k: lax.dynamic_index_in_dim(sums, part ^ k, 0, keepdims=False))
    gain_grads = sum_gains(
        gain_terms, (raw_kept,), (sums,)
    )
    gate_grad, up_grad, down_grad, out_weight_grad, query_grad, key_grad, value_grad = gather_all(
        unit_mine, sums
    )
    return (
        result[None],
        input_grad[None],
        gain_grads[0],
        query_grad,
        key_grad,
        value_grad,
        out_weight_grad,
        gain_grads[1],
        gate_grad,
        up_grad,
        down_grad,
    )


def solution(mesh):
    matrix = P("fsdp", None)
    stream = P("fsdp", "ctx", None)
    return jax.shard_map(
        body,
        mesh=mesh,
        in_specs=(stream, stream, matrix, P("fsdp"))
        + (matrix,) * 4
        + (P("fsdp"),)
        + (matrix,) * 3,
        out_specs=(stream, stream, P("fsdp")) + (matrix,) * 4 + (P("fsdp"),) + (matrix,) * 3,
        check_vma=False,
    )
```

```python
import math

import jax
import jax.numpy as jnp
from jax import lax
from jax.experimental import pallas as pl
from jax.experimental.pallas import tpu as pltpu
from jax.sharding import PartitionSpec as P

HQ = 16
HK = 8
HD = 96
GROUP = HQ // HK
BLK = 128

epsilon = 1e-05
rope_base = 100000.0
masked_score = -1e30
scale = 1.0 / math.sqrt(HD)
low = jnp.bfloat16
wide = jnp.float32
brief = pl.CostEstimate(flops=0, bytes_accessed=0, transcendentals=0)
lasting = pl.CostEstimate(flops=10**11, bytes_accessed=0, transcendentals=0)


def angles_of(places):
    frequency = jnp.exp(jnp.arange(HD // 2, dtype=wide) * (-2.0 * math.log(rope_base) / HD))
    turned = places.astype(wide)[:, None] * frequency[None, :]
    return (jnp.cos(turned)[:, None, :], jnp.sin(turned)[:, None, :])


def product(left, right):
    return jnp.dot(left, right, preferred_element_type=wide)


def contract_last(left, right):
    return lax.dot_general(left, right, (((1,), (1,)), ((), ())), preferred_element_type=wide)


def contract_first(left, right):
    return lax.dot_general(left, right, (((0,), (0,)), ((), ())), preferred_element_type=wide)


def swap(array, axis, bits, size):
    return lax.ppermute(array, axis, [(i, i ^ bits) for i in range(size)])


def over_fsdp(array, bits):
    return swap(array, "fsdp", bits, 4)


def over_ctx(array, bits):
    return swap(array, "ctx", bits, lax.axis_size("ctx"))


def columns(array, index, width):
    return lax.dynamic_slice_in_dim(array, index * width, width, array.ndim - 1)


def rows(array, index, height):
    return lax.dynamic_slice_in_dim(array, index * height, height, 0)


def together(*arrays):
    return lax.optimization_barrier(arrays)


def after(array, *others):
    return lax.optimization_barrier((array, *others))[0]


def add_low(first, *others):
    total = first.astype(wide)
    for other in others:
        total = total + other.astype(wide)
    return total.astype(low)


def gather_fsdp(array, *others):
    far = after(over_fsdp(array, 2), *others)
    pair = over_fsdp(jnp.concatenate([array, far], axis=0), 1)
    return jnp.concatenate([array, far, pair], axis=0)


def scatter_fsdp(terms, *others):
    half, height = terms.shape[0] // 2, terms.shape[0] // 4
    kept, got = terms[:half], over_fsdp(terms[half:], 1)
    passed = add_low(kept[height:], got[height:])
    away = after(over_fsdp(passed, 2), *others)
    total = kept[:height].astype(wide) + got[:height].astype(wide) + away.astype(wide)
    return total, passed


ALL, REST, MINE, OTHER = 0, 3, 4, 8
heads_plan = (
    (0, ALL),
    (1, ALL),
    (2, MINE + 1),
    (2, OTHER + 1),
    (2, REST),
    (3, MINE + 1),
    (3, OTHER + 1),
    (3, REST),
)
outward_plan = ((0, ALL), (1, ALL), (2, MINE + 2), (2, OTHER + 2), (3, MINE + 2), (3, OTHER + 2))
units_plan = ((0, ALL), (1, ALL), (2, MINE + 1), (2, OTHER + 1), (3, MINE + 2), (3, OTHER + 2))


def gather_thirds(own, *others):
    side = lax.axis_index("ctx") % 2
    third = own.shape[1] // 3
    far = after(over_fsdp(columns(own, side, third), 2), *others)
    rest = over_fsdp(after(own[:, 2 * third :], far), 2)
    near = over_fsdp(own, 1)
    other = over_ctx(far, 1)
    return (
        own,
        near,
        far,
        other,
        rest,
        over_fsdp(far, 1),
        over_fsdp(other, 1),
        over_fsdp(rest, 1),
    )


def gather_halves(own):
    far = over_fsdp(columns(own, lax.axis_index("ctx") // 2 % 2, own.shape[1] // 2), 2)
    near = over_fsdp(own, 1)
    other = over_ctx(far, 2)
    return (own, near, far, other, over_fsdp(far, 1), over_fsdp(other, 1))


def fill_weight(code_ref, plan, pieces, out):
    part = code_ref[0]
    for (k, which), piece in zip(plan, pieces):
        height, width = piece.shape
        across = pl.ds(pl.multiple_of((part ^ k) * height, height), height)
        if which == ALL:
            out[across, :] = piece[...]
        elif which == REST:
            out[across, 2 * width :] = piece[...]
        else:
            side = code_ref[which % MINE]
            place = 1 - side if which >= OTHER else side
            out[across, lanes(place, width)] = piece[...]


def whole_call(kernel, code, arrays, outs, scratch, flops, name):
    spec = pl.BlockSpec(memory_space=pltpu.VMEM)
    moved = sum(math.prod(a.shape) * a.dtype.itemsize for a in (*arrays, *outs))
    return pl.pallas_call(
        kernel,
        grid_spec=pltpu.PrefetchScalarGridSpec(
            num_scalar_prefetch=1,
            grid=(),
            in_specs=[spec] * len(arrays),
            out_specs=[spec] * len(outs),
            scratch_shapes=scratch,
        ),
        out_shape=outs,
        compiler_params=pltpu.CompilerParams(vmem_limit_bytes=56 << 20),
        cost_estimate=pl.CostEstimate(flops=flops, bytes_accessed=moved, transcendentals=0),
        name=name,
    )(code, *arrays)


def lanes(index, width):
    return pl.ds(pl.multiple_of(index * width, 128), width)


def gained(code_ref, gains, row, out):
    for k in range(4):
        out[:, lanes(code_ref[0] ^ k, gains[k].shape[1])] = gains[k][row : row + 1, :].astype(wide)


def turned(values, cosine, sine):
    half = values.shape[1] // 2
    return values * cosine + jnp.concatenate([values[:, half:], values[:, :half]], axis=1) * sine


def inverse_rms(values):
    return lax.rsqrt(jnp.mean(values * values, axis=1, keepdims=True) + epsilon)


def slot_of_head(head):
    if head < HQ:
        return head // GROUP, head % GROUP
    return (head - HQ) % HK, GROUP + (head - HQ) // HK


def heads_kernel(code_ref, rows_ref, cosine_ref, sine_ref, *refs):
    gains, pieces = refs[:4], refs[4:12]
    normed_ref, load_ref, gain, weight, total = refs[12:]
    gained(code_ref, gains, 0, gain)
    fill_weight(code_ref, heads_plan, pieces, weight)
    values = rows_ref[...].astype(wide)
    normed_ref[...] = (values * inverse_rms(values) * gain[...]).astype(low)
    total[...] = product(normed_ref[...], weight[...])
    cosine, sine = cosine_ref[...], sine_ref[...]
    for head in range(HQ + 2 * HK):
        part = total[:, head * HD : (head + 1) * HD]
        if head < HQ + HK:
            part = turned(part, cosine, sine)
        group, place = slot_of_head(head)
        load_ref[group, :, place * HD : (place + 1) * HD] = part.astype(low)


def heads_call(code, rows_in, cosine, sine, gains, pieces):
    count, width = rows_in.shape
    total = pieces[0].shape[1]
    outs = [
        jax.ShapeDtypeStruct((count, width), low),
        jax.ShapeDtypeStruct((HK, count, (GROUP + 2) * HD), low),
    ]
    scratch = [
        pltpu.VMEM((1, width), wide),
        pltpu.VMEM((width, total), low),
        pltpu.VMEM((count, total), wide),
    ]
    return whole_call(
        heads_kernel,
        code,
        (rows_in, cosine, sine, *gains, *pieces),
        outs,
        scratch,
        2 * count * width * total,
        "query_key_value",
    )


def middle_kernel(code_ref, rows_ref, mixed_ref, *refs):
    gains, pieces = refs[:4], refs[4:10]
    flat_ref, middle_ref, normed_ref, gain, weight = refs[10:]
    gained(code_ref, gains, 1, gain)
    fill_weight(code_ref, outward_plan, pieces, weight)
    span = mixed_ref.shape[2]
    for group in range(mixed_ref.shape[0]):
        flat_ref[:, group * span : (group + 1) * span] = mixed_ref[group]
    middle = contract_last(flat_ref[...], weight[...]) + rows_ref[...].astype(wide)
    middle_ref[...] = middle
    normed_ref[...] = (middle * inverse_rms(middle) * gain[...]).astype(low)


def middle_call(code, rows_in, mixed, gains, pieces):
    count, width = rows_in.shape
    outs = [
        jax.ShapeDtypeStruct((count, HQ * HD), low),
        jax.ShapeDtypeStruct((count, width), wide),
        jax.ShapeDtypeStruct((count, width), low),
    ]
    return whole_call(
        middle_kernel,
        code,
        (rows_in, mixed, *gains, *pieces),
        outs,
        [pltpu.VMEM((1, width), wide), pltpu.VMEM((width, HQ * HD), low)],
        2 * count * width * HQ * HD,
        "attention_output",
    )


def norm_back(values, gain, grad):
    inverse = inverse_rms(values)
    weighted = gain * grad
    inner = jnp.mean(values * weighted, axis=1, keepdims=True)
    back = inverse * weighted - values * inverse * inverse * inverse * inner
    return back, jnp.sum(grad * values * inverse, axis=0, keepdims=True)


def middle_back_kernel(code_ref, middle_ref, grad_ref, out_grad_ref, *refs):
    gains, pieces = refs[:4], refs[4:10]
    grad_middle_ref, branch_ref, sent_ref, gain_grad_ref, gain, weight = refs[10:]
    gained(code_ref, gains, 1, gain)
    fill_weight(code_ref, outward_plan, pieces, weight)
    back, gain_grad_ref[...] = norm_back(middle_ref[...], gain[...], grad_ref[...])
    grad_middle = out_grad_ref[...].astype(wide) + back
    grad_middle_ref[...] = grad_middle
    branch_ref[...] = grad_middle.astype(low)
    total = product(branch_ref[...], weight[...]).astype(low)
    span = sent_ref.shape[2]
    for group in range(sent_ref.shape[0]):
        sent_ref[group] = total[:, group * span : (group + 1) * span]


def middle_back_call(code, middle, grad, out_grad, gains, pieces):
    count, width = middle.shape
    outs = [
        jax.ShapeDtypeStruct((count, width), wide),
        jax.ShapeDtypeStruct((count, width), low),
        jax.ShapeDtypeStruct((HK, count, GROUP * HD), low),
        jax.ShapeDtypeStruct((1, width), wide),
    ]
    return whole_call(
        middle_back_kernel,
        code,
        (middle, grad, out_grad, *gains, *pieces),
        outs,
        [pltpu.VMEM((1, width), wide), pltpu.VMEM((width, HQ * HD), low)],
        2 * count * width * HQ * HD,
        "attention_output_back",
    )


def turn_back_kernel(code_ref, load_ref, cosine_ref, sine_ref, raw_ref, parts_ref):
    cosine, sine = cosine_ref[...], sine_ref[...]
    for head in range(HQ + 2 * HK):
        group, place = slot_of_head(head)
        part = load_ref[group, :, place * HD : (place + 1) * HD]
        if head < HQ + HK:
            part = turned(part.astype(wide), cosine, -sine).astype(low)
        raw_ref[:, head * HD : (head + 1) * HD] = part
    quarter = parts_ref.shape[2] // 2
    for k in range(4):
        for i in range(2):
            first = (4 * i + k) * quarter
            parts_ref[k, :, i * quarter : (i + 1) * quarter] = raw_ref[:, first : first + quarter]


def turn_back_call(code, load, cosine, sine):
    count, total = load.shape[1], load.shape[0] * load.shape[2]
    outs = [
        jax.ShapeDtypeStruct((count, total), low),
        jax.ShapeDtypeStruct((4, count, total // 4), low),
    ]
    return whole_call(turn_back_kernel, code, (load, cosine, sine), outs, [], 0, "turn_back")


def heads_back_kernel(code_ref, raw_ref, rows_ref, grad_middle_ref, *refs):
    gains, pieces = refs[:4], refs[4:12]
    input_grad_ref, gain_grad_ref, gain, weight = refs[12:]
    gained(code_ref, gains, 0, gain)
    fill_weight(code_ref, heads_plan, pieces, weight)
    grad = contract_last(raw_ref[...], weight[...])
    back, gain_grad_ref[...] = norm_back(rows_ref[...].astype(wide), gain[...], grad)
    input_grad_ref[...] = grad_middle_ref[...] + back


def heads_back_call(code, raw, rows_in, grad_middle, gains, pieces):
    count, width = rows_in.shape
    total = pieces[0].shape[1]
    outs = [
        jax.ShapeDtypeStruct((count, width), wide),
        jax.ShapeDtypeStruct((1, width), wide),
    ]
    return whole_call(
        heads_back_kernel,
        code,
        (raw, rows_in, grad_middle, *gains, *pieces),
        outs,
        [pltpu.VMEM((1, width), wide), pltpu.VMEM((width, total), low)],
        2 * count * width * total,
        "query_key_value_back",
    )


def units_kernel(code_ref, normed_ref, grad_ref, *refs):
    pieces = refs[:6]
    out_ref, back_ref, hidden_ref, grad_gate_ref, grad_up_ref, weights = refs[6:]

    @pl.when(pl.program_id(0) == 0)
    def _():
        for i in range(3):
            fill_weight(code_ref, units_plan, [piece.at[i] for piece in pieces], weights.at[i])

    gate = product(normed_ref[...], weights[0])
    upward = product(normed_ref[...], weights[1])
    sigmoid_gate = jax.nn.sigmoid(gate)
    swish = gate * sigmoid_gate
    hidden = (swish * upward).astype(low)
    hidden_ref[...] = hidden
    grad_hidden = product(grad_ref[...], weights[2])
    grad_gate = (
        grad_hidden * upward * sigmoid_gate * (1.0 + gate * (1.0 - sigmoid_gate))
    ).astype(low)
    grad_up = (grad_hidden * swish).astype(low)
    grad_gate_ref[...] = grad_gate
    grad_up_ref[...] = grad_up
    back_ref[...] = (
        contract_last(grad_gate, weights[0]) + contract_last(grad_up, weights[1])
    ).astype(low)
    out_ref[...] = contract_last(hidden, weights[2]).astype(low)


def units_call(code, normed, grad, pieces):
    count, width = normed.shape
    units = pieces[0].shape[2]
    tile = 512
    wide_block = pl.BlockSpec((tile, width), lambda i, code: (i, 0))
    unit_block = pl.BlockSpec((tile, units), lambda i, code: (i, 0))
    return pl.pallas_call(
        units_kernel,
        grid_spec=pltpu.PrefetchScalarGridSpec(
            num_scalar_prefetch=1,
            grid=(count // tile,),
            in_specs=[wide_block, wide_block]
            + [pl.BlockSpec(memory_space=pltpu.VMEM)] * len(pieces),
            out_specs=[wide_block, wide_block, unit_block, unit_block, unit_block],
            scratch_shapes=[pltpu.VMEM((3, width, units), low)],
        ),
        out_shape=[jax.ShapeDtypeStruct((count, width), low)] * 2
        + [jax.ShapeDtypeStruct((count, units), low)] * 3,
        compiler_params=pltpu.CompilerParams(vmem_limit_bytes=60 << 20),
        cost_estimate=pl.CostEstimate(
            flops=12 * count * width * units,
            bytes_accessed=8 * count * width + 6 * width * units,
            transcendentals=count * units,
        ),
        name="feed_forward",
    )(code, normed, grad, *pieces)


def deal_weights(weights):
    part, here = lax.axis_index("fsdp"), lax.axis_index("ctx")
    width = weights[0].shape[1] // 4

    def taken(k):
        return jnp.stack([columns(weight, part ^ k, width) for weight in weights])

    def half(k, side):
        return jnp.stack(
            [columns(weight, (part ^ k) * 2 + side, width // 2) for weight in weights]
        )

    return taken(0), taken(1), half(2, here % 2), half(3, here // 2 % 2)


def slot_of(ref, slot):
    return ref.at[slot // 2, (slot % 2) * BLK : (slot % 2 + 1) * BLK, :]


def sort_rows(order_ref, load_ref, queries, keys, values):
    for slot in range(2 * load_ref.shape[0]):
        block = order_ref[slot]
        piece = slot_of(load_ref, slot)[...]
        place = pl.ds(pl.multiple_of(block * BLK, BLK), BLK)
        half = pl.ds(pl.multiple_of((block % 2) * BLK, BLK), BLK)
        other = pl.ds(pl.multiple_of((block % 2) * BLK + 2 * BLK, BLK), BLK)
        queries[block // 2, half, :] = piece[:, :HD]
        queries[block // 2, other, :] = piece[:, HD : 2 * HD]
        keys[place, :] = piece[:, 2 * HD : 3 * HD]
        values[place, :] = piece[:, 3 * HD :]


def forward_kernel(order_ref, load_ref, out_ref, queries, keys, values, mixed):
    sort_rows(order_ref, load_ref, queries, keys, values)
    step = 2 * BLK
    query_at = lax.broadcasted_iota(jnp.int32, (2 * step, step), 0) % step
    key_at = lax.broadcasted_iota(jnp.int32, (2 * step, step), 1)
    allowed = key_at <= query_at
    for i in range(keys.shape[0] // step):
        reach = (i + 1) * step
        query = queries[i]
        ahead = contract_last(query, keys[i * step : reach, :]) * scale
        ahead = jnp.where(allowed, ahead, masked_score)
        top = jnp.max(ahead, axis=1, keepdims=True)
        if i:
            before = contract_last(query, keys[: i * step, :]) * scale
            top = jnp.maximum(top, jnp.max(before, axis=1, keepdims=True))
        soft = jnp.exp(ahead - top)
        total = jnp.sum(soft, axis=1, keepdims=True)
        result = product(soft.astype(low), values[i * step : reach, :])
        if i:
            soft = jnp.exp(before - top)
            total = total + jnp.sum(soft, axis=1, keepdims=True)
            result = result + product(soft.astype(low), values[: i * step, :])
        result = (result / total).astype(low)
        mixed[i * step : reach, :HD] = result[:step]
        mixed[i * step : reach, HD:] = result[step:]
    for slot in range(2 * load_ref.shape[0]):
        place = pl.ds(pl.multiple_of(order_ref[slot] * BLK, BLK), BLK)
        slot_of(out_ref, slot)[...] = mixed[place, :]


def backward_kernel(
    order_ref, load_ref, grad_ref, out_ref, queries, keys, values, grads, key_sum, value_sum, sent
):
    sort_rows(order_ref, load_ref, queries, keys, values)
    step = 2 * BLK
    length = keys.shape[0]
    for slot in range(length // BLK):
        block = order_ref[slot]
        piece = slot_of(grad_ref, slot)[...]
        half = pl.ds(pl.multiple_of((block % 2) * BLK, BLK), BLK)
        other = pl.ds(pl.multiple_of((block % 2) * BLK + 2 * BLK, BLK), BLK)
        grads[block // 2, half, :] = piece[:, :HD]
        grads[block // 2, other, :] = piece[:, HD:]
    key_at = lax.broadcasted_iota(jnp.int32, (step, 2 * step), 0)
    query_at = lax.broadcasted_iota(jnp.int32, (step, 2 * step), 1) % step
    allowed = key_at <= query_at
    for i in range(length // step):
        query = queries[i]
        grad = grads[i]
        scores = []
        top = None
        for j in range(i + 1):
            score = contract_last(keys[j * step : (j + 1) * step, :], query) * scale
            if j == i:
                score = jnp.where(allowed, score, masked_score)
            high = jnp.max(score, axis=0, keepdims=True)
            top = high if top is None else jnp.maximum(top, high)
            scores.append(score)
        total = jnp.zeros_like(top)
        delta = jnp.zeros_like(top)
        softs = []
        slopes = []
        for j in range(i + 1):
            soft = jnp.exp(scores[j] - top)
            slope = contract_last(values[j * step : (j + 1) * step, :], grad)
            total = total + jnp.sum(soft, axis=0, keepdims=True)
            delta = delta + jnp.sum(soft * slope, axis=0, keepdims=True)
            softs.append(soft)
            slopes.append(slope)
        share = 1.0 / total
        delta = delta * share
        query_sum = jnp.zeros((2 * step, HD), wide)
        for j in range(i + 1):
            place = slice(j * step, (j + 1) * step)
            soft = softs[j] * share
            steep = (soft * (slopes[j] - delta)).astype(low)
            key_part = product(steep, query)
            value_part = product(soft.astype(low), grad)
            if j == i:
                key_sum[place, :] = key_part
                value_sum[place, :] = value_part
            else:
                key_sum[place, :] += key_part
                value_sum[place, :] += value_part
            query_sum = query_sum + contract_first(steep, keys[place, :])
        query_sum = (query_sum * scale).astype(low)
        sent[i * step : (i + 1) * step, :HD] = query_sum[:step]
        sent[i * step : (i + 1) * step, HD : 2 * HD] = query_sum[step:]
    sent[:, 2 * HD : 3 * HD] = (key_sum[...] * scale).astype(low)
    sent[:, 3 * HD :] = value_sum[...].astype(low)
    for slot in range(length // BLK):
        place = pl.ds(pl.multiple_of(order_ref[slot] * BLK, BLK), BLK)
        slot_of(out_ref, slot)[...] = sent[place, :]


def attention_call(kernel, order, arrays, width, scratch, products, name):
    devices, height = arrays[0].shape[:2]
    length = devices * height
    half = (length * length) // 2 * GROUP
    whole = pl.BlockSpec(memory_space=pltpu.VMEM)
    return pl.pallas_call(
        kernel,
        grid_spec=pltpu.PrefetchScalarGridSpec(
            num_scalar_prefetch=1,
            grid=(),
            in_specs=[whole] * len(arrays),
            out_specs=whole,
            scratch_shapes=scratch,
        ),
        out_shape=jax.ShapeDtypeStruct((devices, height, width), low),
        compiler_params=pltpu.CompilerParams(vmem_limit_bytes=56 << 20),
        cost_estimate=pl.CostEstimate(
            flops=2 * products * half * 256, bytes_accessed=8 * length * width, transcendentals=half
        ),
        name=name,
    )(order, *arrays)


def attention_forward(order, load):
    length = load.shape[0] * load.shape[1]
    scratch = [
        pltpu.VMEM((length // (2 * BLK), 4 * BLK, HD), low),
        pltpu.VMEM((length, HD), low),
        pltpu.VMEM((length, HD), low),
        pltpu.VMEM((length, 2 * HD), low),
    ]
    return attention_call(forward_kernel, order, (load,), 2 * HD, scratch, 2, "attention_forward")


def attention_backward(order, load, grad):
    length = load.shape[0] * load.shape[1]
    scratch = [
        pltpu.VMEM((length // (2 * BLK), 4 * BLK, HD), low),
        pltpu.VMEM((length, HD), low),
        pltpu.VMEM((length, HD), low),
        pltpu.VMEM((length // (2 * BLK), 4 * BLK, HD), low),
        pltpu.VMEM((length, HD), wide),
        pltpu.VMEM((length, HD), wide),
        pltpu.VMEM((length, 4 * HD), low),
    ]
    return attention_call(
        backward_kernel, order, (load, grad), 4 * HD, scratch, 5, "attention_backward"
    )


def scores_of(query_rot, keys_all, own_places, all_places, start, block_size):
    key_block = lax.dynamic_slice_in_dim(keys_all, start, block_size, 0)
    key_places = lax.dynamic_slice_in_dim(all_places, start, block_size, 0)
    raw = (
        jnp.einsum("rkgd,skd->rkgs", query_rot, key_block, preferred_element_type=wide) * scale
    )
    allowed = key_places[None, None, None, :] <= own_places[:, None, None, None]
    return (jnp.where(allowed, raw, masked_score), key_block)


def rows_forward(query_rot, keys_all, values_all, own_places, all_places):
    row_count = query_rot.shape[0]
    key_total = keys_all.shape[0]
    block_size = math.gcd(key_total, 512)

    def step(block_index, carry):
        top_score, total, mixed = carry
        start = block_index * block_size
        scores, _ = scores_of(query_rot, keys_all, own_places, all_places, start, block_size)
        value_block = lax.dynamic_slice_in_dim(values_all, start, block_size, 0)
        new_top = jnp.maximum(top_score, jnp.max(scores, axis=-1))
        soft = jnp.exp(scores - new_top[..., None])
        shrink = jnp.exp(top_score - new_top)
        total = total * shrink + jnp.sum(soft, axis=-1)
        mixed = mixed * shrink[..., None] + jnp.einsum(
            "rkgs,skd->rkgd", soft.astype(low), value_block, preferred_element_type=wide
        )
        return (new_top, total, mixed)

    start_top = jnp.full((row_count, HK, GROUP), masked_score, wide)
    start_total = jnp.zeros((row_count, HK, GROUP), wide)
    start_mixed = jnp.zeros((row_count, HK, GROUP, HD), wide)
    top_score, total, mixed = lax.fori_loop(
        0, key_total // block_size, step, (start_top, start_total, start_mixed)
    )
    return (mixed / total[..., None], top_score + jnp.log(total))


def rows_backward(
    query_rot, keys_all, values_all, own_places, all_places, log_total, delta, grad_mixed
):
    row_count = query_rot.shape[0]
    key_total = keys_all.shape[0]
    block_size = math.gcd(key_total, 512)

    def step(block_index, carry):
        grad_query, grad_keys, grad_values = carry
        start = block_index * block_size
        scores, key_block = scores_of(
            query_rot, keys_all, own_places, all_places, start, block_size
        )
        value_block = lax.dynamic_slice_in_dim(values_all, start, block_size, 0)
        soft = jnp.exp(scores - log_total[..., None])
        grad_soft = jnp.einsum(
            "rkgd,skd->rkgs", grad_mixed, value_block, preferred_element_type=wide
        )
        steep = (soft * (grad_soft - delta[..., None])).astype(low)
        grad_query = grad_query + scale * jnp.einsum(
            "rkgs,skd->rkgd", steep, key_block, preferred_element_type=wide
        )
        key_part = scale * jnp.einsum(
            "rkgs,rkgd->skd", steep, query_rot, preferred_element_type=wide
        )
        value_part = jnp.einsum(
            "rkgs,rkgd->skd", soft.astype(low), grad_mixed, preferred_element_type=wide
        )
        grad_keys = lax.dynamic_update_slice_in_dim(
            grad_keys, key_part.reshape(block_size, HK * HD), start, 0
        )
        grad_values = lax.dynamic_update_slice_in_dim(
            grad_values, value_part.reshape(block_size, HK * HD), start, 0
        )
        return (grad_query, grad_keys, grad_values)

    start_query = jnp.zeros((row_count, HK, GROUP, HD), wide)
    start_keys = jnp.zeros((key_total, HK * HD), wide)
    return lax.fori_loop(
        0, key_total // block_size, step, (start_query, start_keys, start_keys)
    )


def exchange_levels(cut):
    return [over_ctx(cut(k), 2 * k) for k in (1, 2, 3)]


def deal_fsdp(cut, *others):
    got = [over_fsdp(cut(k), k) for k in (1, 2, 3)]
    return jnp.stack([cut(0)] + [after(array, *others) for array in got])


def terms_of(left, right):
    return contract_first(left, right).astype(low).reshape(4, left.shape[1] // 4, right.shape[1])


def side_of(terms, other):
    side, half = lax.axis_index("ctx") % 2, terms.shape[1] // 2
    return lax.dynamic_slice_in_dim(terms, (side ^ other) * half, half, 1)


def level_of(terms, k):
    level, quarter = lax.axis_index("ctx") // 2, terms.shape[1] // 4
    return lax.dynamic_slice_in_dim(terms, (level ^ k) * quarter, quarter, 1)


ring = (0, 2, 4, 6, 7, 5, 3, 1)


def turn_ring(array, step):
    count = len(ring)
    return lax.ppermute(
        array, "ctx", [(ring[i], ring[(i + step) % count]) for i in range(count)]
    )


def gather_plain(units, sums):
    size, part = lax.axis_size("ctx"), lax.axis_index("fsdp")
    _, height, span = units.shape
    units = lax.all_gather(units, "ctx", axis=0)
    units = jnp.stack(
        [lax.dynamic_index_in_dim(units, part ^ k, 1, keepdims=False) for k in range(4)]
    ).reshape(4, size, height, 3, span // 3)
    units = units.transpose(3, 2, 0, 1, 4).reshape(3, height, -1).astype(wide)
    sums = lax.all_gather(sums, "ctx", axis=1, tiled=True)
    sums = [lax.dynamic_index_in_dim(sums, part ^ k, 0, keepdims=False) for k in range(4)]
    sums = jnp.stack(sums, axis=1).astype(wide)
    sums = sums.reshape(height, 4, 3, -1).transpose(2, 0, 1, 3).reshape(3, height, -1)
    half = sums.shape[2] // 2
    return (*units, sums[0], sums[1], sums[2, :, :half], sums[2, :, half:])


UPPER = 176


def deal_kernel(code_ref, *refs):
    count = len(ring)
    outs = refs[2 * count :]
    units, (out_ref, query_ref, key_ref, value_ref) = outs[:3], outs[3:]
    quarter = pl.program_id(0)
    for lower in range(2):
        for step in range(count):
            part = refs[lower * count + step]
            place = code_ref[1 + lower * count + step]
            piece = part.shape[2] // 3
            height = out_ref.shape[0] // count
            first = (2 - lower) * height
            here = slice(UPPER, None) if lower else slice(0, UPPER)
            across = pl.ds(pl.multiple_of(place * piece, piece), piece)
            for i, unit_ref in enumerate(units):
                unit_ref[here, across] = part[0, first:, i * piece : (i + 1) * piece].astype(wide)
            rows_at = pl.multiple_of(((place % 2) * 4 + place // 2) * height, height)
            down = pl.ds(rows_at, height)
            if not lower:
                out_ref[down, :] = part[0, :height].astype(wide)
                query_ref[down, :] = part[0, height:first].astype(wide)
                continue

            @pl.when(quarter < 2)
            def _(part=part, down=down):
                key_ref[down, :] = part[0, :height].astype(wide)

            @pl.when(quarter >= 2)
            def _(part=part, down=down):
                value_ref[down, :] = part[0, :height].astype(wide)


def gather_all(units, sums):
    here, size, part = lax.axis_index("ctx"), lax.axis_size("ctx"), lax.axis_index("fsdp")
    if size != 8:
        return gather_plain(units, sums)
    width = sums.shape[2] // 3
    thirds = [sums[:, :, i * width : (i + 1) * width] for i in range(3)]
    upper = [jnp.concatenate([thirds[0], thirds[1], units[:, :UPPER]], axis=1)]
    lower = [jnp.concatenate([thirds[2], units[:, UPPER:]], axis=1)]
    for _ in range(size - 1):
        upper.append(turn_ring(upper[-1], 1))
        lower.append(turn_ring(lower[-1], -1))
    order = jnp.asarray(ring, jnp.int32)
    turn = jnp.argmax(order == here).astype(jnp.int32)
    steps = jnp.arange(size, dtype=jnp.int32)
    code = jnp.concatenate(
        [part.reshape(1), order[(turn - steps) % size], order[(turn + steps) % size]]
    ).astype(jnp.int32)
    height, across = units.shape[1], units.shape[2] // 3 * size

    def incoming(array):
        return pl.BlockSpec((1,) + array.shape[1:], lambda i, code: (code[0] ^ i, 0, 0))

    def outgoing(count, index):
        return pl.BlockSpec((height, count), lambda i, code: (0, index(i)))

    return pl.pallas_call(
        deal_kernel,
        grid_spec=pltpu.PrefetchScalarGridSpec(
            num_scalar_prefetch=1,
            grid=(4,),
            in_specs=[incoming(array) for array in (*upper, *lower)],
            out_specs=[outgoing(across, lambda i: i)] * 3
            + [outgoing(width, lambda i: i)] * 2
            + [
                outgoing(width, lambda i: jnp.minimum(i, 1)),
                outgoing(width, lambda i: jnp.maximum(i - 2, 0)),
            ],
        ),
        out_shape=[jax.ShapeDtypeStruct((height, 4 * across), wide)] * 3
        + [jax.ShapeDtypeStruct((height, 4 * width), wide)] * 2
        + [jax.ShapeDtypeStruct((height, 2 * width), wide)] * 2,
        compiler_params=pltpu.CompilerParams(vmem_limit_bytes=56 << 20),
        cost_estimate=brief,
        name="deal_gradients",
    )(code, *upper, *lower)


def deal_rows(piece, *others):
    part = lax.axis_index("fsdp")
    return deal_fsdp(lambda k: rows(piece, part ^ k, piece.shape[0] // 4), *others)


def unit_grads_kernel(normed_ref, grad_ref, gate_ref, up_ref, hidden_ref, out_ref, flipped):
    @pl.when(pl.program_id(0) == 0)
    def _():
        flipped[0] = normed_ref[...].T
        flipped[1] = grad_ref[...].T

    piece = hidden_ref.shape[1]
    right = jnp.concatenate([gate_ref[...], up_ref[...]], axis=1)
    out_ref[:, : 2 * piece] = product(flipped[0], right).astype(low)
    out_ref[:, 2 * piece :] = product(flipped[1], hidden_ref[...]).astype(low)


def unit_grads(normed, grad, grad_gate, grad_up, hidden):
    size = lax.axis_size("ctx")
    count, depth = normed.shape
    piece = hidden.shape[1] // size
    rights = (grad_gate, grad_up, hidden)
    if piece % 128:
        cut = [
            contract_first(left, right).astype(low).reshape(depth, size, piece)
            for left, right in zip((normed, normed, grad), rights)
        ]
        return jnp.concatenate(cut, axis=2).transpose(1, 0, 2).reshape(size * depth, 3 * piece)
    whole = pl.BlockSpec(memory_space=pltpu.VMEM)
    return pl.pallas_call(
        unit_grads_kernel,
        grid=(size,),
        in_specs=[whole, whole] + [pl.BlockSpec((count, piece), lambda i: (0, i))] * 3,
        out_specs=pl.BlockSpec((depth, 3 * piece), lambda i: (i, 0)),
        scratch_shapes=[pltpu.VMEM((2, depth, count), low)],
        out_shape=jax.ShapeDtypeStruct((size * depth, 3 * piece), low),
        compiler_params=pltpu.CompilerParams(vmem_limit_bytes=40 << 20),
        cost_estimate=lasting,
        name="unit_grads",
    )(normed, grad, *rights)


def sum_gains(array, *others):
    part, size = lax.axis_index("fsdp"), lax.axis_size("ctx")
    width = array.shape[1] // 4
    array = jnp.sum(deal_fsdp(lambda k: columns(array, part ^ k, width)), axis=0)
    array = array + after(over_ctx(array, 1), *others[0])
    if size == 8:
        return array + sum(after(got, *others[1]) for got in exchange_levels(lambda k: array))
    bits = 2
    while bits < size:
        array = array + over_ctx(array, bits)
        bits *= 2
    return array


def body(
    hidden_in,
    out_grad,
    positions,
    attn_gain,
    w_query,
    w_key,
    w_value,
    w_out,
    ffn_gain,
    w_gate,
    w_up,
    w_down,
):
    part, here, size = lax.axis_index("fsdp"), lax.axis_index("ctx"), lax.axis_size("ctx")
    code = jnp.stack([part, here % 2, here // 2 % 2]).astype(jnp.int32)
    own_gains = jnp.stack([attn_gain, ffn_gain])
    gains = [own_gains] + [over_fsdp(own_gains, k) for k in (1, 2, 3)]
    rows_in, grad_down = hidden_in[0], out_grad[0]
    row_count = rows_in.shape[0]
    all_places = positions[0]
    own_places = lax.dynamic_slice_in_dim(all_places, here * row_count, row_count, 0)
    cosine, sine = angles_of(own_places)
    cosine = jnp.concatenate([cosine[:, 0], cosine[:, 0]], axis=1)
    sine = jnp.concatenate([-sine[:, 0], sine[:, 0]], axis=1)

    own, near, far, both = deal_weights((w_gate, w_up, w_down))
    heads = gather_thirds(jnp.concatenate([w_query, w_key, w_value], axis=1), near, far, both, *gains[1:])
    normed_one, load = heads_call(code, rows_in, cosine, sine, gains, heads)
    outward = gather_halves(w_out)
    load, near, far, both, _ = lax.optimization_barrier((load, near, far, both, outward[2]))
    far, both = over_fsdp(far, 2), over_fsdp(both, 3)
    near = over_fsdp(near, 1)
    far_other, both_other = over_ctx(far, 1), over_ctx(both, 2)

    if size == HK:
        load = lax.all_to_all(load, "ctx", 0, 0, tiled=True)
        order = all_places[::BLK] // BLK
        mixed = attention_forward(order, after(load, far))
        grad_all = gather_fsdp(grad_down, mixed)
        mixed = lax.all_to_all(after(mixed, far_other, outward[3]), "ctx", 0, 0, tiled=True)
    else:
        query_rot = load[:, :, : GROUP * HD].transpose(1, 0, 2)
        query_rot = query_rot.reshape(row_count, HK, GROUP, HD)
        keys_values = load[:, :, GROUP * HD :].transpose(1, 0, 2)
        keys_values = lax.all_gather(keys_values, "ctx", axis=0, tiled=True)
        keys_all, values_all = keys_values[:, :, :HD], keys_values[:, :, HD:]
        mixed_exact, log_total = rows_forward(
            query_rot, keys_all, values_all, own_places, all_places
        )
        mixed = mixed_exact.reshape(row_count, HK, GROUP * HD).transpose(1, 0, 2).astype(low)
        grad_all = gather_fsdp(grad_down)

    dealt = (own, near, far, far_other, both, both_other)
    mixed_low, middle, normed_two = middle_call(
        code, rows_in, after(mixed, both, grad_all), gains, outward
    )
    normed_all = gather_fsdp(normed_two, both_other)
    out_terms, back_terms, hidden, grad_gate, grad_up = units_call(
        code, normed_all, grad_all, dealt
    )
    grad_normed_two, passed = scatter_fsdp(back_terms)
    unit_terms = unit_grads(normed_all, grad_all, after(grad_gate, passed), grad_up, hidden)
    grad_normed_two, unit_terms = lax.optimization_barrier((grad_normed_two, unit_terms))
    grad_middle, grad_branch, grad_mixed, grad_gain_two = middle_back_call(
        code, middle, grad_normed_two, grad_down, gains, outward
    )
    unit_sums = lax.psum_scatter(unit_terms, "ctx", scatter_dimension=0, tiled=True)

    if size == HK:
        grad_mixed = lax.all_to_all(grad_mixed, "ctx", 0, 0, tiled=True)
        grad_load = attention_backward(order, load, grad_mixed)
        mid = grad_load
        grad_load = lax.all_to_all(grad_load, "ctx", 0, 0, tiled=True)
    else:
        grad_mixed = grad_mixed.transpose(1, 0, 2).reshape(row_count, HK, GROUP, HD)
        delta = jnp.sum(grad_mixed.astype(wide) * mixed_exact, axis=-1)
        grad_query, grad_keys, grad_values = rows_backward(
            query_rot, keys_all, values_all, own_places, all_places, log_total, delta, grad_mixed
        )
        grad_keys, grad_values = (
            lax.psum_scatter(whole.astype(low), "ctx", scatter_dimension=0, tiled=True)
            for whole in (grad_keys, grad_values)
        )
        grad_load = jnp.concatenate(
            [
                grad_query.reshape(row_count, HK, GROUP * HD).astype(low),
                grad_keys.reshape(row_count, HK, HD),
                grad_values.reshape(row_count, HK, HD),
            ],
            axis=2,
        ).transpose(1, 0, 2)
        mid = grad_load

    quarter = HQ * HD // 4
    turn = (0, 2, 1, 3)

    def own_columns(cut, *others):
        dealt = deal_fsdp(cut, *others)
        return jnp.concatenate([dealt[k] for k in turn], axis=0)

    branch_all = gather_fsdp(grad_branch, mid)
    mixed_part = own_columns(lambda k: columns(mixed_low, part ^ k, quarter), mid)
    normed_one_all = gather_fsdp(after(normed_one, grad_branch), mid)
    branch_terms = terms_of(branch_all, mixed_part)
    if size == HK:
        out_got = over_ctx(side_of(branch_terms, 1), 1)
    grad_whole, grad_raw = turn_back_call(code, grad_load, cosine, sine)
    input_grad, grad_gain_one = heads_back_call(
        code, grad_whole, rows_in, grad_middle, gains, heads
    )
    result, _ = scatter_fsdp(after(out_terms, grad_normed_two), mid)
    result = (middle + result).astype(low)
    raw_part = own_columns(
        lambda k: lax.dynamic_index_in_dim(grad_raw, part ^ k, 0, keepdims=False)
    )
    gain_terms = jnp.concatenate([grad_gain_one, grad_gain_two], axis=0)
    if size == HK:
        raw_part, out_got = together(raw_part, out_got)
        out_kept = add_low(side_of(branch_terms, 0), out_got)
        raw_terms = terms_of(normed_one_all, raw_part)
        raw_got = over_ctx(side_of(raw_terms, 1), 1)
        out_got = exchange_levels(lambda k: level_of(out_kept, k))
        raw_got, out_got = together(raw_got, out_got)
        raw_kept = add_low(side_of(raw_terms, 0), raw_got)
        out_sums = add_low(level_of(out_kept, 0), *out_got)
        raw_kept, unit_sums = together(raw_kept, unit_sums)
        raw_got = exchange_levels(lambda k: level_of(raw_kept, k))
        unit_mine = deal_rows(unit_sums)
        raw_got, unit_mine = together(raw_got, unit_mine)
        raw_sums = add_low(level_of(raw_kept, 0), *raw_got)
    else:
        raw_terms = terms_of(normed_one_all, raw_part)
        out_sums, raw_sums = (
            lax.psum_scatter(terms, "ctx", scatter_dimension=1, tiled=True)
            for terms in (branch_terms, raw_terms)
        )
        raw_kept = raw_terms
        unit_mine = deal_rows(unit_sums)
    sums = jnp.concatenate([out_sums, raw_sums], axis=2)
    sums = deal_fsdp(lambda k: lax.dynamic_index_in_dim(sums, part ^ k, 0, keepdims=False))
    gain_grads = sum_gains(
        gain_terms, (raw_kept,), (sums,)
    )
    gate_grad, up_grad, down_grad, out_weight_grad, query_grad, key_grad, value_grad = gather_all(
        unit_mine, sums
    )
    return (
        result[None],
        input_grad[None],
        gain_grads[0],
        query_grad,
        key_grad,
        value_grad,
        out_weight_grad,
        gain_grads[1],
        gate_grad,
        up_grad,
        down_grad,
    )


def solution(mesh):
    matrix = P("fsdp", None)
    stream = P("fsdp", "ctx", None)
    return jax.shard_map(
        body,
        mesh=mesh,
        in_specs=(stream, stream, matrix, P("fsdp"))
        + (matrix,) * 4
        + (P("fsdp"),)
        + (matrix,) * 3,
        out_specs=(stream, stream, P("fsdp")) + (matrix,) * 4 + (P("fsdp"),) + (matrix,) * 3,
        check_vma=False,
    )
```

```python
import math

import jax
import jax.numpy as jnp
from jax import lax
from jax.experimental import pallas as pl
from jax.experimental.pallas import tpu as pltpu
from jax.sharding import PartitionSpec as P

HQ = 16
HK = 8
HD = 96
GROUP = HQ // HK
BLK = 128

epsilon = 1e-05
rope_base = 100000.0
masked_score = -1e30
scale = 1.0 / math.sqrt(HD)
low = jnp.bfloat16
wide = jnp.float32
brief = pl.CostEstimate(flops=0, bytes_accessed=0, transcendentals=0)
lasting = pl.CostEstimate(flops=10**11, bytes_accessed=0, transcendentals=0)


def angles_of(places):
    frequency = jnp.exp(jnp.arange(HD // 2, dtype=wide) * (-2.0 * math.log(rope_base) / HD))
    turned = places.astype(wide)[:, None] * frequency[None, :]
    return (jnp.cos(turned)[:, None, :], jnp.sin(turned)[:, None, :])


def product(left, right):
    return jnp.dot(left, right, preferred_element_type=wide)


def contract_last(left, right):
    return lax.dot_general(left, right, (((1,), (1,)), ((), ())), preferred_element_type=wide)


def contract_first(left, right):
    return lax.dot_general(left, right, (((0,), (0,)), ((), ())), preferred_element_type=wide)


def swap(array, axis, bits, size):
    return lax.ppermute(array, axis, [(i, i ^ bits) for i in range(size)])


def over_fsdp(array, bits):
    return swap(array, "fsdp", bits, 4)


def over_ctx(array, bits):
    return swap(array, "ctx", bits, lax.axis_size("ctx"))


def columns(array, index, width):
    return lax.dynamic_slice_in_dim(array, index * width, width, array.ndim - 1)


def rows(array, index, height):
    return lax.dynamic_slice_in_dim(array, index * height, height, 0)


def together(*arrays):
    return lax.optimization_barrier(arrays)


def after(array, *others):
    return lax.optimization_barrier((array, *others))[0]


def add_low(first, *others):
    total = first.astype(wide)
    for other in others:
        total = total + other.astype(wide)
    return total.astype(low)


def gather_fsdp(array, *others):
    far = after(over_fsdp(array, 2), *others)
    pair = over_fsdp(jnp.concatenate([array, far], axis=0), 1)
    return jnp.concatenate([array, far, pair], axis=0)


def scatter_fsdp(terms, *others):
    half, height = terms.shape[0] // 2, terms.shape[0] // 4
    kept, got = terms[:half], over_fsdp(terms[half:], 1)
    passed = add_low(kept[height:], got[height:])
    away = after(over_fsdp(passed, 2), *others)
    total = kept[:height].astype(wide) + got[:height].astype(wide) + away.astype(wide)
    return total, passed


ALL, REST, MINE, OTHER = 0, 3, 4, 8
heads_plan = (
    (0, ALL),
    (1, ALL),
    (2, MINE + 1),
    (2, OTHER + 1),
    (2, REST),
    (3, MINE + 1),
    (3, OTHER + 1),
    (3, REST),
)
outward_plan = ((0, ALL), (1, ALL), (2, MINE + 2), (2, OTHER + 2), (3, MINE + 2), (3, OTHER + 2))
units_plan = ((0, ALL), (1, ALL), (2, MINE + 1), (2, OTHER + 1), (3, MINE + 2), (3, OTHER + 2))


def gather_thirds(own, *others):
    side = lax.axis_index("ctx") % 2
    third = own.shape[1] // 3
    far = after(over_fsdp(columns(own, side, third), 2), *others)
    rest = over_fsdp(after(own[:, 2 * third :], far), 2)
    near = over_fsdp(own, 1)
    other = over_ctx(far, 1)
    return (
        own,
        near,
        far,
        other,
        rest,
        over_fsdp(far, 1),
        over_fsdp(other, 1),
        over_fsdp(rest, 1),
    )


def gather_halves(own):
    far = over_fsdp(columns(own, lax.axis_index("ctx") // 2 % 2, own.shape[1] // 2), 2)
    near = over_fsdp(own, 1)
    other = over_ctx(far, 2)
    return (own, near, far, other, over_fsdp(far, 1), over_fsdp(other, 1))


def fill_weight(code_ref, plan, pieces, out):
    part = code_ref[0]
    for (k, which), piece in zip(plan, pieces):
        height, width = piece.shape
        across = pl.ds(pl.multiple_of((part ^ k) * height, height), height)
        if which == ALL:
            out[across, :] = piece[...]
        elif which == REST:
            out[across, 2 * width :] = piece[...]
        else:
            side = code_ref[which % MINE]
            place = 1 - side if which >= OTHER else side
            out[across, lanes(place, width)] = piece[...]


def whole_call(kernel, code, arrays, outs, scratch, flops, name):
    spec = pl.BlockSpec(memory_space=pltpu.VMEM)
    moved = sum(math.prod(a.shape) * a.dtype.itemsize for a in (*arrays, *outs))
    return pl.pallas_call(
        kernel,
        grid_spec=pltpu.PrefetchScalarGridSpec(
            num_scalar_prefetch=1,
            grid=(),
            in_specs=[spec] * len(arrays),
            out_specs=[spec] * len(outs),
            scratch_shapes=scratch,
        ),
        out_shape=outs,
        compiler_params=pltpu.CompilerParams(vmem_limit_bytes=56 << 20),
        cost_estimate=pl.CostEstimate(flops=flops, bytes_accessed=moved, transcendentals=0),
        name=name,
    )(code, *arrays)


def lanes(index, width):
    return pl.ds(pl.multiple_of(index * width, 128), width)


def gained(code_ref, gains, row, out):
    for k in range(4):
        out[:, lanes(code_ref[0] ^ k, gains[k].shape[1])] = gains[k][row : row + 1, :].astype(wide)


def turned(values, cosine, sine):
    half = values.shape[1] // 2
    return values * cosine + jnp.concatenate([values[:, half:], values[:, :half]], axis=1) * sine


def inverse_rms(values):
    return lax.rsqrt(jnp.mean(values * values, axis=1, keepdims=True) + epsilon)


def slot_of_head(head):
    if head < HQ:
        return head // GROUP, head % GROUP
    return (head - HQ) % HK, GROUP + (head - HQ) // HK


def heads_kernel(code_ref, rows_ref, cosine_ref, sine_ref, *refs):
    gains, pieces = refs[:4], refs[4:12]
    normed_ref, load_ref, gain, weight, total = refs[12:]
    gained(code_ref, gains, 0, gain)
    fill_weight(code_ref, heads_plan, pieces, weight)
    values = rows_ref[...].astype(wide)
    normed_ref[...] = (values * inverse_rms(values) * gain[...]).astype(low)
    total[...] = product(normed_ref[...], weight[...])
    cosine, sine = cosine_ref[...], sine_ref[...]
    for head in range(HQ + 2 * HK):
        part = total[:, head * HD : (head + 1) * HD]
        if head < HQ + HK:
            part = turned(part, cosine, sine)
        group, place = slot_of_head(head)
        load_ref[group, :, place * HD : (place + 1) * HD] = part.astype(low)


def heads_call(code, rows_in, cosine, sine, gains, pieces):
    count, width = rows_in.shape
    total = pieces[0].shape[1]
    outs = [
        jax.ShapeDtypeStruct((count, width), low),
        jax.ShapeDtypeStruct((HK, count, (GROUP + 2) * HD), low),
    ]
    scratch = [
        pltpu.VMEM((1, width), wide),
        pltpu.VMEM((width, total), low),
        pltpu.VMEM((count, total), wide),
    ]
    return whole_call(
        heads_kernel,
        code,
        (rows_in, cosine, sine, *gains, *pieces),
        outs,
        scratch,
        2 * count * width * total,
        "query_key_value",
    )


def middle_kernel(code_ref, rows_ref, mixed_ref, *refs):
    gains, pieces = refs[:4], refs[4:10]
    flat_ref, middle_ref, normed_ref, gain, weight = refs[10:]
    gained(code_ref, gains, 1, gain)
    fill_weight(code_ref, outward_plan, pieces, weight)
    span = mixed_ref.shape[2]
    for group in range(mixed_ref.shape[0]):
        flat_ref[:, group * span : (group + 1) * span] = mixed_ref[group]
    middle = contract_last(flat_ref[...], weight[...]) + rows_ref[...].astype(wide)
    middle_ref[...] = middle
    normed_ref[...] = (middle * inverse_rms(middle) * gain[...]).astype(low)


def middle_call(code, rows_in, mixed, gains, pieces):
    count, width = rows_in.shape
    outs = [
        jax.ShapeDtypeStruct((count, HQ * HD), low),
        jax.ShapeDtypeStruct((count, width), wide),
        jax.ShapeDtypeStruct((count, width), low),
    ]
    return whole_call(
        middle_kernel,
        code,
        (rows_in, mixed, *gains, *pieces),
        outs,
        [pltpu.VMEM((1, width), wide), pltpu.VMEM((width, HQ * HD), low)],
        2 * count * width * HQ * HD,
        "attention_output",
    )


def norm_back(values, gain, grad):
    inverse = inverse_rms(values)
    weighted = gain * grad
    inner = jnp.mean(values * weighted, axis=1, keepdims=True)
    back = inverse * weighted - values * inverse * inverse * inverse * inner
    return back, jnp.sum(grad * values * inverse, axis=0, keepdims=True)


def middle_back_kernel(code_ref, middle_ref, grad_ref, out_grad_ref, *refs):
    gains, pieces = refs[:4], refs[4:10]
    grad_middle_ref, branch_ref, sent_ref, gain_grad_ref, gain, weight = refs[10:]
    gained(code_ref, gains, 1, gain)
    fill_weight(code_ref, outward_plan, pieces, weight)
    back, gain_grad_ref[...] = norm_back(middle_ref[...], gain[...], grad_ref[...])
    grad_middle = out_grad_ref[...].astype(wide) + back
    grad_middle_ref[...] = grad_middle
    branch_ref[...] = grad_middle.astype(low)
    total = product(branch_ref[...], weight[...]).astype(low)
    span = sent_ref.shape[2]
    for group in range(sent_ref.shape[0]):
        sent_ref[group] = total[:, group * span : (group + 1) * span]


def middle_back_call(code, middle, grad, out_grad, gains, pieces):
    count, width = middle.shape
    outs = [
        jax.ShapeDtypeStruct((count, width), wide),
        jax.ShapeDtypeStruct((count, width), low),
        jax.ShapeDtypeStruct((HK, count, GROUP * HD), low),
        jax.ShapeDtypeStruct((1, width), wide),
    ]
    return whole_call(
        middle_back_kernel,
        code,
        (middle, grad, out_grad, *gains, *pieces),
        outs,
        [pltpu.VMEM((1, width), wide), pltpu.VMEM((width, HQ * HD), low)],
        2 * count * width * HQ * HD,
        "attention_output_back",
    )


def turn_back_kernel(code_ref, load_ref, cosine_ref, sine_ref, raw_ref, parts_ref):
    cosine, sine = cosine_ref[...], sine_ref[...]
    for head in range(HQ + 2 * HK):
        group, place = slot_of_head(head)
        part = load_ref[group, :, place * HD : (place + 1) * HD]
        if head < HQ + HK:
            part = turned(part.astype(wide), cosine, -sine).astype(low)
        raw_ref[:, head * HD : (head + 1) * HD] = part
    quarter = parts_ref.shape[2] // 2
    for k in range(4):
        for i in range(2):
            first = (4 * i + k) * quarter
            parts_ref[k, :, i * quarter : (i + 1) * quarter] = raw_ref[:, first : first + quarter]


def turn_back_call(code, load, cosine, sine):
    count, total = load.shape[1], load.shape[0] * load.shape[2]
    outs = [
        jax.ShapeDtypeStruct((count, total), low),
        jax.ShapeDtypeStruct((4, count, total // 4), low),
    ]
    return whole_call(turn_back_kernel, code, (load, cosine, sine), outs, [], 0, "turn_back")


def heads_back_kernel(code_ref, raw_ref, rows_ref, grad_middle_ref, *refs):
    gains, pieces = refs[:4], refs[4:12]
    input_grad_ref, gain_grad_ref, gain, weight = refs[12:]
    gained(code_ref, gains, 0, gain)
    fill_weight(code_ref, heads_plan, pieces, weight)
    grad = contract_last(raw_ref[...], weight[...])
    back, gain_grad_ref[...] = norm_back(rows_ref[...].astype(wide), gain[...], grad)
    input_grad_ref[...] = grad_middle_ref[...] + back


def heads_back_call(code, raw, rows_in, grad_middle, gains, pieces):
    count, width = rows_in.shape
    total = pieces[0].shape[1]
    outs = [
        jax.ShapeDtypeStruct((count, width), wide),
        jax.ShapeDtypeStruct((1, width), wide),
    ]
    return whole_call(
        heads_back_kernel,
        code,
        (raw, rows_in, grad_middle, *gains, *pieces),
        outs,
        [pltpu.VMEM((1, width), wide), pltpu.VMEM((width, total), low)],
        2 * count * width * total,
        "query_key_value_back",
    )


def units_kernel(code_ref, normed_ref, grad_ref, *refs):
    pieces = refs[:6]
    out_ref, back_ref, hidden_ref, grad_gate_ref, grad_up_ref, weights = refs[6:]

    @pl.when(pl.program_id(0) == 0)
    def _():
        for i in range(3):
            fill_weight(code_ref, units_plan, [piece.at[i] for piece in pieces], weights.at[i])

    gate = product(normed_ref[...], weights[0])
    upward = product(normed_ref[...], weights[1])
    sigmoid_gate = jax.nn.sigmoid(gate)
    swish = gate * sigmoid_gate
    hidden = (swish * upward).astype(low)
    hidden_ref[...] = hidden
    grad_hidden = product(grad_ref[...], weights[2])
    grad_gate = (
        grad_hidden * upward * sigmoid_gate * (1.0 + gate * (1.0 - sigmoid_gate))
    ).astype(low)
    grad_up = (grad_hidden * swish).astype(low)
    grad_gate_ref[...] = grad_gate
    grad_up_ref[...] = grad_up
    back_ref[...] = (
        contract_last(grad_gate, weights[0]) + contract_last(grad_up, weights[1])
    ).astype(low)
    out_ref[...] = contract_last(hidden, weights[2]).astype(low)


def units_call(code, normed, grad, pieces):
    count, width = normed.shape
    units = pieces[0].shape[2]
    tile = 512
    wide_block = pl.BlockSpec((tile, width), lambda i, code: (i, 0))
    unit_block = pl.BlockSpec((tile, units), lambda i, code: (i, 0))
    return pl.pallas_call(
        units_kernel,
        grid_spec=pltpu.PrefetchScalarGridSpec(
            num_scalar_prefetch=1,
            grid=(count // tile,),
            in_specs=[wide_block, wide_block]
            + [pl.BlockSpec(memory_space=pltpu.VMEM)] * len(pieces),
            out_specs=[wide_block, wide_block, unit_block, unit_block, unit_block],
            scratch_shapes=[pltpu.VMEM((3, width, units), low)],
        ),
        out_shape=[jax.ShapeDtypeStruct((count, width), low)] * 2
        + [jax.ShapeDtypeStruct((count, units), low)] * 3,
        compiler_params=pltpu.CompilerParams(vmem_limit_bytes=60 << 20),
        cost_estimate=pl.CostEstimate(
            flops=12 * count * width * units,
            bytes_accessed=8 * count * width + 6 * width * units,
            transcendentals=count * units,
        ),
        name="feed_forward",
    )(code, normed, grad, *pieces)


def deal_weights(weights):
    part, here = lax.axis_index("fsdp"), lax.axis_index("ctx")
    width = weights[0].shape[1] // 4

    def taken(k):
        return jnp.stack([columns(weight, part ^ k, width) for weight in weights])

    def half(k, side):
        return jnp.stack(
            [columns(weight, (part ^ k) * 2 + side, width // 2) for weight in weights]
        )

    return taken(0), taken(1), half(2, here % 2), half(3, here // 2 % 2)


def slot_of(ref, slot):
    return ref.at[slot // 2, (slot % 2) * BLK : (slot % 2 + 1) * BLK, :]


def sort_rows(order_ref, load_ref, queries, keys, values):
    for slot in range(2 * load_ref.shape[0]):
        block = order_ref[slot]
        piece = slot_of(load_ref, slot)[...]
        place = pl.ds(pl.multiple_of(block * BLK, BLK), BLK)
        half = pl.ds(pl.multiple_of((block % 2) * BLK, BLK), BLK)
        other = pl.ds(pl.multiple_of((block % 2) * BLK + 2 * BLK, BLK), BLK)
        queries[block // 2, half, :] = piece[:, :HD]
        queries[block // 2, other, :] = piece[:, HD : 2 * HD]
        keys[place, :] = piece[:, 2 * HD : 3 * HD]
        values[place, :] = piece[:, 3 * HD :]


def forward_kernel(order_ref, load_ref, out_ref, queries, keys, values, mixed):
    sort_rows(order_ref, load_ref, queries, keys, values)
    step = 2 * BLK
    query_at = lax.broadcasted_iota(jnp.int32, (2 * step, step), 0) % step
    key_at = lax.broadcasted_iota(jnp.int32, (2 * step, step), 1)
    allowed = key_at <= query_at
    for i in range(keys.shape[0] // step):
        reach = (i + 1) * step
        query = queries[i]
        ahead = contract_last(query, keys[i * step : reach, :]) * scale
        ahead = jnp.where(allowed, ahead, masked_score)
        top = jnp.max(ahead, axis=1, keepdims=True)
        if i:
            before = contract_last(query, keys[: i * step, :]) * scale
            top = jnp.maximum(top, jnp.max(before, axis=1, keepdims=True))
        soft = jnp.exp(ahead - top)
        total = jnp.sum(soft, axis=1, keepdims=True)
        result = product(soft.astype(low), values[i * step : reach, :])
        if i:
            soft = jnp.exp(before - top)
            total = total + jnp.sum(soft, axis=1, keepdims=True)
            result = result + product(soft.astype(low), values[: i * step, :])
        result = (result / total).astype(low)
        mixed[i * step : reach, :HD] = result[:step]
        mixed[i * step : reach, HD:] = result[step:]
    for slot in range(2 * load_ref.shape[0]):
        place = pl.ds(pl.multiple_of(order_ref[slot] * BLK, BLK), BLK)
        slot_of(out_ref, slot)[...] = mixed[place, :]


def backward_kernel(
    order_ref, load_ref, grad_ref, out_ref, queries, keys, values, grads, key_sum, value_sum, sent
):
    sort_rows(order_ref, load_ref, queries, keys, values)
    step = 2 * BLK
    length = keys.shape[0]
    for slot in range(length // BLK):
        block = order_ref[slot]
        piece = slot_of(grad_ref, slot)[...]
        half = pl.ds(pl.multiple_of((block % 2) * BLK, BLK), BLK)
        other = pl.ds(pl.multiple_of((block % 2) * BLK + 2 * BLK, BLK), BLK)
        grads[block // 2, half, :] = piece[:, :HD]
        grads[block // 2, other, :] = piece[:, HD:]
    key_at = lax.broadcasted_iota(jnp.int32, (step, 2 * step), 0)
    query_at = lax.broadcasted_iota(jnp.int32, (step, 2 * step), 1) % step
    allowed = key_at <= query_at
    for i in range(length // step):
        query = queries[i]
        grad = grads[i]
        scores = []
        top = None
        for j in range(i + 1):
            score = contract_last(keys[j * step : (j + 1) * step, :], query) * scale
            if j == i:
                score = jnp.where(allowed, score, masked_score)
            high = jnp.max(score, axis=0, keepdims=True)
            top = high if top is None else jnp.maximum(top, high)
            scores.append(score)
        total = jnp.zeros_like(top)
        delta = jnp.zeros_like(top)
        softs = []
        slopes = []
        for j in range(i + 1):
            soft = jnp.exp(scores[j] - top)
            slope = contract_last(values[j * step : (j + 1) * step, :], grad)
            total = total + jnp.sum(soft, axis=0, keepdims=True)
            delta = delta + jnp.sum(soft * slope, axis=0, keepdims=True)
            softs.append(soft)
            slopes.append(slope)
        share = 1.0 / total
        delta = delta * share
        query_sum = jnp.zeros((2 * step, HD), wide)
        for j in range(i + 1):
            place = slice(j * step, (j + 1) * step)
            soft = softs[j] * share
            steep = (soft * (slopes[j] - delta)).astype(low)
            key_part = product(steep, query)
            value_part = product(soft.astype(low), grad)
            if j == i:
                key_sum[place, :] = key_part
                value_sum[place, :] = value_part
            else:
                key_sum[place, :] += key_part
                value_sum[place, :] += value_part
            query_sum = query_sum + contract_first(steep, keys[place, :])
        query_sum = (query_sum * scale).astype(low)
        sent[i * step : (i + 1) * step, :HD] = query_sum[:step]
        sent[i * step : (i + 1) * step, HD : 2 * HD] = query_sum[step:]
    sent[:, 2 * HD : 3 * HD] = (key_sum[...] * scale).astype(low)
    sent[:, 3 * HD :] = value_sum[...].astype(low)
    for slot in range(length // BLK):
        place = pl.ds(pl.multiple_of(order_ref[slot] * BLK, BLK), BLK)
        slot_of(out_ref, slot)[...] = sent[place, :]


def attention_call(kernel, order, arrays, width, scratch, products, name):
    devices, height = arrays[0].shape[:2]
    length = devices * height
    half = (length * length) // 2 * GROUP
    whole = pl.BlockSpec(memory_space=pltpu.VMEM)
    return pl.pallas_call(
        kernel,
        grid_spec=pltpu.PrefetchScalarGridSpec(
            num_scalar_prefetch=1,
            grid=(),
            in_specs=[whole] * len(arrays),
            out_specs=whole,
            scratch_shapes=scratch,
        ),
        out_shape=jax.ShapeDtypeStruct((devices, height, width), low),
        compiler_params=pltpu.CompilerParams(vmem_limit_bytes=56 << 20),
        cost_estimate=pl.CostEstimate(
            flops=2 * products * half * 256, bytes_accessed=8 * length * width, transcendentals=half
        ),
        name=name,
    )(order, *arrays)


def attention_forward(order, load):
    length = load.shape[0] * load.shape[1]
    scratch = [
        pltpu.VMEM((length // (2 * BLK), 4 * BLK, HD), low),
        pltpu.VMEM((length, HD), low),
        pltpu.VMEM((length, HD), low),
        pltpu.VMEM((length, 2 * HD), low),
    ]
    return attention_call(forward_kernel, order, (load,), 2 * HD, scratch, 2, "attention_forward")


def attention_backward(order, load, grad):
    length = load.shape[0] * load.shape[1]
    scratch = [
        pltpu.VMEM((length // (2 * BLK), 4 * BLK, HD), low),
        pltpu.VMEM((length, HD), low),
        pltpu.VMEM((length, HD), low),
        pltpu.VMEM((length // (2 * BLK), 4 * BLK, HD), low),
        pltpu.VMEM((length, HD), wide),
        pltpu.VMEM((length, HD), wide),
        pltpu.VMEM((length, 4 * HD), low),
    ]
    return attention_call(
        backward_kernel, order, (load, grad), 4 * HD, scratch, 5, "attention_backward"
    )


def scores_of(query_rot, keys_all, own_places, all_places, start, block_size):
    key_block = lax.dynamic_slice_in_dim(keys_all, start, block_size, 0)
    key_places = lax.dynamic_slice_in_dim(all_places, start, block_size, 0)
    raw = (
        jnp.einsum("rkgd,skd->rkgs", query_rot, key_block, preferred_element_type=wide) * scale
    )
    allowed = key_places[None, None, None, :] <= own_places[:, None, None, None]
    return (jnp.where(allowed, raw, masked_score), key_block)


def rows_forward(query_rot, keys_all, values_all, own_places, all_places):
    row_count = query_rot.shape[0]
    key_total = keys_all.shape[0]
    block_size = math.gcd(key_total, 512)

    def step(block_index, carry):
        top_score, total, mixed = carry
        start = block_index * block_size
        scores, _ = scores_of(query_rot, keys_all, own_places, all_places, start, block_size)
        value_block = lax.dynamic_slice_in_dim(values_all, start, block_size, 0)
        new_top = jnp.maximum(top_score, jnp.max(scores, axis=-1))
        soft = jnp.exp(scores - new_top[..., None])
        shrink = jnp.exp(top_score - new_top)
        total = total * shrink + jnp.sum(soft, axis=-1)
        mixed = mixed * shrink[..., None] + jnp.einsum(
            "rkgs,skd->rkgd", soft.astype(low), value_block, preferred_element_type=wide
        )
        return (new_top, total, mixed)

    start_top = jnp.full((row_count, HK, GROUP), masked_score, wide)
    start_total = jnp.zeros((row_count, HK, GROUP), wide)
    start_mixed = jnp.zeros((row_count, HK, GROUP, HD), wide)
    top_score, total, mixed = lax.fori_loop(
        0, key_total // block_size, step, (start_top, start_total, start_mixed)
    )
    return (mixed / total[..., None], top_score + jnp.log(total))


def rows_backward(
    query_rot, keys_all, values_all, own_places, all_places, log_total, delta, grad_mixed
):
    row_count = query_rot.shape[0]
    key_total = keys_all.shape[0]
    block_size = math.gcd(key_total, 512)

    def step(block_index, carry):
        grad_query, grad_keys, grad_values = carry
        start = block_index * block_size
        scores, key_block = scores_of(
            query_rot, keys_all, own_places, all_places, start, block_size
        )
        value_block = lax.dynamic_slice_in_dim(values_all, start, block_size, 0)
        soft = jnp.exp(scores - log_total[..., None])
        grad_soft = jnp.einsum(
            "rkgd,skd->rkgs", grad_mixed, value_block, preferred_element_type=wide
        )
        steep = (soft * (grad_soft - delta[..., None])).astype(low)
        grad_query = grad_query + scale * jnp.einsum(
            "rkgs,skd->rkgd", steep, key_block, preferred_element_type=wide
        )
        key_part = scale * jnp.einsum(
            "rkgs,rkgd->skd", steep, query_rot, preferred_element_type=wide
        )
        value_part = jnp.einsum(
            "rkgs,rkgd->skd", soft.astype(low), grad_mixed, preferred_element_type=wide
        )
        grad_keys = lax.dynamic_update_slice_in_dim(
            grad_keys, key_part.reshape(block_size, HK * HD), start, 0
        )
        grad_values = lax.dynamic_update_slice_in_dim(
            grad_values, value_part.reshape(block_size, HK * HD), start, 0
        )
        return (grad_query, grad_keys, grad_values)

    start_query = jnp.zeros((row_count, HK, GROUP, HD), wide)
    start_keys = jnp.zeros((key_total, HK * HD), wide)
    return lax.fori_loop(
        0, key_total // block_size, step, (start_query, start_keys, start_keys)
    )


def exchange_levels(cut):
    return [over_ctx(cut(k), 2 * k) for k in (1, 2, 3)]


def deal_fsdp(cut, *others):
    got = [over_fsdp(cut(k), k) for k in (1, 2, 3)]
    return jnp.stack([cut(0)] + [after(array, *others) for array in got])


def terms_of(left, right):
    return contract_first(left, right).astype(low).reshape(4, left.shape[1] // 4, right.shape[1])


def side_of(terms, other):
    side, half = lax.axis_index("ctx") % 2, terms.shape[1] // 2
    return lax.dynamic_slice_in_dim(terms, (side ^ other) * half, half, 1)


def level_of(terms, k):
    level, quarter = lax.axis_index("ctx") // 2, terms.shape[1] // 4
    return lax.dynamic_slice_in_dim(terms, (level ^ k) * quarter, quarter, 1)


ring = (0, 2, 4, 6, 7, 5, 3, 1)


def turn_ring(array, step):
    count = len(ring)
    return lax.ppermute(
        array, "ctx", [(ring[i], ring[(i + step) % count]) for i in range(count)]
    )


def gather_plain(units, sums):
    size, part = lax.axis_size("ctx"), lax.axis_index("fsdp")
    _, height, span = units.shape
    units = lax.all_gather(units, "ctx", axis=0)
    units = jnp.stack(
        [lax.dynamic_index_in_dim(units, part ^ k, 1, keepdims=False) for k in range(4)]
    ).reshape(4, size, height, 3, span // 3)
    units = units.transpose(3, 2, 0, 1, 4).reshape(3, height, -1).astype(wide)
    sums = lax.all_gather(sums, "ctx", axis=1, tiled=True)
    sums = [lax.dynamic_index_in_dim(sums, part ^ k, 0, keepdims=False) for k in range(4)]
    sums = jnp.stack(sums, axis=1).astype(wide)
    sums = sums.reshape(height, 4, 3, -1).transpose(2, 0, 1, 3).reshape(3, height, -1)
    half = sums.shape[2] // 2
    return (*units, sums[0], sums[1], sums[2, :, :half], sums[2, :, half:])


UPPER = 176


def deal_kernel(code_ref, *refs):
    count = len(ring)
    outs = refs[2 * count :]
    units, (out_ref, query_ref, key_ref, value_ref) = outs[:3], outs[3:]
    quarter = pl.program_id(0)
    for lower in range(2):
        for step in range(count):
            part = refs[lower * count + step]
            place = code_ref[1 + lower * count + step]
            piece = part.shape[2] // 3
            height = out_ref.shape[0] // count
            first = (2 - lower) * height
            here = slice(UPPER, None) if lower else slice(0, UPPER)
            across = pl.ds(pl.multiple_of(place * piece, piece), piece)
            for i, unit_ref in enumerate(units):
                unit_ref[here, across] = part[0, first:, i * piece : (i + 1) * piece].astype(wide)
            rows_at = pl.multiple_of(((place % 2) * 4 + place // 2) * height, height)
            down = pl.ds(rows_at, height)
            if not lower:
                out_ref[down, :] = part[0, :height].astype(wide)
                query_ref[down, :] = part[0, height:first].astype(wide)
                continue

            @pl.when(quarter < 2)
            def _(part=part, down=down):
                key_ref[down, :] = part[0, :height].astype(wide)

            @pl.when(quarter >= 2)
            def _(part=part, down=down):
                value_ref[down, :] = part[0, :height].astype(wide)


def gather_all(units, sums):
    here, size, part = lax.axis_index("ctx"), lax.axis_size("ctx"), lax.axis_index("fsdp")
    if size != 8:
        return gather_plain(units, sums)
    width = sums.shape[2] // 3
    thirds = [sums[:, :, i * width : (i + 1) * width] for i in range(3)]
    upper = [jnp.concatenate([thirds[0], thirds[1], units[:, :UPPER]], axis=1)]
    lower = [jnp.concatenate([thirds[2], units[:, UPPER:]], axis=1)]
    for _ in range(size - 1):
        upper.append(turn_ring(upper[-1], 1))
        lower.append(turn_ring(lower[-1], -1))
    order = jnp.asarray(ring, jnp.int32)
    turn = jnp.argmax(order == here).astype(jnp.int32)
    steps = jnp.arange(size, dtype=jnp.int32)
    code = jnp.concatenate(
        [part.reshape(1), order[(turn - steps) % size], order[(turn + steps) % size]]
    ).astype(jnp.int32)
    height, across = units.shape[1], units.shape[2] // 3 * size

    def incoming(array):
        return pl.BlockSpec((1,) + array.shape[1:], lambda i, code: (code[0] ^ i, 0, 0))

    def outgoing(count, index):
        return pl.BlockSpec((height, count), lambda i, code: (0, index(i)))

    return pl.pallas_call(
        deal_kernel,
        grid_spec=pltpu.PrefetchScalarGridSpec(
            num_scalar_prefetch=1,
            grid=(4,),
            in_specs=[incoming(array) for array in (*upper, *lower)],
            out_specs=[outgoing(across, lambda i: i)] * 3
            + [outgoing(width, lambda i: i)] * 2
            + [
                outgoing(width, lambda i: jnp.minimum(i, 1)),
                outgoing(width, lambda i: jnp.maximum(i - 2, 0)),
            ],
        ),
        out_shape=[jax.ShapeDtypeStruct((height, 4 * across), wide)] * 3
        + [jax.ShapeDtypeStruct((height, 4 * width), wide)] * 2
        + [jax.ShapeDtypeStruct((height, 2 * width), wide)] * 2,
        compiler_params=pltpu.CompilerParams(vmem_limit_bytes=56 << 20),
        cost_estimate=brief,
        name="deal_gradients",
    )(code, *upper, *lower)


def deal_rows(piece, *others):
    part = lax.axis_index("fsdp")
    return deal_fsdp(lambda k: rows(piece, part ^ k, piece.shape[0] // 4), *others)


def unit_grads_kernel(normed_ref, grad_ref, gate_ref, up_ref, hidden_ref, out_ref, flipped):
    @pl.when(pl.program_id(0) == 0)
    def _():
        flipped[0] = normed_ref[...].T
        flipped[1] = grad_ref[...].T

    piece = hidden_ref.shape[1]
    right = jnp.concatenate([gate_ref[...], up_ref[...]], axis=1)
    out_ref[:, : 2 * piece] = product(flipped[0], right).astype(low)
    out_ref[:, 2 * piece :] = product(flipped[1], hidden_ref[...]).astype(low)


def unit_grads(normed, grad, grad_gate, grad_up, hidden):
    size = lax.axis_size("ctx")
    count, depth = normed.shape
    piece = hidden.shape[1] // size
    rights = (grad_gate, grad_up, hidden)
    if piece % 128:
        cut = [
            contract_first(left, right).astype(low).reshape(depth, size, piece)
            for left, right in zip((normed, normed, grad), rights)
        ]
        return jnp.concatenate(cut, axis=2).transpose(1, 0, 2).reshape(size * depth, 3 * piece)
    whole = pl.BlockSpec(memory_space=pltpu.VMEM)
    return pl.pallas_call(
        unit_grads_kernel,
        grid=(size,),
        in_specs=[whole, whole] + [pl.BlockSpec((count, piece), lambda i: (0, i))] * 3,
        out_specs=pl.BlockSpec((depth, 3 * piece), lambda i: (i, 0)),
        scratch_shapes=[pltpu.VMEM((2, depth, count), low)],
        out_shape=jax.ShapeDtypeStruct((size * depth, 3 * piece), low),
        compiler_params=pltpu.CompilerParams(vmem_limit_bytes=40 << 20),
        cost_estimate=lasting,
        name="unit_grads",
    )(normed, grad, *rights)


def sum_gains(array, *others):
    part, size = lax.axis_index("fsdp"), lax.axis_size("ctx")
    width = array.shape[1] // 4
    array = jnp.sum(deal_fsdp(lambda k: columns(array, part ^ k, width)), axis=0)
    array = array + after(over_ctx(array, 1), *others[0])
    if size == 8:
        return array + sum(after(got, *others[1]) for got in exchange_levels(lambda k: array))
    bits = 2
    while bits < size:
        array = array + over_ctx(array, bits)
        bits *= 2
    return array


def body(
    hidden_in,
    out_grad,
    positions,
    attn_gain,
    w_query,
    w_key,
    w_value,
    w_out,
    ffn_gain,
    w_gate,
    w_up,
    w_down,
):
    part, here, size = lax.axis_index("fsdp"), lax.axis_index("ctx"), lax.axis_size("ctx")
    code = jnp.stack([part, here % 2, here // 2 % 2]).astype(jnp.int32)
    own_gains = jnp.stack([attn_gain, ffn_gain])
    gains = [own_gains] + [over_fsdp(own_gains, k) for k in (1, 2, 3)]
    rows_in, grad_down = hidden_in[0], out_grad[0]
    row_count = rows_in.shape[0]
    all_places = positions[0]
    own_places = lax.dynamic_slice_in_dim(all_places, here * row_count, row_count, 0)
    cosine, sine = angles_of(own_places)
    cosine = jnp.concatenate([cosine[:, 0], cosine[:, 0]], axis=1)
    sine = jnp.concatenate([-sine[:, 0], sine[:, 0]], axis=1)

    own, near, far, both = deal_weights((w_gate, w_up, w_down))
    heads = gather_thirds(jnp.concatenate([w_query, w_key, w_value], axis=1), near, far, both, *gains[1:])
    normed_one, load = heads_call(code, rows_in, cosine, sine, gains, heads)
    outward = gather_halves(w_out)
    load, near, far, both, _ = lax.optimization_barrier((load, near, far, both, outward[2]))
    far, both = over_fsdp(far, 2), over_fsdp(both, 3)
    near = over_fsdp(near, 1)
    far_other, both_other = over_ctx(far, 1), over_ctx(both, 2)

    if size == HK:
        load = lax.all_to_all(load, "ctx", 0, 0, tiled=True)
        order = all_places[::BLK] // BLK
        mixed = attention_forward(order, after(load, far))
        grad_all = gather_fsdp(grad_down, mixed)
        mixed = lax.all_to_all(after(mixed, far_other, outward[3]), "ctx", 0, 0, tiled=True)
    else:
        query_rot = load[:, :, : GROUP * HD].transpose(1, 0, 2)
        query_rot = query_rot.reshape(row_count, HK, GROUP, HD)
        keys_values = load[:, :, GROUP * HD :].transpose(1, 0, 2)
        keys_values = lax.all_gather(keys_values, "ctx", axis=0, tiled=True)
        keys_all, values_all = keys_values[:, :, :HD], keys_values[:, :, HD:]
        mixed_exact, log_total = rows_forward(
            query_rot, keys_all, values_all, own_places, all_places
        )
        mixed = mixed_exact.reshape(row_count, HK, GROUP * HD).transpose(1, 0, 2).astype(low)
        grad_all = gather_fsdp(grad_down)

    dealt = (own, near, far, far_other, both, both_other)
    mixed_low, middle, normed_two = middle_call(
        code, rows_in, after(mixed, both, grad_all), gains, outward
    )
    normed_all = gather_fsdp(normed_two, both_other)
    out_terms, back_terms, hidden, grad_gate, grad_up = units_call(
        code, normed_all, grad_all, dealt
    )
    grad_normed_two, passed = scatter_fsdp(back_terms)
    unit_terms = unit_grads(normed_all, grad_all, after(grad_gate, passed), grad_up, hidden)
    grad_normed_two, unit_terms = lax.optimization_barrier((grad_normed_two, unit_terms))
    grad_middle, grad_branch, grad_mixed, grad_gain_two = middle_back_call(
        code, middle, grad_normed_two, grad_down, gains, outward
    )
    unit_sums = lax.psum_scatter(unit_terms, "ctx", scatter_dimension=0, tiled=True)

    if size == HK:
        grad_mixed = lax.all_to_all(grad_mixed, "ctx", 0, 0, tiled=True)
        grad_load = attention_backward(order, load, grad_mixed)
        mid = grad_load
        grad_load = lax.all_to_all(grad_load, "ctx", 0, 0, tiled=True)
    else:
        grad_mixed = grad_mixed.transpose(1, 0, 2).reshape(row_count, HK, GROUP, HD)
        delta = jnp.sum(grad_mixed.astype(wide) * mixed_exact, axis=-1)
        grad_query, grad_keys, grad_values = rows_backward(
            query_rot, keys_all, values_all, own_places, all_places, log_total, delta, grad_mixed
        )
        grad_keys, grad_values = (
            lax.psum_scatter(whole.astype(low), "ctx", scatter_dimension=0, tiled=True)
            for whole in (grad_keys, grad_values)
        )
        grad_load = jnp.concatenate(
            [
                grad_query.reshape(row_count, HK, GROUP * HD).astype(low),
                grad_keys.reshape(row_count, HK, HD),
                grad_values.reshape(row_count, HK, HD),
            ],
            axis=2,
        ).transpose(1, 0, 2)
        mid = grad_load

    quarter = HQ * HD // 4
    turn = (0, 2, 1, 3)

    def own_columns(cut, *others):
        dealt = deal_fsdp(cut, *others)
        return jnp.concatenate([dealt[k] for k in turn], axis=0)

    branch_all = gather_fsdp(grad_branch, mid)
    mixed_part = own_columns(lambda k: columns(mixed_low, part ^ k, quarter), mid)
    normed_one_all = gather_fsdp(after(normed_one, grad_branch), mid)
    branch_terms = terms_of(branch_all, mixed_part)
    if size == HK:
        out_got = over_ctx(side_of(branch_terms, 1), 1)
    grad_whole, grad_raw = turn_back_call(code, grad_load, cosine, sine)
    input_grad, grad_gain_one = heads_back_call(
        code, grad_whole, rows_in, grad_middle, gains, heads
    )
    result, _ = scatter_fsdp(after(out_terms, grad_normed_two), mid)
    result = (middle + result).astype(low)
    raw_part = own_columns(
        lambda k: lax.dynamic_index_in_dim(grad_raw, part ^ k, 0, keepdims=False)
    )
    gain_terms = jnp.concatenate([grad_gain_one, grad_gain_two], axis=0)
    if size == HK:
        raw_part, out_got = together(raw_part, out_got)
        out_kept = add_low(side_of(branch_terms, 0), out_got)
        raw_terms = terms_of(normed_one_all, raw_part)
        raw_got = over_ctx(side_of(raw_terms, 1), 1)
        out_got = exchange_levels(lambda k: level_of(out_kept, k))
        raw_got, out_got, input_grad = together(raw_got, out_got, input_grad)
        raw_kept = add_low(side_of(raw_terms, 0), raw_got)
        out_sums = add_low(level_of(out_kept, 0), *out_got)
        raw_got = exchange_levels(lambda k: level_of(raw_kept, k))
        raw_got, unit_sums = together(raw_got, unit_sums)
        unit_mine = deal_rows(unit_sums)
        raw_sums = add_low(level_of(raw_kept, 0), *raw_got)
    else:
        raw_terms = terms_of(normed_one_all, raw_part)
        out_sums, raw_sums = (
            lax.psum_scatter(terms, "ctx", scatter_dimension=1, tiled=True)
            for terms in (branch_terms, raw_terms)
        )
        raw_kept = raw_terms
        unit_mine = deal_rows(unit_sums)
    sums = jnp.concatenate([out_sums, raw_sums], axis=2)
    sums = deal_fsdp(lambda k: lax.dynamic_index_in_dim(sums, part ^ k, 0, keepdims=False))
    gain_grads = sum_gains(
        gain_terms, (raw_kept,), (sums,)
    )
    gate_grad, up_grad, down_grad, out_weight_grad, query_grad, key_grad, value_grad = gather_all(
        unit_mine, sums
    )
    return (
        result[None],
        input_grad[None],
        gain_grads[0],
        query_grad,
        key_grad,
        value_grad,
        out_weight_grad,
        gain_grads[1],
        gate_grad,
        up_grad,
        down_grad,
    )


def solution(mesh):
    matrix = P("fsdp", None)
    stream = P("fsdp", "ctx", None)
    return jax.shard_map(
        body,
        mesh=mesh,
        in_specs=(stream, stream, matrix, P("fsdp"))
        + (matrix,) * 4
        + (P("fsdp"),)
        + (matrix,) * 3,
        out_specs=(stream, stream, P("fsdp")) + (matrix,) * 4 + (P("fsdp"),) + (matrix,) * 3,
        check_vma=False,
    )
```
